512 devices in a mesh: seq: 64 (over z, y), chan: 8 (over x, core).
Axes of the slice: x: 4, y: 4, z: 16, core: 2. Of those that a mesh axis runs over, the one named last changes fastest.
Arguments:
- signal: bfloat16 [8192, 2048], P('seq', 'chan'), may hold values from -6 to 6
- cotangent: bfloat16 [8192, 2048], P('seq', 'chan'), may hold values from -6 to 6
- w_proj: bfloat16 [2048, 560], P('chan'), may hold values from -0.009765625 to 0.009765625
- w_delta: bfloat16 [2, 256, 2048], P(None, None, 'chan'), may hold values from -5.03125 to 5.03125
- delta_bias: float32 [2, 2048], P(None, 'chan'), may hold values from -1 to 0.5
- decay_log: float32 [2, 12, 2048], P(None, None, 'chan'), may hold values from -12 to -3, as said below
- skip_gain: float32 [2048], P('chan'), may hold values from 0.5 to 1.5
Outputs:
- layer_out: bfloat16 [8192, 2048], P('seq', 'chan')
- signal_grad: bfloat16 [8192, 2048], P('seq', 'chan')
The draws below stay inside these ranges and needn't reach their ends.
Inputs may be any that keep to these rules, and one draw needn't show every extreme that they name: `decay_log`: each entry is the logarithm of a positive decay rate.
All inputs are finite; a program needn't handle non-finite values.
Results may differ from the reference program's by a relative error of at most 0.0085.
Values may be sent and summed in bfloat16 or wider, within the bound.
No kernel may reach another device: no remote copies, remote signals or barrier semaphores. Data moves between devices by JAX's collectives and lax.ppermute only.
A program may use at most 64 MiB of HBM per device.

```python
import math
import jax
import jax.numpy as jnp
from jax import lax

D = 2048
STATE = 12
RANK = 256
TOKENS = 8192
PROJ = 560


def draw_decay_log(key, part):
    level_key, pick_key = jax.random.split(jax.random.fold_in(key, 11))
    level = jax.random.uniform(level_key, (2, STATE, D), jnp.float32)
    picker = jax.random.uniform(pick_key, (2, STATE, D), jnp.float32)
    slow_share = 0.5
    lowest = math.log(0.1 / TOKENS)
    middle = math.log(2.0 / TOKENS)
    highest = math.log(0.04)
    slow_part = lowest + level * (middle - lowest)
    fast_part = middle + level * (highest - middle)
    return jnp.where(picker < slow_share, slow_part, fast_part).astype(jnp.float32)


def level_of(rng, extent, cuts, low, high):
    level = 1.0
    for dim, shards_of in cuts:
        steps = jax.random.uniform(jax.random.fold_in(jax.random.fold_in(rng, 6), dim), (shards_of,), jnp.float32, low / len(cuts), high / len(cuts))
        level = level * jnp.repeat(jnp.exp(steps), extent[dim] // shards_of).reshape((-1,) + (1,) * (len(extent) - 1 - dim))
    return level


def gaussian(rng, shape, spread, most, cuts=(), held_as=jnp.bfloat16):
    factor_of = level_of(rng, shape, cuts, -0.22, 0.18) if cuts else 1.0
    result = jax.random.normal(rng, shape, jnp.float32) * spread * factor_of
    return jnp.minimum(jnp.maximum(result, -most), most).astype(held_as)


def setup_inputs(seed: int = 0) -> dict:
    streams_of = jax.random.split(jax.random.key(seed), 8)
    return {
        "signal": gaussian(streams_of[0], (TOKENS, D), 1.0, 6.0, ((0, 64), (1, 8))),
        "cotangent": gaussian(streams_of[1], (TOKENS, D), 1.0, 6.0, ((0, 64), (1, 8))),
        "w_proj": gaussian(streams_of[2], (D, PROJ), (D * 2 * TOKENS ** 0.5) ** -0.5, 0.009765625, ((0, 8),)),
        "w_delta": gaussian(streams_of[3], (2, RANK, D), ((2 * TOKENS ** 0.5 / RANK) ** 0.5), 5.03125, ((2, 8),)),
        "delta_bias": jnp.clip(-1.0 + 1.5 * jax.random.uniform(streams_of[4], (2, D), jnp.float32) ** level_of(streams_of[4], (2, D), ((1, 8),), -0.2, 0.2), -1.0, 0.5),
        "decay_log": draw_decay_log(jax.random.fold_in(streams_of[7], 71), 0),
        "skip_gain": jnp.clip(0.5 + 1.0 * jax.random.uniform(streams_of[6], (D,), jnp.float32) ** level_of(streams_of[6], (D,), ((0, 8),), -0.2, 0.2), 0.5, 1.5),
    }


def compose_one(earlier, later):
    return (earlier[0] * later[0], later[0] * earlier[1] + later[1])

def linear_scan(decay, drive, falling):
    return lax.associative_scan(compose_one, (decay, drive), reverse=falling, axis=0)[1]

def both_directions(signal_part, pre_fwd, pre_bwd, in_fwd, out_fwd, in_bwd, out_bwd, log_fwd, log_bwd):
    total = jnp.zeros(signal_part.shape, jnp.float32)
    for pre, in_mat, out_mat, logs, falling in ((pre_fwd, in_fwd, out_fwd, log_fwd, False), (pre_bwd, in_bwd, out_bwd, log_bwd, True)):
        delta = jax.nn.softplus(pre)
        rate = -jnp.exp(logs)
        decay = jnp.exp(delta[:, None, :] * rate[None])
        drive = (delta * signal_part)[:, None, :] * in_mat[:, :, None]
        states = linear_scan(decay, drive, falling)
        total = total + lax.optimization_barrier(jnp.sum(out_mat[:, :, None] * states, 1))
    return total

def reference(signal, cotangent, w_proj, w_delta, delta_bias, decay_log, skip_gain):
    projected = jnp.dot(signal, w_proj, preferred_element_type=jnp.float32).astype(jnp.bfloat16)
    low_fwd = projected[:, :RANK]
    low_bwd = projected[:, RANK:2 * RANK]
    gates = projected[:, 2 * RANK:].astype(jnp.float32)
    in_fwd = gates[:, :STATE]
    out_fwd = gates[:, STATE:2 * STATE]
    in_bwd = gates[:, 2 * STATE:3 * STATE]
    out_bwd = gates[:, 3 * STATE:4 * STATE]
    pre_fwd = jnp.dot(low_fwd, w_delta[0], preferred_element_type=jnp.float32) + delta_bias[0]
    pre_bwd = jnp.dot(low_bwd, w_delta[1], preferred_element_type=jnp.float32) + delta_bias[1]
    signal_wide = signal.astype(jnp.float32)
    cot_wide = cotangent.astype(jnp.float32)
    lanes = min(128, D)
    blocks = D // lanes

    def split(array):
        return array.reshape(TOKENS, blocks, lanes).transpose(1, 0, 2)

    def join(array):
        return array.transpose(1, 0, 2).reshape(TOKENS, D)
    log_blocks = decay_log.reshape(2, STATE, blocks, lanes).transpose(2, 0, 1, 3)

    def per_block(items):
        signal_part, pre_one, pre_two, cot_part, logs = items

        def core_fn(sig_in, first_pre, second_pre, in_one, out_one, in_two, out_two):
            return both_directions(sig_in, first_pre, second_pre, in_one, out_one, in_two, out_two, logs[0], logs[1])
        core_part, pullback = jax.vjp(core_fn, signal_part, pre_one, pre_two, in_fwd, out_fwd, in_bwd, out_bwd)
        return (core_part,) + tuple(pullback(cot_part))
    results = lax.map(per_block, (split(signal_wide), split(pre_fwd), split(pre_bwd), split(cot_wide), log_blocks))
    core = join(results[0])
    grad_sig = join(results[1])
    grad_pre_fwd = join(results[2]).astype(jnp.bfloat16)
    grad_pre_bwd = join(results[3]).astype(jnp.bfloat16)
    grad_in_fwd = lax.optimization_barrier(jnp.sum(results[4], 0))
    grad_out_fwd = lax.optimization_barrier(jnp.sum(results[5], 0))
    grad_in_bwd = lax.optimization_barrier(jnp.sum(results[6], 0))
    grad_out_bwd = lax.optimization_barrier(jnp.sum(results[7], 0))
    layer_out = (core + skip_gain * signal_wide).astype(jnp.bfloat16)
    dims = (((1,), (1,)), ((), ()))
    grad_low_fwd = lax.dot_general(grad_pre_fwd, w_delta[0], dims, preferred_element_type=jnp.float32)
    grad_low_bwd = lax.dot_general(grad_pre_bwd, w_delta[1], dims, preferred_element_type=jnp.float32)
    grad_proj = jnp.concatenate([grad_low_fwd, grad_low_bwd, grad_in_fwd, grad_out_fwd, grad_in_bwd, grad_out_bwd], 1).astype(jnp.bfloat16)
    signal_grad = lax.dot_general(grad_proj, w_proj, dims, preferred_element_type=jnp.float32) + grad_sig + skip_gain * cot_wide
    return (layer_out, signal_grad.astype(jnp.bfloat16))
```

```python
import math

import jax
import jax.numpy as jnp
from jax import lax
from jax.experimental import pallas as pl
from jax.experimental.pallas import tpu as pltpu
from jax.sharding import PartitionSpec as P

GROUPS = 8
LANES = 128
SLOTS = 16
LOG2E = math.log2(math.e)
LN2 = math.log(2.0)
FAR = 1e30
NT = (((1,), (1,)), ((), ()))
F32 = jnp.float32
BF16 = jnp.bfloat16


def dot(a, b, dims=(((1,), (0,)), ((), ()))):
    return lax.dot_general(a, b, dims, preferred_element_type=F32)


def grouping(rows, inverse=False):
    steps = rows // GROUPS
    row = lax.broadcasted_iota(jnp.int32, (rows, rows), 1 if inverse else 0)
    token = lax.broadcasted_iota(jnp.int32, (rows, rows), 0 if inverse else 1)
    return jnp.where(token == (row % GROUPS) * steps + row // GROUPS, 1.0, 0.0).astype(BF16)


def project_kernel(signal, cotangent, w_proj, signal_out, cot_out, part_out):
    order = grouping(signal.shape[0])
    grouped = dot(order, signal[...])
    signal_out[...] = grouped
    cot_out[...] = dot(order, cotangent[...])
    part_out[...] = dot(grouped.astype(BF16), w_proj[...]).astype(BF16)


def spread_gates(gates, spread):
    count = gates.shape[1]
    for pair in range(count // 2):
        source = lax.broadcasted_iota(jnp.int32, (count, 2 * LANES), 0)
        lane = lax.broadcasted_iota(jnp.int32, (count, 2 * LANES), 1)
        pick = jnp.where(source == 2 * pair + lane // LANES, 1.0, 0.0).astype(BF16)
        spread[:, pair * 2 * LANES : (pair + 1) * 2 * LANES] = dot(gates, pick)


def at(step):
    return pl.ds(pl.multiple_of(step * GROUPS, GROUPS), GROUPS)


def lane_block(block):
    return slice(block * LANES, (block + 1) * LANES)


def spread_rates(decay_log, rates):
    depth = decay_log.shape[1]
    width = decay_log.shape[2]
    for way in range(2):
        scaled = -jnp.exp(decay_log[way]) * LOG2E
        for n in range(depth):
            rates[way, n] = jnp.broadcast_to(scaled[n : n + 1], (GROUPS, width))


def summary_kernel(
    projected,
    w_delta,
    bias,
    decay_log,
    signal,
    cot,
    delta_out,
    slope_out,
    local_out,
    ahead_out,
    payload,
    spread,
    rates,
    weight,
):
    rows, width = signal.shape
    rank = w_delta.shape[1]
    depth = decay_log.shape[1]
    steps = rows // GROUPS
    blocks = width // LANES
    spread_gates(projected[:, 2 * rank :], spread)
    spread_rates(decay_log, rates)
    payload[...] = jnp.zeros_like(payload)
    group = lax.broadcasted_iota(jnp.int32, (GROUPS, LANES), 0)
    for way in range(2):
        pre = dot(projected[:, way * rank : (way + 1) * rank], w_delta[way]) + bias[way : way + 1]
        delta = jnp.maximum(pre, 0.0) + jnp.log1p(jnp.exp(-jnp.abs(pre)))
        delta_out[way] = delta
        slope_out[way] = 1.0 / (1.0 + jnp.exp(-pre))
        weight[...] = delta * signal[...]
        falling = way == 1

        def gate(step, which, n):
            column = (2 * way + which) * depth + n
            return spread[at(step), column * LANES : (column + 1) * LANES]

        def walk(index, carry):
            states, carried, total = carry
            low, high = index, steps - 1 - index
            state_step = high if falling else low
            adjoint_step = low if falling else high
            new_states = []
            new_carried = []
            new_total = []
            for block in range(blocks):
                lanes = lane_block(block)
                d_state = delta_out[way, at(state_step), lanes]
                d_adjoint = delta_out[way, at(adjoint_step), lanes]
                w_state = weight[at(state_step), lanes]
                g_adjoint = cot[at(adjoint_step), lanes]
                new_total.append(total[block] + d_state)
                for n in range(depth):
                    rate = rates[way, n, :, lanes]
                    slot = block * depth + n
                    new_states.append(
                        jnp.exp2(d_state * rate) * states[slot] + w_state * gate(state_step, 0, n)
                    )
                    new_carried.append(
                        jnp.exp2(d_adjoint * rate)
                        * (g_adjoint * gate(adjoint_step, 1, n) + carried[slot])
                    )
            return (tuple(new_states), tuple(new_carried), tuple(new_total))

        zero = jnp.zeros((GROUPS, LANES), F32)
        many = (zero,) * (blocks * depth)
        states, carried, total = lax.fori_loop(0, steps, walk, (many, many, (zero,) * blocks))
        for block in range(blocks):
            lanes = lane_block(block)

            def shift(array, by, down):
                return pltpu.roll(array, GROUPS - by if down else by, 0)

            def beyond(by, down):
                return group >= GROUPS - by if down else group < by

            whole = jnp.sum(total[block], 0, keepdims=True)
            for kind, down, finals in ((0, falling, states), (1, not falling, carried)):
                windows = []
                window = total[block]
                ahead = jnp.where(beyond(1, down), 0.0, shift(window, 1, down))
                for by in (1, 2, 4):
                    windows.append(jnp.where(beyond(by, down), FAR, window))
                    outside = beyond(by, down)
                    window = window + jnp.where(outside, 0.0, shift(window, by, down))
                    ahead = ahead + jnp.where(outside, 0.0, shift(ahead, by, down))
                ahead_out[2 * way + kind, :, lanes] = ahead
                edge = 0 if down else GROUPS - 1
                for n in range(depth):
                    rate = rates[way, n, :, lanes]
                    scanned = finals[block * depth + n]
                    for by, span in zip((1, 2, 4), windows):
                        scanned = scanned + jnp.exp2(rate * span) * shift(scanned, by, down)
                    local_out[2 * way + kind, n, :, lanes] = jnp.where(
                        beyond(1, down), 0.0, shift(scanned, 1, down)
                    )
                    slot = (2 * way + kind) * SLOTS + n
                    payload[slot, block : block + 1] = scanned[edge : edge + 1]
                    payload[slot, blocks + block : blocks + block + 1] = jnp.exp2(
                        rate[:1] * whole
                    )


def shard_scan_kernel(place, parts, entries):
    shards, double, _ = parts.shape
    blocks = double // 2

    def scan(order):
        state = jnp.zeros((blocks, LANES), F32)
        for shard in order:
            entries[shard] = state
            state = parts[shard, blocks:] * state + parts[shard, :blocks]

    kind = place[0] // SLOTS
    falling = jnp.logical_or(kind == 1, kind == 2)

    @pl.when(falling)
    def _():
        scan(range(shards - 1, -1, -1))

    @pl.when(jnp.logical_not(falling))
    def _():
        scan(range(shards))


def gradient_kernel(
    projected,
    w_delta,
    decay_log,
    skip_gain,
    signal,
    cot,
    delta,
    slope,
    local,
    ahead,
    entries,
    layer_out,
    parts_out,
    direct_out,
    spread,
    rates,
    weight,
    core,
    grad_pre,
    kept,
    products,
    sums,
):
    rows, width = signal.shape
    rank = w_delta.shape[1]
    depth = decay_log.shape[1]
    steps = rows // GROUPS
    blocks = width // LANES
    spread_gates(projected[:, 2 * rank :], spread)
    spread_rates(decay_log, rates)
    core[...] = skip_gain[...] * signal[...]
    direct_out[...] = skip_gain[...] * cot[...]
    for way in range(2):
        weight[...] = delta[way] * signal[...]
        falling = way == 1

        def gate(step, which, n):
            column = (2 * way + which) * depth + n
            return spread[at(step), column * LANES : (column + 1) * LANES]

        def entering(kind):
            result = []
            for block in range(blocks):
                lanes = lane_block(block)
                gap = ahead[2 * way + kind, :, lanes]
                for n in range(depth):
                    slot = (2 * way + kind) * SLOTS + n
                    result.append(
                        local[2 * way + kind, n, :, lanes]
                        + jnp.exp2(gap * rates[way, n, :, lanes]) * entries[slot, block : block + 1]
                    )
            return tuple(result)

        def put_products(which, step, pieces):
            start = pl.multiple_of(step * depth * GROUPS, SLOTS)
            for block in range(blocks):
                stacked = jnp.concatenate(pieces[block], 0).astype(BF16)
                products[which, pl.ds(start, depth * GROUPS), lane_block(block)] = stacked

        def walk_states(index, states):
            step = steps - 1 - index if falling else index
            result = []
            pieces = []
            for block in range(blocks):
                lanes = lane_block(block)
                d = delta[way, at(step), lanes]
                w = weight[at(step), lanes]
                g = cot[at(step), lanes]
                total = core[at(step), lanes]
                row = []
                for n in range(depth):
                    slot = block * depth + n
                    faded = jnp.exp2(d * rates[way, n, :, lanes]) * states[slot]
                    kept[step, n, :, lanes] = faded
                    state = faded + w * gate(step, 0, n)
                    total = total + gate(step, 1, n) * state
                    row.append(g * state)
                    result.append(state)
                core[at(step), lanes] = total
                pieces.append(row)
            put_products(2 * way + 1, step, pieces)
            return tuple(result)

        lax.fori_loop(0, steps, walk_states, entering(0))

        def walk_adjoints(index, carried):
            step = index if falling else steps - 1 - index
            result = []
            pieces = []
            for block in range(blocks):
                lanes = lane_block(block)
                d = delta[way, at(step), lanes]
                w = weight[at(step), lanes]
                g = cot[at(step), lanes]
                through = jnp.zeros((GROUPS, LANES), F32)
                fading = jnp.zeros((GROUPS, LANES), F32)
                row = []
                for n in range(depth):
                    slot = block * depth + n
                    rate = rates[way, n, :, lanes]
                    adjoint = g * gate(step, 1, n) + carried[slot]
                    result.append(jnp.exp2(d * rate) * adjoint)
                    through = through + adjoint * gate(step, 0, n)
                    fading = fading + adjoint * kept[step, n, :, lanes] * rate
                    row.append(adjoint * w)
                grad_delta = through * signal[at(step), lanes] + fading * LN2
                direct_out[at(step), lanes] = direct_out[at(step), lanes] + through * d
                grad_pre[way, at(step), lanes] = grad_delta * slope[way, at(step), lanes]
                pieces.append(row)
            put_products(2 * way, step, pieces)
            return tuple(result)

        lax.fori_loop(0, steps, walk_adjoints, entering(1))

    ungroup = grouping(rows, inverse=True)
    layer_out[...] = dot(ungroup, core[...].astype(BF16)).astype(BF16)
    for way in range(2):
        parts_out[:, way * rank : (way + 1) * rank] = dot(
            grad_pre[way].astype(BF16), w_delta[way], NT
        ).astype(BF16)
    ones = jnp.ones((width, LANES), BF16)
    for which in range(4):
        sums[which] = dot(products[which], ones)
    lane = lax.broadcasted_iota(jnp.int32, (GROUPS, LANES), 1)
    for step in range(steps):
        merged = jnp.zeros((GROUPS, LANES), F32)
        for which in range(4):
            for n in range(depth):
                start = (step * depth + n) * GROUPS
                merged = jnp.where(
                    lane == which * depth + n, sums[which, start : start + GROUPS], merged
                )
        parts_out[step * GROUPS : (step + 1) * GROUPS, 2 * rank :] = merged[
            :, : 4 * depth
        ].astype(BF16)


def finish_kernel(grad_proj, w_proj, direct, signal_grad):
    total = dot(grad_proj[...], w_proj[...], NT) + direct[...]
    ungroup = grouping(direct.shape[0], inverse=True)
    signal_grad[...] = dot(ungroup, total.astype(BF16)).astype(BF16)


def shape(*dims, dtype=F32):
    return jax.ShapeDtypeStruct(dims, dtype)


def sum_over_chan(part):
    count = lax.axis_size("chan")
    rows, columns = part.shape
    pieces = part.reshape(count, rows // count, columns)
    arrived = lax.all_to_all(pieces, "chan", 0, 0, tiled=True)
    total = jnp.sum(arrived.astype(F32), 0).astype(BF16)
    copies = jnp.broadcast_to(total[None], (count,) + total.shape)
    return lax.all_to_all(copies, "chan", 0, 0, tiled=True).reshape(rows, columns)


def local(signal, cotangent, w_proj, w_delta, delta_bias, decay_log, skip_gain):
    rows, width = signal.shape
    columns = w_proj.shape[1]
    depth = decay_log.shape[1]
    steps = rows // GROUPS
    blocks = width // LANES
    shards = lax.axis_size("seq")
    if shards != 4 * SLOTS or depth > SLOTS:
        raise ValueError("shard count")
    gates = 4 * depth
    signal_wide, cot_wide, part = pl.pallas_call(
        project_kernel,
        out_shape=(shape(rows, width), shape(rows, width), shape(rows, columns, dtype=BF16)),
        name="project",
    )(signal, cotangent, w_proj)
    projected = sum_over_chan(part)
    delta, slope, local_states, ahead, payload = pl.pallas_call(
        summary_kernel,
        out_shape=(
            shape(2, rows, width),
            shape(2, rows, width),
            shape(4, depth, GROUPS, width),
            shape(4, GROUPS, width),
            shape(shards, 2 * blocks, LANES),
        ),
        scratch_shapes=[
            pltpu.VMEM((rows, gates * LANES), F32),
            pltpu.VMEM((2, depth, GROUPS, width), F32),
            pltpu.VMEM((rows, width), F32),
        ],
        name="summary",
    )(projected, w_delta, delta_bias, decay_log, signal_wide, cot_wide)
    parts = lax.all_to_all(payload, "seq", 0, 0, tiled=True)
    place = lax.axis_index("seq").astype(jnp.int32).reshape(1)
    entries = pl.pallas_call(
        shard_scan_kernel,
        out_shape=shape(shards, blocks, LANES),
        in_specs=[
            pl.BlockSpec(memory_space=pltpu.SMEM),
            pl.BlockSpec(memory_space=pltpu.VMEM),
        ],
        out_specs=pl.BlockSpec(memory_space=pltpu.VMEM),
        name="shard_scan",
    )(place, parts)
    entries = lax.all_to_all(entries, "seq", 0, 0, tiled=True)
    layer_out, grad_parts, direct = pl.pallas_call(
        gradient_kernel,
        out_shape=(
            shape(rows, width, dtype=BF16),
            shape(rows, columns, dtype=BF16),
            shape(rows, width),
        ),
        scratch_shapes=[
            pltpu.VMEM((rows, gates * LANES), F32),
            pltpu.VMEM((2, depth, GROUPS, width), F32),
            pltpu.VMEM((rows, width), F32),
            pltpu.VMEM((rows, width), F32),
            pltpu.VMEM((2, rows, width), F32),
            pltpu.VMEM((steps, depth, GROUPS, width), F32),
            pltpu.VMEM((4, rows * depth, width), BF16),
            pltpu.VMEM((4, rows * depth, LANES), F32),
        ],
        name="gradient",
    )(
        projected,
        w_delta,
        decay_log,
        skip_gain.reshape(1, width),
        signal_wide,
        cot_wide,
        delta,
        slope,
        local_states,
        ahead,
        entries,
    )
    grad_proj = sum_over_chan(grad_parts)
    signal_grad = pl.pallas_call(
        finish_kernel, out_shape=shape(rows, width, dtype=BF16), name="finish"
    )(grad_proj, w_proj, direct)
    return (layer_out, signal_grad)


def solution(mesh):
    in_specs = (
        P("seq", "chan"),
        P("seq", "chan"),
        P("chan", None),
        P(None, None, "chan"),
        P(None, "chan"),
        P(None, None, "chan"),
        P("chan"),
    )
    out_specs = (P("seq", "chan"), P("seq", "chan"))
    return jax.shard_map(local, mesh=mesh, in_specs=in_specs, out_specs=out_specs, check_vma=False)
```

```python
import math

import jax
import jax.numpy as jnp
from jax import lax
from jax.experimental import pallas as pl
from jax.experimental.pallas import tpu as pltpu
from jax.sharding import PartitionSpec as P

GROUPS = 8
LANES = 128
SLOTS = 16
LOG2E = math.log2(math.e)
LN2 = math.log(2.0)
FAR = 1e30
NT = (((1,), (1,)), ((), ()))
F32 = jnp.float32
BF16 = jnp.bfloat16


def dot(a, b, dims=(((1,), (0,)), ((), ()))):
    return lax.dot_general(a, b, dims, preferred_element_type=F32)


def grouping(rows, inverse=False):
    steps = rows // GROUPS
    row = lax.broadcasted_iota(jnp.int32, (rows, rows), 1 if inverse else 0)
    token = lax.broadcasted_iota(jnp.int32, (rows, rows), 0 if inverse else 1)
    return jnp.where(token == (row % GROUPS) * steps + row // GROUPS, 1.0, 0.0).astype(BF16)


def project_kernel(signal, w_proj, signal_out, part_out):
    grouped = dot(grouping(signal.shape[0]), signal[...])
    signal_out[...] = grouped
    part_out[...] = dot(grouped.astype(BF16), w_proj[...], NT).astype(BF16)


def prepare_kernel(cotangent, decay_log, cot_out, rates):
    cot_out[...] = dot(grouping(cotangent.shape[0]), cotangent[...])
    depth, _, width = decay_log.shape
    for n in range(depth):
        scaled = -jnp.exp(decay_log[n]) * LOG2E
        for way in range(2):
            rates[way, n] = jnp.broadcast_to(scaled[way : way + 1], (GROUPS, width))


def at(step):
    return pl.ds(pl.multiple_of(step * GROUPS, GROUPS), GROUPS)


def lane_block(block):
    return slice(block * LANES, (block + 1) * LANES)


def spread(row, column):
    return jnp.broadcast_to(row[:, column : column + 1], (GROUPS, LANES))


def summary_kernel(
    projected,
    w_delta,
    bias,
    rates,
    signal,
    cot,
    delta_out,
    slope_out,
    local_out,
    ahead_out,
    payload,
    gates,
    weight,
    fades,
):
    rows, width = signal.shape
    rank = w_delta.shape[1]
    depth = rates.shape[1]
    steps = rows // GROUPS
    blocks = width // LANES
    gates[:, : 4 * depth] = projected[:, 2 * rank :].astype(F32)
    payload[...] = jnp.zeros_like(payload)
    group = lax.broadcasted_iota(jnp.int32, (GROUPS, LANES), 0)
    for way in range(2):
        pre = dot(projected[:, way * rank : (way + 1) * rank], w_delta[way]) + bias[way : way + 1]
        delta = jnp.maximum(pre, 0.0) + jnp.log1p(jnp.exp(-jnp.abs(pre)))
        delta_out[way] = delta
        slope_out[way] = 1.0 / (1.0 + jnp.exp(-pre))
        weight[...] = delta * signal[...]
        falling = way == 1
        zero = jnp.zeros((GROUPS, LANES), F32)
        many = (zero,) * (blocks * depth)

        def walk_states(index, carry):
            states, total = carry
            step = steps - 1 - index if falling else index
            row = gates[at(step), :]
            d = [delta_out[way, at(step), lane_block(block)] for block in range(blocks)]
            w = [weight[at(step), lane_block(block)] for block in range(blocks)]
            result = []
            for n in range(depth):
                gate = spread(row, 2 * way * depth + n)
                for block in range(blocks):
                    fade = jnp.exp2(d[block] * rates[way, n, :, lane_block(block)])
                    fades[step, n, :, lane_block(block)] = fade
                    result.append(fade * states[n * blocks + block] + w[block] * gate)
            return (tuple(result), tuple(t + x for t, x in zip(total, d)))

        states, total = lax.fori_loop(0, steps, walk_states, (many, (zero,) * blocks))

        def walk_adjoints(index, carried):
            step = index if falling else steps - 1 - index
            row = gates[at(step), :]
            g = [cot[at(step), lane_block(block)] for block in range(blocks)]
            result = []
            for n in range(depth):
                gate = spread(row, (2 * way + 1) * depth + n)
                for block in range(blocks):
                    fade = fades[step, n, :, lane_block(block)]
                    result.append(fade * (g[block] * gate + carried[n * blocks + block]))
            return tuple(result)

        carried = lax.fori_loop(0, steps, walk_adjoints, many)
        for block in range(blocks):
            lanes = lane_block(block)

            def shift(array, by, down):
                return pltpu.roll(array, GROUPS - by if down else by, 0)

            def beyond(by, down):
                return group >= GROUPS - by if down else group < by

            whole = jnp.sum(total[block], 0, keepdims=True)
            for kind, down, finals in ((0, falling, states), (1, not falling, carried)):
                windows = []
                window = total[block]
                ahead = jnp.where(beyond(1, down), 0.0, shift(window, 1, down))
                for by in (1, 2, 4):
                    windows.append(jnp.where(beyond(by, down), FAR, window))
                    outside = beyond(by, down)
                    window = window + jnp.where(outside, 0.0, shift(window, by, down))
                    ahead = ahead + jnp.where(outside, 0.0, shift(ahead, by, down))
                ahead_out[2 * way + kind, :, lanes] = ahead
                edge = 0 if down else GROUPS - 1
                for n in range(depth):
                    rate = rates[way, n, :, lanes]
                    scanned = finals[n * blocks + block]
                    for by, span in zip((1, 2, 4), windows):
                        scanned = scanned + jnp.exp2(rate * span) * shift(scanned, by, down)
                    local_out[2 * way + kind, n, :, lanes] = jnp.where(
                        beyond(1, down), 0.0, shift(scanned, 1, down)
                    )
                    slot = (2 * way + kind) * SLOTS + n
                    payload[slot, block : block + 1] = scanned[edge : edge + 1]
                    payload[slot, blocks + block : blocks + block + 1] = jnp.exp2(
                        rate[:1] * whole
                    )


def shard_scan_kernel(place, parts, entries):
    shards, double, _ = parts.shape
    blocks = double // 2

    def scan(order):
        state = jnp.zeros((blocks, LANES), F32)
        for shard in order:
            entries[shard] = state
            state = parts[shard, blocks:] * state + parts[shard, :blocks]

    kind = place[0] // SLOTS
    falling = jnp.logical_or(kind == 1, kind == 2)

    @pl.when(falling)
    def _():
        scan(range(shards - 1, -1, -1))

    @pl.when(jnp.logical_not(falling))
    def _():
        scan(range(shards))


def gradient_kernel(
    projected,
    w_delta,
    rates,
    skip_gain,
    signal,
    cot,
    delta,
    slope,
    local,
    ahead,
    entries,
    layer_out,
    parts_out,
    direct_out,
    gates,
    weight,
    core,
    grad_pre,
    fades,
    kept,
    gate_grad,
):
    rows, width = signal.shape
    rank = w_delta.shape[1]
    depth = rates.shape[1]
    steps = rows // GROUPS
    blocks = width // LANES
    gates[:, : 4 * depth] = projected[:, 2 * rank :].astype(F32)
    core[...] = skip_gain[...] * signal[...]
    direct_out[...] = skip_gain[...] * cot[...]
    gate_grad[...] = jnp.zeros_like(gate_grad)
    lane = lax.broadcasted_iota(jnp.int32, (GROUPS, LANES), 1)
    for way in range(2):
        weight[...] = delta[way] * signal[...]
        falling = way == 1
        first = 2 * way * depth

        def entering(kind):
            gap = [ahead[2 * way + kind, :, lane_block(block)] for block in range(blocks)]
            return tuple(
                local[2 * way + kind, n, :, lane_block(block)]
                + jnp.exp2(gap[block] * rates[way, n, :, lane_block(block)])
                * entries[(2 * way + kind) * SLOTS + n, block : block + 1]
                for n in range(depth)
                for block in range(blocks)
            )

        def pieces(array, step):
            return [array[at(step), lane_block(block)] for block in range(blocks)]

        def total_over_lanes(products):
            return jnp.sum(sum(products[1:], products[0]), 1, keepdims=True)

        def walk_states(index, states):
            step = steps - 1 - index if falling else index
            row = gates[at(step), :]
            d, w, g = pieces(delta.at[way], step), pieces(weight, step), pieces(cot, step)
            total = pieces(core, step)
            merged = gate_grad[at(step), :]
            result = []
            for n in range(depth):
                gate_in = spread(row, first + n)
                gate_out = spread(row, first + depth + n)
                products = []
                for block in range(blocks):
                    lanes = lane_block(block)
                    fade = jnp.exp2(d[block] * rates[way, n, :, lanes])
                    fades[step, n, :, lanes] = fade
                    faded = fade * states[n * blocks + block]
                    kept[step, n, :, lanes] = faded
                    state = faded + w[block] * gate_in
                    total[block] = total[block] + gate_out * state
                    products.append(g[block] * state)
                    result.append(state)
                merged = jnp.where(lane == first + depth + n, total_over_lanes(products), merged)
            for block in range(blocks):
                core[at(step), lane_block(block)] = total[block]
            gate_grad[at(step), :] = merged
            return tuple(result)

        lax.fori_loop(0, steps, walk_states, entering(0))

        def walk_adjoints(index, carried):
            step = index if falling else steps - 1 - index
            row = gates[at(step), :]
            w, g = pieces(weight, step), pieces(cot, step)
            merged = gate_grad[at(step), :]
            through = [jnp.zeros((GROUPS, LANES), F32)] * blocks
            fading = [jnp.zeros((GROUPS, LANES), F32)] * blocks
            result = []
            for n in range(depth):
                gate_in = spread(row, first + n)
                gate_out = spread(row, first + depth + n)
                products = []
                for block in range(blocks):
                    lanes = lane_block(block)
                    adjoint = g[block] * gate_out + carried[n * blocks + block]
                    result.append(fades[step, n, :, lanes] * adjoint)
                    through[block] = through[block] + adjoint * gate_in
                    fading[block] = fading[block] + (
                        adjoint * kept[step, n, :, lanes] * rates[way, n, :, lanes]
                    )
                    products.append(adjoint * w[block])
                merged = jnp.where(lane == first + n, total_over_lanes(products), merged)
            gate_grad[at(step), :] = merged
            for block in range(blocks):
                lanes = lane_block(block)
                grad_delta = through[block] * signal[at(step), lanes] + fading[block] * LN2
                direct_out[at(step), lanes] = (
                    direct_out[at(step), lanes] + through[block] * delta[way, at(step), lanes]
                )
                grad_pre[way, at(step), lanes] = grad_delta * slope[way, at(step), lanes]
            return tuple(result)

        lax.fori_loop(0, steps, walk_adjoints, entering(1))

    for way in range(2):
        parts_out[:, way * rank : (way + 1) * rank] = dot(
            grad_pre[way].astype(BF16), w_delta[way], NT
        ).astype(BF16)
    parts_out[:, 2 * rank :] = gate_grad[:, : 4 * depth].astype(BF16)
    ungroup = grouping(rows, inverse=True)
    layer_out[...] = dot(ungroup, core[...].astype(BF16)).astype(BF16)


def finish_kernel(grad_proj, w_proj, direct, signal_grad):
    total = dot(grad_proj[...], w_proj[...]) + direct[...]
    ungroup = grouping(direct.shape[0], inverse=True)
    signal_grad[...] = dot(ungroup, total.astype(BF16)).astype(BF16)


def shape(*dims, dtype=F32):
    return jax.ShapeDtypeStruct(dims, dtype)


def sum_over_chan(part):
    count = lax.axis_size("chan")
    rows, columns = part.shape
    pieces = part.reshape(count, rows // count, columns)
    arrived = lax.all_to_all(pieces, "chan", 0, 0, tiled=True)
    total = jnp.sum(arrived.astype(F32), 0).astype(BF16)
    copies = jnp.broadcast_to(total[None], (count,) + total.shape)
    return lax.all_to_all(copies, "chan", 0, 0, tiled=True).reshape(rows, columns)


def kernel(body, out_shape, mebibytes, scratch=(), cost=0, **more):
    return pl.pallas_call(
        body,
        out_shape=out_shape,
        scratch_shapes=[pltpu.VMEM(dims, dtype) for dims, dtype in scratch],
        compiler_params=pltpu.CompilerParams(vmem_limit_bytes=mebibytes << 20),
        cost_estimate=pl.CostEstimate(flops=cost, bytes_accessed=cost, transcendentals=0),
        name=body.__name__,
        **more,
    )


def local(signal, cotangent, w_proj, w_delta, delta_bias, decay_log, skip_gain):
    rows, width = signal.shape
    columns = w_proj.shape[1]
    depth = decay_log.shape[1]
    steps = rows // GROUPS
    blocks = width // LANES
    shards = lax.axis_size("seq")
    if shards != 4 * SLOTS or depth > SLOTS:
        raise ValueError("shard count")
    w_turned = w_proj.T
    place = lax.axis_index("seq").astype(jnp.int32).reshape(1)
    signal_wide, part = kernel(
        project_kernel, (shape(rows, width), shape(rows, columns, dtype=BF16)), 8
    )(signal, w_turned)
    cot_wide, rates = kernel(
        prepare_kernel,
        (shape(rows, width), shape(2, depth, GROUPS, width)),
        8,
        cost=1 << 20,
    )(cotangent, decay_log.transpose(1, 0, 2))
    projected = sum_over_chan(part)
    stack = ((steps, depth, GROUPS, width), F32)
    delta, slope, local_states, ahead, payload = kernel(
        summary_kernel,
        (
            shape(2, rows, width),
            shape(2, rows, width),
            shape(4, depth, GROUPS, width),
            shape(4, GROUPS, width),
            shape(shards, 2 * blocks, LANES),
        ),
        20,
        (((rows, LANES), F32), ((rows, width), F32), stack),
    )(projected, w_delta, delta_bias, rates, signal_wide, cot_wide)
    parts = lax.all_to_all(payload, "seq", 0, 0, tiled=True)
    entries = kernel(
        shard_scan_kernel,
        shape(shards, blocks, LANES),
        4,
        in_specs=[
            pl.BlockSpec(memory_space=pltpu.SMEM),
            pl.BlockSpec(memory_space=pltpu.VMEM),
        ],
        out_specs=pl.BlockSpec(memory_space=pltpu.VMEM),
    )(place, parts)
    entries = lax.all_to_all(entries, "seq", 0, 0, tiled=True)
    layer_out, grad_parts, direct = kernel(
        gradient_kernel,
        (
            shape(rows, width, dtype=BF16),
            shape(rows, columns, dtype=BF16),
            shape(rows, width),
        ),
        24,
        (
            ((rows, LANES), F32),
            ((rows, width), F32),
            ((rows, width), F32),
            ((2, rows, width), F32),
            stack,
            stack,
            ((rows, LANES), F32),
        ),
    )(
        projected,
        w_delta,
        rates,
        skip_gain.reshape(1, width),
        signal_wide,
        cot_wide,
        delta,
        slope,
        local_states,
        ahead,
        entries,
    )
    grad_proj = sum_over_chan(grad_parts)
    signal_grad = kernel(finish_kernel, shape(rows, width, dtype=BF16), 8)(
        grad_proj, w_turned, direct
    )
    return (layer_out, signal_grad)


def solution(mesh):
    in_specs = (
        P("seq", "chan"),
        P("seq", "chan"),
        P("chan", None),
        P(None, None, "chan"),
        P(None, "chan"),
        P(None, None, "chan"),
        P("chan"),
    )
    out_specs = (P("seq", "chan"), P("seq", "chan"))
    return jax.shard_map(local, mesh=mesh, in_specs=in_specs, out_specs=out_specs, check_vma=False)
```

```python
import math

import jax
import jax.numpy as jnp
from jax import lax
from jax.experimental import pallas as pl
from jax.experimental.pallas import tpu as pltpu
from jax.sharding import PartitionSpec as P

GROUPS = 8
LANES = 128
LOG2E = math.log2(math.e)
LN2 = math.log(2.0)
FAR = 1e30
NT = (((1,), (1,)), ((), ()))
F32 = jnp.float32
BF16 = jnp.bfloat16


def dot(a, b, dims=(((1,), (0,)), ((), ()))):
    return lax.dot_general(a, b, dims, preferred_element_type=F32)


def grouping(rows, inverse=False):
    steps = rows // GROUPS
    row = lax.broadcasted_iota(jnp.int32, (rows, rows), 1 if inverse else 0)
    token = lax.broadcasted_iota(jnp.int32, (rows, rows), 0 if inverse else 1)
    return jnp.where(token == (row % GROUPS) * steps + row // GROUPS, 1.0, 0.0).astype(BF16)


def project_kernel(signal, w_proj, signal_out, part_out):
    grouped = dot(grouping(signal.shape[0]), signal[...])
    signal_out[...] = grouped
    part_out[...] = dot(grouped.astype(BF16), w_proj[...], NT).astype(BF16)


def prepare_kernel(cotangent, decay_log, bias, skip_gain, cot_out, rates, flat, bias_out, gain_out):
    cot_out[...] = dot(grouping(cotangent.shape[0]), cotangent[...])
    bias_out[...] = bias[...]
    gain_out[...] = skip_gain[...]
    depth, _, width = decay_log.shape
    flat[...] = jnp.zeros_like(flat)
    for n in range(depth):
        scaled = -jnp.exp(decay_log[n]) * LOG2E
        for way in range(2):
            rates[way, n] = jnp.broadcast_to(scaled[way : way + 1], (GROUPS, width))
            flat[way, n : n + 1] = scaled[way : way + 1]


def at(step):
    return pl.ds(pl.multiple_of(step * GROUPS, GROUPS), GROUPS)


def lane_block(block):
    return slice(block * LANES, (block + 1) * LANES)


def spread_gates(gates, spread):
    count = gates.shape[1]
    for pair in range(count // 2):
        source = lax.broadcasted_iota(jnp.int32, (count, 2 * LANES), 0)
        lane = lax.broadcasted_iota(jnp.int32, (count, 2 * LANES), 1)
        pick = jnp.where(source == 2 * pair + lane // LANES, 1.0, 0.0).astype(BF16)
        spread[:, pair * 2 * LANES : (pair + 1) * 2 * LANES] = dot(gates, pick)


def gate_at(spread, step, column):
    return spread[at(step), column * LANES : (column + 1) * LANES]


def summary_kernel(
    projected,
    w_delta,
    bias,
    rates,
    signal,
    cot,
    delta_out,
    slope_out,
    local_out,
    ahead_out,
    payload,
    weight,
    fades,
    spread,
):
    rows, width = signal.shape
    rank = w_delta.shape[1]
    depth = rates.shape[1]
    steps = rows // GROUPS
    blocks = width // LANES
    spread_gates(projected[:, 2 * rank :], spread)
    payload[...] = jnp.zeros_like(payload)
    group = lax.broadcasted_iota(jnp.int32, (GROUPS, LANES), 0)
    for way in range(2):
        pre = dot(projected[:, way * rank : (way + 1) * rank], w_delta[way]) + bias[way : way + 1]
        delta = jnp.maximum(pre, 0.0) + jnp.log1p(jnp.exp(-jnp.abs(pre)))
        delta_out[way] = delta
        slope_out[way] = 1.0 / (1.0 + jnp.exp(-pre))
        weight[...] = delta * signal[...]
        falling = way == 1
        zero = jnp.zeros((GROUPS, LANES), F32)
        many = (zero,) * (blocks * depth)

        def walk_states(index, carry):
            states, total = carry
            step = steps - 1 - index if falling else index
            d = [delta_out[way, at(step), lane_block(block)] for block in range(blocks)]
            w = [weight[at(step), lane_block(block)] for block in range(blocks)]
            result = []
            for n in range(depth):
                gate = gate_at(spread, step, 2 * way * depth + n)
                for block in range(blocks):
                    fade = jnp.exp2(d[block] * rates[way, n, :, lane_block(block)])
                    fades[step, n, :, lane_block(block)] = fade
                    result.append(fade * states[n * blocks + block] + w[block] * gate)
            return (tuple(result), tuple(t + x for t, x in zip(total, d)))

        states, total = lax.fori_loop(0, steps, walk_states, (many, (zero,) * blocks))

        def walk_adjoints(index, carried):
            step = index if falling else steps - 1 - index
            g = [cot[at(step), lane_block(block)] for block in range(blocks)]
            result = []
            for n in range(depth):
                gate = gate_at(spread, step, (2 * way + 1) * depth + n)
                for block in range(blocks):
                    fade = fades[step, n, :, lane_block(block)]
                    result.append(fade * (g[block] * gate + carried[n * blocks + block]))
            return tuple(result)

        carried = lax.fori_loop(0, steps, walk_adjoints, many)
        for block in range(blocks):
            lanes = lane_block(block)

            def shift(array, by, down):
                return pltpu.roll(array, GROUPS - by if down else by, 0)

            def beyond(by, down):
                return group >= GROUPS - by if down else group < by

            whole = jnp.sum(total[block], 0, keepdims=True)
            for kind, down, finals in ((0, falling, states), (1, not falling, carried)):
                windows = []
                window = total[block]
                ahead = jnp.where(beyond(1, down), 0.0, shift(window, 1, down))
                for by in (1, 2, 4):
                    windows.append(jnp.where(beyond(by, down), FAR, window))
                    outside = beyond(by, down)
                    window = window + jnp.where(outside, 0.0, shift(window, by, down))
                    ahead = ahead + jnp.where(outside, 0.0, shift(ahead, by, down))
                ahead_out[2 * way + kind, :, lanes] = ahead
                edge = 0 if down else GROUPS - 1
                for n in range(depth):
                    rate = rates[way, n, :, lanes]
                    scanned = finals[n * blocks + block]
                    for by, span in zip((1, 2, 4), windows):
                        scanned = scanned + jnp.exp2(rate * span) * shift(scanned, by, down)
                    local_out[2 * way + kind, n, :, lanes] = jnp.where(
                        beyond(1, down), 0.0, shift(scanned, 1, down)
                    )
                    payload[2 * way + kind, n : n + 1, lanes] = scanned[edge : edge + 1]
                payload[2 * way + kind, depth : depth + 1, lanes] = whole


def fall_or_rise(kind, run):
    falling = jnp.logical_or(kind == 1, kind == 2)

    @pl.when(falling)
    def _():
        run(True)

    @pl.when(jnp.logical_not(falling))
    def _():
        run(False)


def order(count, falling):
    return range(count - 1, -1, -1) if falling else range(count)


def shard_fade(parts, flat, way, shard):
    depth = parts.shape[1] - 4
    return jnp.exp2(flat[way] * parts[shard, depth : depth + 1])


def row_kernel(place, parts, flat, copies):
    shards, slots, width = parts.shape
    depth = slots - 4
    kind = place[1]
    slot = lax.broadcasted_iota(jnp.int32, (slots, width), 0)

    def run(falling):
        state = jnp.zeros((slots, width), F32)
        for shard in order(shards, falling):
            state = shard_fade(parts, flat, kind // 2, shard) * state + parts[shard]
        total = parts[0, depth : depth + 1]
        for shard in range(1, shards):
            total = total + parts[shard, depth : depth + 1]
        coarse = total.astype(BF16).astype(F32)
        packed = jnp.where(slot == depth, coarse, state)
        packed = jnp.where(slot == depth + 1, total - coarse, packed).astype(BF16)
        for copy in range(copies.shape[0]):
            copies[copy] = packed

    fall_or_rise(kind, run)


def entry_kernel(place, rows, parts, flat, entries):
    count, slots, width = rows.shape
    shards = parts.shape[0]
    depth = slots - 4
    here = place[0]
    kind = place[1]
    rates = flat[kind // 2]

    def run(falling):
        state = jnp.zeros((slots, width), F32)
        for row in order(count, falling):
            block = rows[row].astype(F32)
            total = block[depth : depth + 1] + block[depth + 1 : depth + 2]
            passed = jnp.exp2(rates * total) * state + block
            before = row > here if falling else row < here
            state = jnp.where(before, passed, state)
        for shard in order(shards, falling):
            entries[shard] = state
            state = shard_fade(parts, flat, kind // 2, shard) * state + parts[shard]

    fall_or_rise(kind, run)


def gradient_kernel(
    projected,
    w_delta,
    rates,
    skip_gain,
    signal,
    cot,
    delta,
    slope,
    local,
    ahead,
    entries,
    layer_out,
    parts_out,
    direct_out,
    weight,
    core,
    grad_pre,
    fades,
    kept,
    products,
    spread,
):
    rows, width = signal.shape
    rank = w_delta.shape[1]
    depth = rates.shape[1]
    steps = rows // GROUPS
    blocks = width // LANES
    spread_gates(projected[:, 2 * rank :], spread)
    core[...] = skip_gain[...] * signal[...]
    direct_out[...] = skip_gain[...] * cot[...]
    for way in range(2):
        weight[...] = delta[way] * signal[...]
        falling = way == 1
        first = 2 * way * depth

        def entering(kind):
            gap = [ahead[2 * way + kind, :, lane_block(block)] for block in range(blocks)]
            return tuple(
                local[2 * way + kind, n, :, lane_block(block)]
                + jnp.exp2(gap[block] * rates[way, n, :, lane_block(block)])
                * entries[2 * way + kind, n : n + 1, lane_block(block)]
                for n in range(depth)
                for block in range(blocks)
            )

        def pieces(array, step):
            return [array[at(step), lane_block(block)] for block in range(blocks)]

        def put_products(which, step, rows_of):
            start = pl.multiple_of(step * depth * GROUPS, 2 * GROUPS)
            for block in range(blocks):
                stacked = jnp.concatenate(rows_of[block], 0).astype(BF16)
                products[which, pl.ds(start, depth * GROUPS), lane_block(block)] = stacked

        def walk_states(index, states):
            step = steps - 1 - index if falling else index
            d, w, g = pieces(delta.at[way], step), pieces(weight, step), pieces(cot, step)
            total = pieces(core, step)
            rows_of = [[] for _ in range(blocks)]
            result = []
            for n in range(depth):
                gate_in = gate_at(spread, step, first + n)
                gate_out = gate_at(spread, step, first + depth + n)
                for block in range(blocks):
                    lanes = lane_block(block)
                    fade = jnp.exp2(d[block] * rates[way, n, :, lanes])
                    fades[step, n, :, lanes] = fade
                    faded = fade * states[n * blocks + block]
                    kept[step, n, :, lanes] = faded
                    state = faded + w[block] * gate_in
                    total[block] = total[block] + gate_out * state
                    rows_of[block].append(g[block] * state)
                    result.append(state)
            for block in range(blocks):
                core[at(step), lane_block(block)] = total[block]
            put_products(2 * way + 1, step, rows_of)
            return tuple(result)

        lax.fori_loop(0, steps, walk_states, entering(0))

        def walk_adjoints(index, carried):
            step = index if falling else steps - 1 - index
            w, g = pieces(weight, step), pieces(cot, step)
            rows_of = [[] for _ in range(blocks)]
            through = [jnp.zeros((GROUPS, LANES), F32)] * blocks
            fading = [jnp.zeros((GROUPS, LANES), F32)] * blocks
            result = []
            for n in range(depth):
                gate_in = gate_at(spread, step, first + n)
                gate_out = gate_at(spread, step, first + depth + n)
                for block in range(blocks):
                    lanes = lane_block(block)
                    adjoint = g[block] * gate_out + carried[n * blocks + block]
                    result.append(fades[step, n, :, lanes] * adjoint)
                    through[block] = through[block] + adjoint * gate_in
                    fading[block] = fading[block] + (
                        adjoint * kept[step, n, :, lanes] * rates[way, n, :, lanes]
                    )
                    rows_of[block].append(adjoint * w[block])
            put_products(2 * way, step, rows_of)
            for block in range(blocks):
                lanes = lane_block(block)
                grad_delta = through[block] * signal[at(step), lanes] + fading[block] * LN2
                direct_out[at(step), lanes] = (
                    direct_out[at(step), lanes] + through[block] * delta[way, at(step), lanes]
                )
                grad_pre[way, at(step), lanes] = grad_delta * slope[way, at(step), lanes]
            return tuple(result)

        lax.fori_loop(0, steps, walk_adjoints, entering(1))

    for way in range(2):
        parts_out[:, way * rank : (way + 1) * rank] = dot(
            grad_pre[way].astype(BF16), w_delta[way], NT
        ).astype(BF16)
    ones = jnp.ones((width, LANES), BF16)
    lane = lax.broadcasted_iota(jnp.int32, (GROUPS, LANES), 1)
    height = depth * GROUPS
    for start in range(0, steps, 4):
        merged = [jnp.zeros((GROUPS, LANES), F32)] * 4
        for which in range(4):
            sums = dot(products[which, start * height : (start + 4) * height], ones)
            for step in range(4):
                for n in range(depth):
                    row = step * height + n * GROUPS
                    merged[step] = jnp.where(
                        lane == which * depth + n, sums[row : row + GROUPS], merged[step]
                    )
        stacked = jnp.concatenate(merged, 0)[:, : 4 * depth].astype(BF16)
        parts_out[start * GROUPS : (start + 4) * GROUPS, 2 * rank :] = stacked
    ungroup = grouping(rows, inverse=True)
    layer_out[...] = dot(ungroup, core[...].astype(BF16)).astype(BF16)


def finish_kernel(grad_proj, w_proj, direct, signal_grad):
    total = dot(grad_proj[...], w_proj[...]) + direct[...]
    ungroup = grouping(direct.shape[0], inverse=True)
    signal_grad[...] = dot(ungroup, total.astype(BF16)).astype(BF16)


def shape(*dims, dtype=F32):
    return jax.ShapeDtypeStruct(dims, dtype)


def sum_over_chan(part):
    count = lax.axis_size("chan")
    rows, columns = part.shape
    pieces = part.reshape(count, rows // count, columns)
    arrived = lax.all_to_all(pieces, "chan", 0, 0, tiled=True)
    total = jnp.sum(arrived.astype(F32), 0).astype(BF16)
    copies = jnp.broadcast_to(total[None], (count,) + total.shape)
    return lax.all_to_all(copies, "chan", 0, 0, tiled=True).reshape(rows, columns)


def kernel(body, out_shape, mebibytes, scratch=(), cost=0, **more):
    return pl.pallas_call(
        body,
        out_shape=out_shape,
        scratch_shapes=[pltpu.VMEM(dims, dtype) for dims, dtype in scratch],
        compiler_params=pltpu.CompilerParams(vmem_limit_bytes=mebibytes << 20),
        cost_estimate=pl.CostEstimate(flops=cost, bytes_accessed=cost, transcendentals=0),
        name=body.__name__,
        **more,
    )


def local(signal, cotangent, w_proj, w_delta, delta_bias, decay_log, skip_gain):
    rows, width = signal.shape
    columns = w_proj.shape[1]
    depth = decay_log.shape[1]
    steps = rows // GROUPS
    shards = lax.axis_size("seq")
    if shards % 4:
        raise ValueError("shard count")
    w_turned = w_proj.T
    shard = lax.axis_index("seq").astype(jnp.int32)
    place = jnp.stack([shard // 4, shard % 4])
    along_y = [[z * 4 + y for y in range(4)] for z in range(shards // 4)]
    along_z = [[z * 4 + y for z in range(shards // 4)] for y in range(4)]
    slots = depth + 4
    whole = pl.BlockSpec(memory_space=pltpu.VMEM)
    scalars = pl.BlockSpec(memory_space=pltpu.SMEM)

    def exchange(array, groups):
        return lax.all_to_all(array, "seq", 0, 0, tiled=True, axis_index_groups=groups)

    signal_wide, part = kernel(
        project_kernel, (shape(rows, width), shape(rows, columns, dtype=BF16)), 8
    )(signal, w_turned)
    cot_wide, rates, flat, bias, gain = kernel(
        prepare_kernel,
        (
            shape(rows, width),
            shape(2, depth, GROUPS, width),
            shape(2, slots, width),
            shape(2, width),
            shape(1, width),
        ),
        8,
        cost=1 << 20,
    )(cotangent, decay_log.transpose(1, 0, 2), delta_bias, skip_gain.reshape(1, width))
    projected = sum_over_chan(part)
    wide = ((rows, 4 * depth * LANES), F32)
    stack = ((steps, depth, GROUPS, width), F32)
    delta, slope, local_states, ahead, payload = kernel(
        summary_kernel,
        (
            shape(2, rows, width),
            shape(2, rows, width),
            shape(4, depth, GROUPS, width),
            shape(4, GROUPS, width),
            shape(4, slots, width),
        ),
        20,
        (((rows, width), F32), stack, wide),
    )(projected, w_delta, bias, rates, signal_wide, cot_wide)
    parts = exchange(payload, along_y)
    copies = kernel(
        row_kernel,
        shape(shards // 4, slots, width, dtype=BF16),
        4,
        in_specs=[scalars, whole, whole],
        out_specs=whole,
    )(place, parts, flat)
    row_totals = exchange(copies, along_z)
    entries = kernel(
        entry_kernel,
        shape(4, slots, width),
        4,
        in_specs=[scalars, whole, whole, whole],
        out_specs=whole,
    )(place, row_totals, parts, flat)
    entries = exchange(entries, along_y)
    layer_out, grad_parts, direct = kernel(
        gradient_kernel,
        (
            shape(rows, width, dtype=BF16),
            shape(rows, columns, dtype=BF16),
            shape(rows, width),
        ),
        28,
        (
            ((rows, width), F32),
            ((rows, width), F32),
            ((2, rows, width), F32),
            stack,
            stack,
            ((4, rows * depth, width), BF16),
            wide,
        ),
    )(
        projected,
        w_delta,
        rates,
        gain,
        signal_wide,
        cot_wide,
        delta,
        slope,
        local_states,
        ahead,
        entries,
    )
    grad_proj = sum_over_chan(grad_parts)
    signal_grad = kernel(finish_kernel, shape(rows, width, dtype=BF16), 8)(
        grad_proj, w_turned, direct
    )
    return (layer_out, signal_grad)


def solution(mesh):
    in_specs = (
        P("seq", "chan"),
        P("seq", "chan"),
        P("chan", None),
        P(None, None, "chan"),
        P(None, "chan"),
        P(None, None, "chan"),
        P("chan"),
    )
    out_specs = (P("seq", "chan"), P("seq", "chan"))
    return jax.shard_map(local, mesh=mesh, in_specs=in_specs, out_specs=out_specs, check_vma=False)
```

```python
import math

import jax
import jax.numpy as jnp
from jax import lax
from jax.experimental import pallas as pl
from jax.experimental.pallas import tpu as pltpu
from jax.sharding import PartitionSpec as P

GROUPS = 8
LANES = 128
LOG2E = math.log2(math.e)
LN2 = math.log(2.0)
FAR = 1e30
NT = (((1,), (1,)), ((), ()))
F32 = jnp.float32
BF16 = jnp.bfloat16


def dot(a, b, dims=(((1,), (0,)), ((), ()))):
    return lax.dot_general(a, b, dims, preferred_element_type=F32)


def grouping(rows, inverse=False):
    steps = rows // GROUPS
    row = lax.broadcasted_iota(jnp.int32, (rows, rows), 1 if inverse else 0)
    token = lax.broadcasted_iota(jnp.int32, (rows, rows), 0 if inverse else 1)
    return jnp.where(token == (row % GROUPS) * steps + row // GROUPS, 1.0, 0.0).astype(BF16)


def project_kernel(signal, w_proj, signal_out, part_out, signal_here, w_here, done):
    fetches = [
        pltpu.make_async_copy(signal, signal_here, done.at[0]),
        pltpu.make_async_copy(w_proj, w_here, done.at[1]),
    ]
    for fetch in fetches:
        fetch.start()
    order = grouping(signal_here.shape[0])
    fetches[0].wait()
    grouped = dot(order, signal_here[...])
    signal_out[...] = grouped
    fetches[1].wait()
    part_out[...] = dot(grouped.astype(BF16), w_here[...], NT)


def pair_kernel(place, both, copies):
    half = both.shape[0] // 4
    start = pl.multiple_of(place[2] * half, half)
    total = both[pl.ds(start, half), :] + both[pl.ds(2 * half + start, half), :]
    for copy in range(copies.shape[0]):
        copies[copy] = total.astype(BF16)


def chips_kernel(parts, total):
    result = parts[0].astype(F32)
    for chip in range(1, parts.shape[0]):
        result = result + parts[chip].astype(F32)
    total[...] = result.astype(BF16)


def prepare_kernel(cotangent, decay_log, bias, skip_gain, cot_out, rates, flat, bias_out, gain_out):
    cot_out[...] = dot(grouping(cotangent.shape[0]), cotangent[...])
    bias_out[...] = bias[...]
    gain_out[...] = skip_gain[...]
    depth, _, width = decay_log.shape
    flat[...] = jnp.zeros_like(flat)
    for n in range(depth):
        scaled = -jnp.exp(decay_log[n]) * LOG2E
        for way in range(2):
            rates[way, n] = jnp.broadcast_to(scaled[way : way + 1], (GROUPS, width))
            flat[way, n : n + 1] = scaled[way : way + 1]


def at(step):
    return pl.ds(pl.multiple_of(step * GROUPS, GROUPS), GROUPS)


def lane_block(block):
    return slice(block * LANES, (block + 1) * LANES)


def spread_gates(gates, spread):
    count = gates.shape[1]
    for pair in range(count // 2):
        source = lax.broadcasted_iota(jnp.int32, (count, 2 * LANES), 0)
        lane = lax.broadcasted_iota(jnp.int32, (count, 2 * LANES), 1)
        pick = jnp.where(source == 2 * pair + lane // LANES, 1.0, 0.0).astype(BF16)
        spread[:, pair * 2 * LANES : (pair + 1) * 2 * LANES] = dot(gates, pick)


def gate_at(spread, step, column):
    return spread[at(step), column * LANES : (column + 1) * LANES]


def summary_kernel(
    projected,
    w_delta,
    bias,
    rates,
    signal,
    cot,
    delta_out,
    slope_out,
    local_out,
    ahead_out,
    payload,
    weight,
    fades,
    spread,
):
    rows, width = signal.shape
    rank = w_delta.shape[1]
    depth = rates.shape[1]
    steps = rows // GROUPS
    blocks = width // LANES
    spread_gates(projected[:, 2 * rank :], spread)
    payload[...] = jnp.zeros_like(payload)
    group = lax.broadcasted_iota(jnp.int32, (GROUPS, LANES), 0)
    for way in range(2):
        pre = dot(projected[:, way * rank : (way + 1) * rank], w_delta[way]) + bias[way : way + 1]
        delta = jnp.maximum(pre, 0.0) + jnp.log1p(jnp.exp(-jnp.abs(pre)))
        delta_out[way] = delta
        slope_out[way] = 1.0 / (1.0 + jnp.exp(-pre))
        weight[...] = delta * signal[...]
        falling = way == 1
        zero = jnp.zeros((GROUPS, LANES), F32)
        many = (zero,) * (blocks * depth)

        def walk_states(index, carry):
            states, total = carry
            step = steps - 1 - index if falling else index
            d = [delta_out[way, at(step), lane_block(block)] for block in range(blocks)]
            w = [weight[at(step), lane_block(block)] for block in range(blocks)]
            result = []
            for n in range(depth):
                gate = gate_at(spread, step, 2 * way * depth + n)
                for block in range(blocks):
                    fade = jnp.exp2(d[block] * rates[way, n, :, lane_block(block)])
                    fades[step, n, :, lane_block(block)] = fade
                    result.append(fade * states[n * blocks + block] + w[block] * gate)
            return (tuple(result), tuple(t + x for t, x in zip(total, d)))

        states, total = lax.fori_loop(0, steps, walk_states, (many, (zero,) * blocks))

        def walk_adjoints(index, carried):
            step = index if falling else steps - 1 - index
            g = [cot[at(step), lane_block(block)] for block in range(blocks)]
            result = []
            for n in range(depth):
                gate = gate_at(spread, step, (2 * way + 1) * depth + n)
                for block in range(blocks):
                    fade = fades[step, n, :, lane_block(block)]
                    result.append(fade * (g[block] * gate + carried[n * blocks + block]))
            return tuple(result)

        carried = lax.fori_loop(0, steps, walk_adjoints, many)
        for block in range(blocks):
            lanes = lane_block(block)

            def shift(array, by, down):
                return pltpu.roll(array, GROUPS - by if down else by, 0)

            def beyond(by, down):
                return group >= GROUPS - by if down else group < by

            whole = jnp.sum(total[block], 0, keepdims=True)
            for kind, down, finals in ((0, falling, states), (1, not falling, carried)):
                windows = []
                window = total[block]
                ahead = jnp.where(beyond(1, down), 0.0, shift(window, 1, down))
                for by in (1, 2, 4):
                    windows.append(jnp.where(beyond(by, down), FAR, window))
                    outside = beyond(by, down)
                    window = window + jnp.where(outside, 0.0, shift(window, by, down))
                    ahead = ahead + jnp.where(outside, 0.0, shift(ahead, by, down))
                ahead_out[2 * way + kind, :, lanes] = ahead
                edge = 0 if down else GROUPS - 1
                for n in range(depth):
                    rate = rates[way, n, :, lanes]
                    scanned = finals[n * blocks + block]
                    for by, span in zip((1, 2, 4), windows):
                        scanned = scanned + jnp.exp2(rate * span) * shift(scanned, by, down)
                    local_out[2 * way + kind, n, :, lanes] = jnp.where(
                        beyond(1, down), 0.0, shift(scanned, 1, down)
                    )
                    payload[2 * way + kind, n : n + 1, lanes] = scanned[edge : edge + 1]
                payload[2 * way + kind, depth : depth + 1, lanes] = whole


def fall_or_rise(kind, run):
    falling = jnp.logical_or(kind == 1, kind == 2)

    @pl.when(falling)
    def _():
        run(True)

    @pl.when(jnp.logical_not(falling))
    def _():
        run(False)


def order(count, falling):
    return range(count - 1, -1, -1) if falling else range(count)


def shard_fade(parts, flat, way, shard):
    depth = parts.shape[1] - 4
    return jnp.exp2(flat[way] * parts[shard, depth : depth + 1])


def row_kernel(place, parts, flat, copies):
    shards, slots, width = parts.shape
    depth = slots - 4
    kind = place[1]
    slot = lax.broadcasted_iota(jnp.int32, (slots, width), 0)

    def run(falling):
        state = jnp.zeros((slots, width), F32)
        for shard in order(shards, falling):
            state = shard_fade(parts, flat, kind // 2, shard) * state + parts[shard]
        total = parts[0, depth : depth + 1]
        for shard in range(1, shards):
            total = total + parts[shard, depth : depth + 1]
        coarse = total.astype(BF16).astype(F32)
        packed = jnp.where(slot == depth, coarse, state)
        packed = jnp.where(slot == depth + 1, total - coarse, packed).astype(BF16)
        for copy in range(copies.shape[0]):
            copies[copy] = packed

    fall_or_rise(kind, run)


def entry_kernel(place, rows, parts, flat, entries):
    count, slots, width = rows.shape
    shards = parts.shape[0]
    depth = slots - 4
    here = place[0]
    kind = place[1]
    rates = flat[kind // 2]

    def run(falling):
        state = jnp.zeros((slots, width), F32)
        for row in order(count, falling):
            block = rows[row].astype(F32)
            total = block[depth : depth + 1] + block[depth + 1 : depth + 2]
            passed = jnp.exp2(rates * total) * state + block
            before = row > here if falling else row < here
            state = jnp.where(before, passed, state)
        for shard in order(shards, falling):
            entries[shard] = state
            state = shard_fade(parts, flat, kind // 2, shard) * state + parts[shard]

    fall_or_rise(kind, run)


def gradient_kernel(
    projected,
    w_delta,
    rates,
    skip_gain,
    signal,
    cot,
    delta,
    slope,
    local,
    ahead,
    entries,
    layer_out,
    parts_out,
    direct_out,
    weight,
    core,
    grad_pre,
    fades,
    kept,
    products,
    spread,
):
    rows, width = signal.shape
    rank = w_delta.shape[1]
    depth = rates.shape[1]
    steps = rows // GROUPS
    blocks = width // LANES
    spread_gates(projected[:, 2 * rank :], spread)
    core[...] = skip_gain[...] * signal[...]
    direct_out[...] = skip_gain[...] * cot[...]
    for way in range(2):
        weight[...] = delta[way] * signal[...]
        falling = way == 1
        first = 2 * way * depth

        def entering(kind):
            gap = [ahead[2 * way + kind, :, lane_block(block)] for block in range(blocks)]
            return tuple(
                local[2 * way + kind, n, :, lane_block(block)]
                + jnp.exp2(gap[block] * rates[way, n, :, lane_block(block)])
                * entries[2 * way + kind, n : n + 1, lane_block(block)]
                for n in range(depth)
                for block in range(blocks)
            )

        def pieces(array, step):
            return [array[at(step), lane_block(block)] for block in range(blocks)]

        def put_products(which, step, rows_of):
            start = pl.multiple_of(step * depth * GROUPS, 2 * GROUPS)
            for block in range(blocks):
                stacked = jnp.concatenate(rows_of[block], 0).astype(BF16)
                products[which, pl.ds(start, depth * GROUPS), lane_block(block)] = stacked

        def walk_states(index, states):
            step = steps - 1 - index if falling else index
            d, w, g = pieces(delta.at[way], step), pieces(weight, step), pieces(cot, step)
            total = pieces(core, step)
            rows_of = [[] for _ in range(blocks)]
            result = []
            for n in range(depth):
                gate_in = gate_at(spread, step, first + n)
                gate_out = gate_at(spread, step, first + depth + n)
                for block in range(blocks):
                    lanes = lane_block(block)
                    fade = jnp.exp2(d[block] * rates[way, n, :, lanes])
                    fades[step, n, :, lanes] = fade
                    faded = fade * states[n * blocks + block]
                    kept[step, n, :, lanes] = faded
                    state = faded + w[block] * gate_in
                    total[block] = total[block] + gate_out * state
                    rows_of[block].append(g[block] * state)
                    result.append(state)
            for block in range(blocks):
                core[at(step), lane_block(block)] = total[block]
            put_products(2 * way + 1, step, rows_of)
            return tuple(result)

        lax.fori_loop(0, steps, walk_states, entering(0))

        def walk_adjoints(index, carried):
            step = index if falling else steps - 1 - index
            w, g = pieces(weight, step), pieces(cot, step)
            rows_of = [[] for _ in range(blocks)]
            through = [jnp.zeros((GROUPS, LANES), F32)] * blocks
            fading = [jnp.zeros((GROUPS, LANES), F32)] * blocks
            result = []
            for n in range(depth):
                gate_in = gate_at(spread, step, first + n)
                gate_out = gate_at(spread, step, first + depth + n)
                for block in range(blocks):
                    lanes = lane_block(block)
                    adjoint = g[block] * gate_out + carried[n * blocks + block]
                    result.append(fades[step, n, :, lanes] * adjoint)
                    through[block] = through[block] + adjoint * gate_in
                    fading[block] = fading[block] + (
                        adjoint * kept[step, n, :, lanes] * rates[way, n, :, lanes]
                    )
                    rows_of[block].append(adjoint * w[block])
            put_products(2 * way, step, rows_of)
            for block in range(blocks):
                lanes = lane_block(block)
                grad_delta = through[block] * signal[at(step), lanes] + fading[block] * LN2
                direct_out[at(step), lanes] = (
                    direct_out[at(step), lanes] + through[block] * delta[way, at(step), lanes]
                )
                grad_pre[way, at(step), lanes] = grad_delta * slope[way, at(step), lanes]
            return tuple(result)

        lax.fori_loop(0, steps, walk_adjoints, entering(1))

    for way in range(2):
        parts_out[:, way * rank : (way + 1) * rank] = dot(
            grad_pre[way].astype(BF16), w_delta[way], NT
        )
    ones = jnp.ones((width, LANES), BF16)
    lane = lax.broadcasted_iota(jnp.int32, (GROUPS, LANES), 1)
    height = depth * GROUPS
    for start in range(0, steps, 4):
        merged = [jnp.zeros((GROUPS, LANES), F32)] * 4
        for which in range(4):
            sums = dot(products[which, start * height : (start + 4) * height], ones)
            for step in range(4):
                for n in range(depth):
                    row = step * height + n * GROUPS
                    merged[step] = jnp.where(
                        lane == which * depth + n, sums[row : row + GROUPS], merged[step]
                    )
        stacked = jnp.concatenate(merged, 0)[:, : 4 * depth]
        parts_out[start * GROUPS : (start + 4) * GROUPS, 2 * rank :] = stacked
    ungroup = grouping(rows, inverse=True)
    layer_out[...] = dot(ungroup, core[...].astype(BF16)).astype(BF16)


def finish_kernel(grad_proj, w_proj, direct, signal_grad):
    total = dot(grad_proj[...], w_proj[...]) + direct[...]
    ungroup = grouping(direct.shape[0], inverse=True)
    signal_grad[...] = dot(ungroup, total.astype(BF16)).astype(BF16)


def shape(*dims, dtype=F32):
    return jax.ShapeDtypeStruct(dims, dtype)


WHOLE = pl.BlockSpec(memory_space=pltpu.VMEM)
SCALARS = pl.BlockSpec(memory_space=pltpu.SMEM)


def kernel(body, out_shape, mebibytes, scratch=(), cost=0, **more):
    return pl.pallas_call(
        body,
        out_shape=out_shape,
        scratch_shapes=[
            pltpu.VMEM(*each) if isinstance(each, tuple) else each for each in scratch
        ],
        compiler_params=pltpu.CompilerParams(vmem_limit_bytes=mebibytes << 20),
        cost_estimate=pl.CostEstimate(flops=cost, bytes_accessed=cost, transcendentals=0),
        name=body.__name__,
        **more,
    )


def sum_over_chan(part, place):
    count = lax.axis_size("chan")
    rows, columns = part.shape
    pairs = [[2 * chip, 2 * chip + 1] for chip in range(count // 2)]
    across = [list(range(core, count, 2)) for core in range(2)]
    both = lax.all_gather(part, "chan", axis=0, tiled=True, axis_index_groups=pairs)
    copies = kernel(
        pair_kernel,
        shape(count // 2, rows // 2, columns, dtype=BF16),
        4,
        in_specs=[SCALARS, WHOLE],
        out_specs=WHOLE,
    )(place, both)
    parts = lax.all_to_all(copies, "chan", 0, 0, tiled=True, axis_index_groups=across)
    half = kernel(chips_kernel, shape(rows // 2, columns, dtype=BF16), 4)(parts)
    return lax.all_gather(half, "chan", axis=0, tiled=True, axis_index_groups=pairs)


def local(signal, cotangent, w_proj, w_delta, delta_bias, decay_log, skip_gain):
    rows, width = signal.shape
    columns = w_proj.shape[1]
    depth = decay_log.shape[1]
    steps = rows // GROUPS
    shards = lax.axis_size("seq")
    if shards % 4:
        raise ValueError("shard count")
    w_turned = w_proj.T
    shard = lax.axis_index("seq").astype(jnp.int32)
    core = lax.axis_index("chan").astype(jnp.int32) % 2
    place = jnp.stack([shard // 4, shard % 4, core])
    along_y = [[z * 4 + y for y in range(4)] for z in range(shards // 4)]
    along_z = [[z * 4 + y for z in range(shards // 4)] for y in range(4)]
    slots = depth + 4

    def exchange(array, groups):
        return lax.all_to_all(array, "seq", 0, 0, tiled=True, axis_index_groups=groups)

    signal_wide, part = kernel(
        project_kernel,
        (shape(rows, width), shape(rows, columns)),
        8,
        (((rows, width), BF16), ((columns, width), BF16), pltpu.SemaphoreType.DMA((2,))),
        in_specs=[pl.BlockSpec(memory_space=pltpu.HBM)] * 2,
        out_specs=(WHOLE, WHOLE),
    )(*(pltpu.with_memory_space_constraint(each, pltpu.HBM) for each in (signal, w_turned)))
    cot_wide, rates, flat, bias, gain = kernel(
        prepare_kernel,
        (
            shape(rows, width),
            shape(2, depth, GROUPS, width),
            shape(2, slots, width),
            shape(2, width),
            shape(1, width),
        ),
        8,
        cost=1 << 20,
    )(cotangent, decay_log.transpose(1, 0, 2), delta_bias, skip_gain.reshape(1, width))
    projected = sum_over_chan(part, place)
    wide = ((rows, 4 * depth * LANES), F32)
    stack = ((steps, depth, GROUPS, width), F32)
    delta, slope, local_states, ahead, payload = kernel(
        summary_kernel,
        (
            shape(2, rows, width),
            shape(2, rows, width),
            shape(4, depth, GROUPS, width),
            shape(4, GROUPS, width),
            shape(4, slots, width),
        ),
        20,
        (((rows, width), F32), stack, wide),
    )(projected, w_delta, bias, rates, signal_wide, cot_wide)
    parts = exchange(payload, along_y)
    copies = kernel(
        row_kernel,
        shape(shards // 4, slots, width, dtype=BF16),
        4,
        in_specs=[SCALARS, WHOLE, WHOLE],
        out_specs=WHOLE,
    )(place, parts, flat)
    row_totals = exchange(copies, along_z)
    entries = kernel(
        entry_kernel,
        shape(4, slots, width),
        4,
        in_specs=[SCALARS, WHOLE, WHOLE, WHOLE],
        out_specs=WHOLE,
    )(place, row_totals, parts, flat)
    entries = exchange(entries, along_y)
    layer_out, grad_parts, direct = kernel(
        gradient_kernel,
        (
            shape(rows, width, dtype=BF16),
            shape(rows, columns),
            shape(rows, width),
        ),
        28,
        (
            ((rows, width), F32),
            ((rows, width), F32),
            ((2, rows, width), F32),
            stack,
            stack,
            ((4, rows * depth, width), BF16),
            wide,
        ),
    )(
        projected,
        w_delta,
        rates,
        gain,
        signal_wide,
        cot_wide,
        delta,
        slope,
        local_states,
        ahead,
        entries,
    )
    grad_proj = sum_over_chan(grad_parts, place)
    signal_grad = kernel(finish_kernel, shape(rows, width, dtype=BF16), 8)(
        grad_proj, w_turned, direct
    )
    return (layer_out, signal_grad)


def solution(mesh):
    in_specs = (
        P("seq", "chan"),
        P("seq", "chan"),
        P("chan", None),
        P(None, None, "chan"),
        P(None, "chan"),
        P(None, None, "chan"),
        P("chan"),
    )
    out_specs = (P("seq", "chan"), P("seq", "chan"))
    return jax.shard_map(local, mesh=mesh, in_specs=in_specs, out_specs=out_specs, check_vma=False)
```

```python
import math

import jax
import jax.numpy as jnp
from jax import lax
from jax.experimental import pallas as pl
from jax.experimental.pallas import tpu as pltpu
from jax.sharding import PartitionSpec as P

GROUPS = 8
LANES = 128
LOG2E = math.log2(math.e)
LN2 = math.log(2.0)
FAR = 1e30
NT = (((1,), (1,)), ((), ()))
F32 = jnp.float32
BF16 = jnp.bfloat16


def dot(a, b, dims=(((1,), (0,)), ((), ()))):
    return lax.dot_general(a, b, dims, preferred_element_type=F32)


def grouping(rows, inverse=False):
    steps = rows // GROUPS
    row = lax.broadcasted_iota(jnp.int32, (rows, rows), 1 if inverse else 0)
    token = lax.broadcasted_iota(jnp.int32, (rows, rows), 0 if inverse else 1)
    return jnp.where(token == (row % GROUPS) * steps + row // GROUPS, 1.0, 0.0).astype(BF16)


def project_kernel(signal, w_proj, signal_out, part_out, signal_here, w_here, done):
    fetches = [
        pltpu.make_async_copy(signal, signal_here, done.at[0]),
        pltpu.make_async_copy(w_proj, w_here, done.at[1]),
    ]
    for fetch in fetches:
        fetch.start()
    order = grouping(signal_here.shape[0])
    fetches[0].wait()
    grouped = dot(order, signal_here[...])
    signal_out[...] = grouped
    fetches[1].wait()
    part_out[...] = dot(grouped.astype(BF16), w_here[...], NT)


def pair_kernel(both, copies):
    half = both.shape[0] // 4
    start = pl.multiple_of(lax.axis_index("chan") % 2 * half, half)
    total = both[pl.ds(start, half), :] + both[pl.ds(2 * half + start, half), :]
    for copy in range(copies.shape[0]):
        copies[copy] = total.astype(BF16)


def chips_kernel(parts, total):
    result = parts[0].astype(F32)
    for chip in range(1, parts.shape[0]):
        result = result + parts[chip].astype(F32)
    total[...] = result.astype(BF16)


def prepare_kernel(cotangent, decay_log, bias, skip_gain, cot_out, rates, flat, bias_out, gain_out):
    cot_out[...] = dot(grouping(cotangent.shape[0]), cotangent[...])
    bias_out[...] = bias[...]
    gain_out[...] = skip_gain[...]
    depth, _, width = decay_log.shape
    flat[...] = jnp.zeros_like(flat)
    for n in range(depth):
        scaled = -jnp.exp(decay_log[n]) * LOG2E
        for way in range(2):
            rates[way, n] = jnp.broadcast_to(scaled[way : way + 1], (GROUPS, width))
            flat[way, n : n + 1] = scaled[way : way + 1]


def at(step):
    return pl.ds(pl.multiple_of(step * GROUPS, GROUPS), GROUPS)


def lane_block(block):
    return slice(block * LANES, (block + 1) * LANES)


def spread_gates(gates, spread):
    count = gates.shape[1]
    for pair in range(count // 2):
        source = lax.broadcasted_iota(jnp.int32, (count, 2 * LANES), 0)
        lane = lax.broadcasted_iota(jnp.int32, (count, 2 * LANES), 1)
        pick = jnp.where(source == 2 * pair + lane // LANES, 1.0, 0.0).astype(BF16)
        spread[:, pair * 2 * LANES : (pair + 1) * 2 * LANES] = dot(gates, pick)


def gate_at(spread, step, column):
    return spread[at(step), column * LANES : (column + 1) * LANES]


def put_total(shares, kind, lanes, total):
    depth = shares.shape[1] - 4
    coarse = total.astype(BF16).astype(F32)
    shares[kind, depth : depth + 1, lanes] = coarse
    shares[kind, depth + 1 : depth + 2, lanes] = total - coarse


def summary_kernel(
    projected,
    w_delta,
    bias,
    rates,
    signal,
    cot,
    delta_out,
    slope_out,
    local_out,
    ahead_out,
    payload,
    weight,
    fades,
    spread,
    shares,
):
    rows, width = signal.shape
    rank = w_delta.shape[1]
    depth = rates.shape[1]
    steps = rows // GROUPS
    blocks = width // LANES
    spread_gates(projected[:, 2 * rank :], spread)
    shares[...] = jnp.zeros_like(shares)
    group = lax.broadcasted_iota(jnp.int32, (GROUPS, LANES), 0)
    for way in range(2):
        pre = dot(projected[:, way * rank : (way + 1) * rank], w_delta[way]) + bias[way : way + 1]
        delta = jnp.maximum(pre, 0.0) + jnp.log1p(jnp.exp(-jnp.abs(pre)))
        delta_out[way] = delta
        slope_out[way] = 1.0 / (1.0 + jnp.exp(-pre))
        weight[...] = delta * signal[...]
        falling = way == 1
        zero = jnp.zeros((GROUPS, LANES), F32)
        many = (zero,) * (blocks * depth)

        def walk_states(index, carry):
            states, total = carry
            step = steps - 1 - index if falling else index
            d = [delta_out[way, at(step), lane_block(block)] for block in range(blocks)]
            w = [weight[at(step), lane_block(block)] for block in range(blocks)]
            result = []
            for n in range(depth):
                gate = gate_at(spread, step, 2 * way * depth + n)
                for block in range(blocks):
                    fade = jnp.exp2(d[block] * rates[way, n, :, lane_block(block)])
                    fades[step, n, :, lane_block(block)] = fade
                    result.append(fade * states[n * blocks + block] + w[block] * gate)
            return (tuple(result), tuple(t + x for t, x in zip(total, d)))

        states, total = lax.fori_loop(0, steps, walk_states, (many, (zero,) * blocks))

        def walk_adjoints(index, carried):
            step = index if falling else steps - 1 - index
            g = [cot[at(step), lane_block(block)] for block in range(blocks)]
            result = []
            for n in range(depth):
                gate = gate_at(spread, step, (2 * way + 1) * depth + n)
                for block in range(blocks):
                    fade = fades[step, n, :, lane_block(block)]
                    result.append(fade * (g[block] * gate + carried[n * blocks + block]))
            return tuple(result)

        carried = lax.fori_loop(0, steps, walk_adjoints, many)
        for block in range(blocks):
            lanes = lane_block(block)

            def shift(array, by, down):
                return pltpu.roll(array, GROUPS - by if down else by, 0)

            def beyond(by, down):
                return group >= GROUPS - by if down else group < by

            whole = jnp.sum(total[block], 0, keepdims=True)
            for kind, down, finals in ((0, falling, states), (1, not falling, carried)):
                windows = []
                window = total[block]
                ahead = jnp.where(beyond(1, down), 0.0, shift(window, 1, down))
                for by in (1, 2, 4):
                    windows.append(jnp.where(beyond(by, down), FAR, window))
                    outside = beyond(by, down)
                    window = window + jnp.where(outside, 0.0, shift(window, by, down))
                    ahead = ahead + jnp.where(outside, 0.0, shift(ahead, by, down))
                ahead_out[2 * way + kind, :, lanes] = ahead
                edge = 0 if down else GROUPS - 1
                for n in range(depth):
                    rate = rates[way, n, :, lanes]
                    scanned = finals[n * blocks + block]
                    for by, span in zip((1, 2, 4), windows):
                        scanned = scanned + jnp.exp2(rate * span) * shift(scanned, by, down)
                    local_out[2 * way + kind, n, :, lanes] = jnp.where(
                        beyond(1, down), 0.0, shift(scanned, 1, down)
                    )
                    shares[2 * way + kind, n : n + 1, lanes] = scanned[edge : edge + 1]
                put_total(shares, 2 * way + kind, lanes, whole)
    payload[0] = shares[...].astype(BF16)
    for copy in range(1, payload.shape[0]):
        payload[copy] = payload[0]


RISING = (0, 3)
FALLING = (1, 2)


def order(count, falling):
    return range(count - 1, -1, -1) if falling else range(count)


def pass_by(state, block, rates):
    depth = block.shape[0] - 4
    total = block[depth : depth + 1] + block[depth + 1 : depth + 2]
    return jnp.exp2(rates * total) * state + block


def row_kernel(parts, flat, copies):
    shards, _, slots, width = parts.shape
    depth = slots - 4
    here = lax.axis_index("seq") // shards
    slot = lax.broadcasted_iota(jnp.int32, (slots, width), 0)
    packed = []
    for kind in range(4):
        state = jnp.zeros((slots, width), F32)
        total = jnp.zeros((1, width), F32)
        for shard in order(shards, kind in FALLING):
            block = parts[shard, kind].astype(F32)
            total = total + block[depth : depth + 1] + block[depth + 1 : depth + 2]
            state = pass_by(state, block, flat[kind // 2])
        coarse = total.astype(BF16).astype(F32)
        state = jnp.where(slot == depth, coarse, state)
        state = jnp.where(slot == depth + 1, total - coarse, state)
        packed.append(jnp.where(slot > depth + 1, 0.0, state).astype(BF16))
    for row in range(copies.shape[0]):

        @pl.when(row > here)
        def _():
            for place, kind in enumerate(RISING):
                copies[row, place] = packed[kind]

        @pl.when(row <= here)
        def _():
            for place, kind in enumerate(FALLING):
                copies[row, place] = packed[kind]


def entry_kernel(rows, parts, flat, entries):
    count, _, slots, width = rows.shape
    shards = parts.shape[0]
    place = lax.axis_index("seq")
    row_here = place // shards
    here = place % shards
    for falling, kinds in ((False, RISING), (True, FALLING)):
        for slot, kind in enumerate(kinds):
            rates = flat[kind // 2]
            state = jnp.zeros((slots, width), F32)
            for row in order(count, falling):
                passed = pass_by(state, rows[row, slot].astype(F32), rates)
                state = jnp.where(row > row_here if falling else row < row_here, passed, state)
            for shard in order(shards, falling):
                passed = pass_by(state, parts[shard, kind].astype(F32), rates)
                state = jnp.where(shard > here if falling else shard < here, passed, state)
            entries[kind] = state


def gradient_kernel(
    projected,
    w_delta,
    rates,
    skip_gain,
    signal,
    cot,
    delta,
    slope,
    local,
    ahead,
    entries,
    layer_out,
    parts_out,
    direct_out,
    weight,
    core,
    grad_pre,
    fades,
    kept,
    products,
    spread,
):
    rows, width = signal.shape
    rank = w_delta.shape[1]
    depth = rates.shape[1]
    steps = rows // GROUPS
    blocks = width // LANES
    spread_gates(projected[:, 2 * rank :], spread)
    core[...] = skip_gain[...] * signal[...]
    direct_out[...] = skip_gain[...] * cot[...]
    for way in range(2):
        weight[...] = delta[way] * signal[...]
        falling = way == 1
        first = 2 * way * depth

        def entering(kind):
            gap = [ahead[2 * way + kind, :, lane_block(block)] for block in range(blocks)]
            return tuple(
                local[2 * way + kind, n, :, lane_block(block)]
                + jnp.exp2(gap[block] * rates[way, n, :, lane_block(block)])
                * entries[2 * way + kind, n : n + 1, lane_block(block)]
                for n in range(depth)
                for block in range(blocks)
            )

        def pieces(array, step):
            return [array[at(step), lane_block(block)] for block in range(blocks)]

        def put_products(which, step, rows_of):
            start = pl.multiple_of(step * depth * GROUPS, 2 * GROUPS)
            for block in range(blocks):
                stacked = jnp.concatenate(rows_of[block], 0).astype(BF16)
                products[which, pl.ds(start, depth * GROUPS), lane_block(block)] = stacked

        def walk_states(index, states):
            step = steps - 1 - index if falling else index
            d, w, g = pieces(delta.at[way], step), pieces(weight, step), pieces(cot, step)
            total = pieces(core, step)
            rows_of = [[] for _ in range(blocks)]
            result = []
            for n in range(depth):
                gate_in = gate_at(spread, step, first + n)
                gate_out = gate_at(spread, step, first + depth + n)
                for block in range(blocks):
                    lanes = lane_block(block)
                    fade = jnp.exp2(d[block] * rates[way, n, :, lanes])
                    fades[step, n, :, lanes] = fade
                    faded = fade * states[n * blocks + block]
                    kept[step, n, :, lanes] = faded
                    state = faded + w[block] * gate_in
                    total[block] = total[block] + gate_out * state
                    rows_of[block].append(g[block] * state)
                    result.append(state)
            for block in range(blocks):
                core[at(step), lane_block(block)] = total[block]
            put_products(2 * way + 1, step, rows_of)
            return tuple(result)

        lax.fori_loop(0, steps, walk_states, entering(0))

        def walk_adjoints(index, carried):
            step = index if falling else steps - 1 - index
            w, g = pieces(weight, step), pieces(cot, step)
            rows_of = [[] for _ in range(blocks)]
            through = [jnp.zeros((GROUPS, LANES), F32)] * blocks
            fading = [jnp.zeros((GROUPS, LANES), F32)] * blocks
            result = []
            for n in range(depth):
                gate_in = gate_at(spread, step, first + n)
                gate_out = gate_at(spread, step, first + depth + n)
                for block in range(blocks):
                    lanes = lane_block(block)
                    adjoint = g[block] * gate_out + carried[n * blocks + block]
                    result.append(fades[step, n, :, lanes] * adjoint)
                    through[block] = through[block] + adjoint * gate_in
                    fading[block] = fading[block] + (
                        adjoint * kept[step, n, :, lanes] * rates[way, n, :, lanes]
                    )
                    rows_of[block].append(adjoint * w[block])
            put_products(2 * way, step, rows_of)
            for block in range(blocks):
                lanes = lane_block(block)
                grad_delta = through[block] * signal[at(step), lanes] + fading[block] * LN2
                direct_out[at(step), lanes] = (
                    direct_out[at(step), lanes] + through[block] * delta[way, at(step), lanes]
                )
                grad_pre[way, at(step), lanes] = grad_delta * slope[way, at(step), lanes]
            return tuple(result)

        lax.fori_loop(0, steps, walk_adjoints, entering(1))

    for way in range(2):
        parts_out[:, way * rank : (way + 1) * rank] = dot(
            grad_pre[way].astype(BF16), w_delta[way], NT
        )
    ones = jnp.ones((width, LANES), BF16)
    lane = lax.broadcasted_iota(jnp.int32, (GROUPS, LANES), 1)
    height = depth * GROUPS
    for start in range(0, steps, 4):
        merged = [jnp.zeros((GROUPS, LANES), F32)] * 4
        for which in range(4):
            sums = dot(products[which, start * height : (start + 4) * height], ones)
            for step in range(4):
                for n in range(depth):
                    row = step * height + n * GROUPS
                    merged[step] = jnp.where(
                        lane == which * depth + n, sums[row : row + GROUPS], merged[step]
                    )
        stacked = jnp.concatenate(merged, 0)[:, : 4 * depth]
        parts_out[start * GROUPS : (start + 4) * GROUPS, 2 * rank :] = stacked
    ungroup = grouping(rows, inverse=True)
    layer_out[...] = dot(ungroup, core[...].astype(BF16)).astype(BF16)


def finish_kernel(grad_proj, w_proj, direct, signal_grad):
    total = dot(grad_proj[...], w_proj[...]) + direct[...]
    ungroup = grouping(direct.shape[0], inverse=True)
    signal_grad[...] = dot(ungroup, total.astype(BF16)).astype(BF16)


def shape(*dims, dtype=F32):
    return jax.ShapeDtypeStruct(dims, dtype)


WHOLE = pl.BlockSpec(memory_space=pltpu.VMEM)


def kernel(body, out_shape, mebibytes, scratch=(), cost=0, **more):
    return pl.pallas_call(
        body,
        out_shape=out_shape,
        scratch_shapes=[
            pltpu.VMEM(*each) if isinstance(each, tuple) else each for each in scratch
        ],
        compiler_params=pltpu.CompilerParams(vmem_limit_bytes=mebibytes << 20),
        cost_estimate=pl.CostEstimate(flops=cost, bytes_accessed=cost, transcendentals=0),
        name=body.__name__,
        **more,
    )


def sum_over_chan(part):
    count = lax.axis_size("chan")
    rows, columns = part.shape
    pairs = [[2 * chip, 2 * chip + 1] for chip in range(count // 2)]
    across = [list(range(core, count, 2)) for core in range(2)]
    both = lax.all_gather(part, "chan", axis=0, tiled=True, axis_index_groups=pairs)
    copies = kernel(
        pair_kernel,
        shape(count // 2, rows // 2, columns, dtype=BF16),
        4,
    )(both)
    parts = lax.all_to_all(copies, "chan", 0, 0, tiled=True, axis_index_groups=across)
    half = kernel(chips_kernel, shape(rows // 2, columns, dtype=BF16), 4)(parts)
    return lax.all_gather(half, "chan", axis=0, tiled=True, axis_index_groups=pairs)


def local(signal, cotangent, w_proj, w_delta, delta_bias, decay_log, skip_gain):
    rows, width = signal.shape
    columns = w_proj.shape[1]
    depth = decay_log.shape[1]
    steps = rows // GROUPS
    shards = lax.axis_size("seq")
    if shards % 4:
        raise ValueError("shard count")
    w_turned = w_proj.T
    along_y = [[z * 4 + y for y in range(4)] for z in range(shards // 4)]
    along_z = [[z * 4 + y for z in range(shards // 4)] for y in range(4)]
    slots = depth + 4

    def exchange(array, groups):
        return lax.all_to_all(array, "seq", 0, 0, tiled=True, axis_index_groups=groups)

    signal_wide, part = kernel(
        project_kernel,
        (shape(rows, width), shape(rows, columns)),
        8,
        (((rows, width), BF16), ((columns, width), BF16), pltpu.SemaphoreType.DMA((2,))),
        in_specs=[pl.BlockSpec(memory_space=pltpu.HBM)] * 2,
        out_specs=(WHOLE, WHOLE),
    )(*(pltpu.with_memory_space_constraint(each, pltpu.HBM) for each in (signal, w_turned)))
    cot_wide, rates, flat, bias, gain = kernel(
        prepare_kernel,
        (
            shape(rows, width),
            shape(2, depth, GROUPS, width),
            shape(2, slots, width),
            shape(2, width),
            shape(1, width),
        ),
        8,
        cost=1 << 20,
    )(cotangent, decay_log.transpose(1, 0, 2), delta_bias, skip_gain.reshape(1, width))
    projected = sum_over_chan(part)
    wide = ((rows, 4 * depth * LANES), F32)
    stack = ((steps, depth, GROUPS, width), F32)
    delta, slope, local_states, ahead, payload = kernel(
        summary_kernel,
        (
            shape(2, rows, width),
            shape(2, rows, width),
            shape(4, depth, GROUPS, width),
            shape(4, GROUPS, width),
            shape(4, 4, slots, width, dtype=BF16),
        ),
        20,
        (((rows, width), F32), stack, wide, ((4, slots, width), F32)),
    )(projected, w_delta, bias, rates, signal_wide, cot_wide)
    parts = exchange(payload, along_y)
    copies = kernel(row_kernel, shape(shards // 4, 2, slots, width, dtype=BF16), 4)(parts, flat)
    row_totals = exchange(copies, along_z)
    entries = kernel(entry_kernel, shape(4, slots, width), 4)(row_totals, parts, flat)
    layer_out, grad_parts, direct = kernel(
        gradient_kernel,
        (
            shape(rows, width, dtype=BF16),
            shape(rows, columns),
            shape(rows, width),
        ),
        28,
        (
            ((rows, width), F32),
            ((rows, width), F32),
            ((2, rows, width), F32),
            stack,
            stack,
            ((4, rows * depth, width), BF16),
            wide,
        ),
    )(
        projected,
        w_delta,
        rates,
        gain,
        signal_wide,
        cot_wide,
        delta,
        slope,
        local_states,
        ahead,
        entries,
    )
    grad_proj = sum_over_chan(grad_parts)
    signal_grad = kernel(finish_kernel, shape(rows, width, dtype=BF16), 8)(
        grad_proj, w_turned, direct
    )
    return (layer_out, signal_grad)


def solution(mesh):
    in_specs = (
        P("seq", "chan"),
        P("seq", "chan"),
        P("chan", None),
        P(None, None, "chan"),
        P(None, "chan"),
        P(None, None, "chan"),
        P("chan"),
    )
    out_specs = (P("seq", "chan"), P("seq", "chan"))
    return jax.shard_map(local, mesh=mesh, in_specs=in_specs, out_specs=out_specs, check_vma=False)
```

```python
import math

import jax
import jax.numpy as jnp
from jax import lax
from jax.experimental import pallas as pl
from jax.experimental.pallas import tpu as pltpu
from jax.sharding import PartitionSpec as P

GROUPS = 8
LANES = 128
LOG2E = math.log2(math.e)
LN2 = math.log(2.0)
FAR = 1e30
NT = (((1,), (1,)), ((), ()))
F32 = jnp.float32
BF16 = jnp.bfloat16


def dot(a, b, dims=(((1,), (0,)), ((), ()))):
    return lax.dot_general(a, b, dims, preferred_element_type=F32)


def grouping(rows, inverse=False):
    steps = rows // GROUPS
    row = lax.broadcasted_iota(jnp.int32, (rows, rows), 1 if inverse else 0)
    token = lax.broadcasted_iota(jnp.int32, (rows, rows), 0 if inverse else 1)
    return jnp.where(token == (row % GROUPS) * steps + row // GROUPS, 1.0, 0.0).astype(BF16)


def project_kernel(signal, w_proj, signal_out, part_out, signal_here, w_here, done):
    fetches = [
        pltpu.make_async_copy(signal, signal_here, done.at[0]),
        pltpu.make_async_copy(w_proj, w_here, done.at[1]),
    ]
    for fetch in fetches:
        fetch.start()
    order = grouping(signal_here.shape[0])
    fetches[0].wait()
    grouped = dot(order, signal_here[...])
    signal_out[...] = grouped
    fetches[1].wait()
    part_out[...] = dot(grouped.astype(BF16), w_here[...], NT)


def pair_kernel(both, copies):
    half = both.shape[0] // 4
    start = pl.multiple_of(lax.axis_index("chan") % 2 * half, half)
    total = both[pl.ds(start, half), :] + both[pl.ds(2 * half + start, half), :]
    for copy in range(copies.shape[0]):
        copies[copy] = total.astype(BF16)


def chips_kernel(parts, total):
    result = parts[0].astype(F32)
    for chip in range(1, parts.shape[0]):
        result = result + parts[chip].astype(F32)
    total[...] = result.astype(BF16)


def prepare_kernel(cotangent, decay_log, bias, skip_gain, cot_out, rates, flat, bias_out, gain_out):
    cot_out[...] = dot(grouping(cotangent.shape[0]), cotangent[...])
    bias_out[...] = bias[...]
    gain_out[...] = skip_gain[...]
    depth, _, width = decay_log.shape
    flat[...] = jnp.zeros_like(flat)
    for n in range(depth):
        scaled = -jnp.exp(decay_log[n]) * LOG2E
        for way in range(2):
            rates[way, n] = jnp.broadcast_to(scaled[way : way + 1], (GROUPS, width))
            flat[way, n : n + 1] = scaled[way : way + 1]


def at(step):
    return pl.ds(pl.multiple_of(step * GROUPS, GROUPS), GROUPS)


def lane_block(block):
    return slice(block * LANES, (block + 1) * LANES)


def spread_gates(gates, spread, first=0):
    count = gates.shape[1]
    for pair in range(spread.shape[1] // (2 * LANES)):
        source = lax.broadcasted_iota(jnp.int32, (count, 2 * LANES), 0)
        lane = lax.broadcasted_iota(jnp.int32, (count, 2 * LANES), 1)
        pick = jnp.where(source == first + 2 * pair + lane // LANES, 1.0, 0.0).astype(BF16)
        spread[:, pair * 2 * LANES : (pair + 1) * 2 * LANES] = dot(gates, pick)


def gate_at(spread, step, column):
    return spread[at(step), column * LANES : (column + 1) * LANES]


def put_total(shares, kind, lanes, total):
    depth = shares.shape[1] - 4
    coarse = total.astype(BF16).astype(F32)
    shares[kind, depth : depth + 1, lanes] = coarse
    shares[kind, depth + 1 : depth + 2, lanes] = total - coarse


def summary_kernel(
    projected,
    w_delta,
    bias,
    rates,
    signal,
    cot,
    delta_out,
    slope_out,
    local_out,
    ahead_out,
    payload,
    weight,
    fades,
    spread,
    shares,
):
    rows, width = signal.shape
    rank = w_delta.shape[1]
    depth = rates.shape[1]
    steps = rows // GROUPS
    blocks = width // LANES
    spread_gates(projected[:, 2 * rank :], spread)
    shares[...] = jnp.zeros_like(shares)
    group = lax.broadcasted_iota(jnp.int32, (GROUPS, LANES), 0)
    for way in range(2):
        pre = dot(projected[:, way * rank : (way + 1) * rank], w_delta[way]) + bias[way : way + 1]
        delta = jnp.maximum(pre, 0.0) + jnp.log1p(jnp.exp(-jnp.abs(pre)))
        delta_out[way] = delta
        slope_out[way] = 1.0 / (1.0 + jnp.exp(-pre))
        weight[...] = delta * signal[...]
        falling = way == 1
        zero = jnp.zeros((GROUPS, LANES), F32)
        many = (zero,) * (blocks * depth)

        def walk_states(index, carry):
            states, total = carry
            step = steps - 1 - index if falling else index
            d = [delta_out[way, at(step), lane_block(block)] for block in range(blocks)]
            w = [weight[at(step), lane_block(block)] for block in range(blocks)]
            result = []
            for n in range(depth):
                gate = gate_at(spread, step, 2 * way * depth + n)
                for block in range(blocks):
                    fade = jnp.exp2(d[block] * rates[way, n, :, lane_block(block)])
                    fades[step, n, :, lane_block(block)] = fade
                    result.append(fade * states[n * blocks + block] + w[block] * gate)
            return (tuple(result), tuple(t + x for t, x in zip(total, d)))

        states, total = lax.fori_loop(0, steps, walk_states, (many, (zero,) * blocks))

        def walk_adjoints(index, carried):
            step = index if falling else steps - 1 - index
            g = [cot[at(step), lane_block(block)] for block in range(blocks)]
            result = []
            for n in range(depth):
                gate = gate_at(spread, step, (2 * way + 1) * depth + n)
                for block in range(blocks):
                    fade = fades[step, n, :, lane_block(block)]
                    result.append(fade * (g[block] * gate + carried[n * blocks + block]))
            return tuple(result)

        carried = lax.fori_loop(0, steps, walk_adjoints, many)
        for block in range(blocks):
            lanes = lane_block(block)

            def shift(array, by, down):
                return pltpu.roll(array, GROUPS - by if down else by, 0)

            def beyond(by, down):
                return group >= GROUPS - by if down else group < by

            whole = jnp.sum(total[block], 0, keepdims=True)
            for kind, down, finals in ((0, falling, states), (1, not falling, carried)):
                windows = []
                window = total[block]
                ahead = jnp.where(beyond(1, down), 0.0, shift(window, 1, down))
                for by in (1, 2, 4):
                    windows.append(jnp.where(beyond(by, down), FAR, window))
                    outside = beyond(by, down)
                    window = window + jnp.where(outside, 0.0, shift(window, by, down))
                    ahead = ahead + jnp.where(outside, 0.0, shift(ahead, by, down))
                ahead_out[2 * way + kind, :, lanes] = ahead
                edge = 0 if down else GROUPS - 1
                for n in range(depth):
                    rate = rates[way, n, :, lanes]
                    scanned = finals[n * blocks + block]
                    for by, span in zip((1, 2, 4), windows):
                        scanned = scanned + jnp.exp2(rate * span) * shift(scanned, by, down)
                    local_out[2 * way + kind, n, :, lanes] = jnp.where(
                        beyond(1, down), 0.0, shift(scanned, 1, down)
                    )
                    shares[2 * way + kind, n : n + 1, lanes] = scanned[edge : edge + 1]
                put_total(shares, 2 * way + kind, lanes, whole)
    for shard in range(payload.shape[0]):
        way = shard % 2
        payload[shard] = shares[2 * way : 2 * way + 2].astype(BF16)


def order(count, falling):
    return range(count - 1, -1, -1) if falling else range(count)


def pass_by(state, block, rates):
    depth = block.shape[0] - 4
    total = block[depth : depth + 1] + block[depth + 1 : depth + 2]
    return jnp.exp2(rates * total) * state + block


def place_of(shards):
    place = lax.axis_index("seq")
    return place // shards, place % shards, place % 2


def row_kernel(parts, flat, copies):
    shards, _, slots, width = parts.shape
    depth = slots - 4
    here, _, way = place_of(shards)
    slot = lax.broadcasted_iota(jnp.int32, (slots, width), 0)
    packed = []
    for falling in (False, True):
        state = jnp.zeros((slots, width), F32)
        total = jnp.zeros((1, width), F32)
        for shard in order(shards, falling):
            block = parts[shard, 1 - way if falling else way].astype(F32)
            total = total + block[depth : depth + 1] + block[depth + 1 : depth + 2]
            state = pass_by(state, block, flat[way])
        coarse = total.astype(BF16).astype(F32)
        state = jnp.where(slot == depth, coarse, state)
        state = jnp.where(slot == depth + 1, total - coarse, state)
        packed.append(jnp.where(slot > depth + 1, 0.0, state).astype(BF16))
    for row in range(copies.shape[0]):

        @pl.when(row > here)
        def _():
            copies[row] = packed[0]

        @pl.when(row <= here)
        def _():
            copies[row] = packed[1]


def entry_kernel(rows, parts, flat, mine, other, every):
    count, slots, width = rows.shape
    shards = parts.shape[0]
    row_here, here, way = place_of(shards)
    rates = flat[way]
    for falling in (False, True):
        kind = 1 - way if falling else way
        state = jnp.zeros((slots, width), F32)
        for row in order(count, falling):
            passed = pass_by(state, rows[row].astype(F32), rates)
            state = jnp.where(row > row_here if falling else row < row_here, passed, state)
        for shard in order(shards, falling):
            every[shard] = state
            state = pass_by(state, parts[shard, kind].astype(F32), rates)
        mine[kind] = every[here]
        other[kind] = every[here + 1 - 2 * way]


def direction_gradient(
    way,
    projected,
    w_delta,
    rates,
    signal,
    cot,
    delta,
    slope,
    local,
    ahead,
    entries,
    core,
    direct,
    low,
    gate_grad,
    weight,
    grad_pre,
    fades,
    kept,
    products,
    spread,
):
    rows, width = signal.shape
    rank = w_delta.shape[1]
    depth = rates.shape[1]
    steps = rows // GROUPS
    blocks = width // LANES
    first = 2 * way * depth
    spread_gates(projected[:, 2 * rank :], spread, first)
    weight[...] = delta[way] * signal[...]

    def entering(kind):
        gap = [ahead[2 * way + kind, :, lane_block(block)] for block in range(blocks)]
        return tuple(
            local[2 * way + kind, n, :, lane_block(block)]
            + jnp.exp2(gap[block] * rates[way, n, :, lane_block(block)])
            * entries[kind, n : n + 1, lane_block(block)]
            for n in range(depth)
            for block in range(blocks)
        )

    def pieces(array, step):
        return [array[at(step), lane_block(block)] for block in range(blocks)]

    def put_products(which, step, rows_of):
        start = pl.multiple_of(step * depth * GROUPS, 2 * GROUPS)
        for block in range(blocks):
            stacked = jnp.concatenate(rows_of[block], 0).astype(BF16)
            products[which, pl.ds(start, depth * GROUPS), lane_block(block)] = stacked

    def walk_states(index, states):
        step = index + way * (steps - 1 - 2 * index)
        d, w, g = pieces(delta.at[way], step), pieces(weight, step), pieces(cot, step)
        total = pieces(core, step)
        rows_of = [[] for _ in range(blocks)]
        result = []
        for n in range(depth):
            gate_in = gate_at(spread, step, n)
            gate_out = gate_at(spread, step, depth + n)
            for block in range(blocks):
                lanes = lane_block(block)
                fade = jnp.exp2(d[block] * rates[way, n, :, lanes])
                fades[step, n, :, lanes] = fade
                faded = fade * states[n * blocks + block]
                kept[step, n, :, lanes] = faded
                state = faded + w[block] * gate_in
                total[block] = total[block] + gate_out * state
                rows_of[block].append(g[block] * state)
                result.append(state)
        for block in range(blocks):
            core[at(step), lane_block(block)] = total[block]
        put_products(1, step, rows_of)
        return tuple(result)

    lax.fori_loop(0, steps, walk_states, entering(0))

    def walk_adjoints(index, carried):
        step = steps - 1 - index + way * (2 * index - steps + 1)
        w, g = pieces(weight, step), pieces(cot, step)
        rows_of = [[] for _ in range(blocks)]
        through = [jnp.zeros((GROUPS, LANES), F32)] * blocks
        fading = [jnp.zeros((GROUPS, LANES), F32)] * blocks
        result = []
        for n in range(depth):
            gate_in = gate_at(spread, step, n)
            gate_out = gate_at(spread, step, depth + n)
            for block in range(blocks):
                lanes = lane_block(block)
                adjoint = g[block] * gate_out + carried[n * blocks + block]
                result.append(fades[step, n, :, lanes] * adjoint)
                through[block] = through[block] + adjoint * gate_in
                fading[block] = fading[block] + (
                    adjoint * kept[step, n, :, lanes] * rates[way, n, :, lanes]
                )
                rows_of[block].append(adjoint * w[block])
        put_products(0, step, rows_of)
        for block in range(blocks):
            lanes = lane_block(block)
            grad_delta = through[block] * signal[at(step), lanes] + fading[block] * LN2
            direct[at(step), lanes] = (
                direct[at(step), lanes] + through[block] * delta[way, at(step), lanes]
            )
            grad_pre[at(step), lanes] = grad_delta * slope[way, at(step), lanes]
        return tuple(result)

    lax.fori_loop(0, steps, walk_adjoints, entering(1))
    low[...] = dot(grad_pre[...].astype(BF16), w_delta[way], NT)
    ones = jnp.ones((width, LANES), BF16)
    lane = lax.broadcasted_iota(jnp.int32, (GROUPS, LANES), 1) - first
    height = depth * GROUPS
    for start in range(0, steps, 4):
        merged = [
            gate_grad[(start + step) * GROUPS : (start + step + 1) * GROUPS] for step in range(4)
        ]
        for which in range(2):
            sums = dot(products[which, start * height : (start + 4) * height], ones)
            for step in range(4):
                for n in range(depth):
                    row = step * height + n * GROUPS
                    merged[step] = jnp.where(
                        lane == which * depth + n, sums[row : row + GROUPS], merged[step]
                    )
        gate_grad[start * GROUPS : (start + 4) * GROUPS] = jnp.concatenate(merged, 0)


def own_gradient_kernel(skip_gain, *refs):
    signal, cot = refs[3:5]
    core, direct, _, gate_grad = refs[10:14]
    core[...] = skip_gain[...] * signal[...]
    direct[...] = skip_gain[...] * cot[...]
    gate_grad[...] = jnp.zeros_like(gate_grad)
    direction_gradient(lax.axis_index("seq") % 2, *refs)


def other_gradient_kernel(own_core, own_direct, own_low, own_gates, *refs):
    inputs = refs[:10]
    layer_out, parts_out, direct, core, low, gate_grad = refs[10:16]
    way = 1 - lax.axis_index("seq") % 2
    core[...] = own_core[...]
    direct[...] = own_direct[...]
    gate_grad[...] = own_gates[...]
    direction_gradient(way, *inputs, core, direct, low, gate_grad, *refs[16:])
    rows, rank = low.shape
    gates = parts_out.shape[1] - 2 * rank
    parts_out[:, pl.ds(pl.multiple_of(way * rank, LANES), rank)] = low[...]
    parts_out[:, pl.ds(pl.multiple_of((1 - way) * rank, LANES), rank)] = own_low[...]
    parts_out[:, 2 * rank :] = gate_grad[:, :gates]
    ungroup = grouping(rows, inverse=True)
    layer_out[...] = dot(ungroup, core[...].astype(BF16)).astype(BF16)


def finish_kernel(grad_proj, w_proj, direct, signal_grad):
    total = dot(grad_proj[...], w_proj[...]) + direct[...]
    ungroup = grouping(direct.shape[0], inverse=True)
    signal_grad[...] = dot(ungroup, total.astype(BF16)).astype(BF16)


def shape(*dims, dtype=F32):
    return jax.ShapeDtypeStruct(dims, dtype)


WHOLE = pl.BlockSpec(memory_space=pltpu.VMEM)


def kernel(body, out_shape, mebibytes, scratch=(), cost=0, **more):
    return pl.pallas_call(
        body,
        out_shape=out_shape,
        scratch_shapes=[
            pltpu.VMEM(*each) if isinstance(each, tuple) else each for each in scratch
        ],
        compiler_params=pltpu.CompilerParams(vmem_limit_bytes=mebibytes << 20),
        cost_estimate=pl.CostEstimate(flops=cost, bytes_accessed=cost, transcendentals=0),
        name=body.__name__,
        **more,
    )


def sum_over_chan(part):
    count = lax.axis_size("chan")
    rows, columns = part.shape
    pairs = [[2 * chip, 2 * chip + 1] for chip in range(count // 2)]
    across = [list(range(core, count, 2)) for core in range(2)]
    both = lax.all_gather(part, "chan", axis=0, tiled=True, axis_index_groups=pairs)
    copies = kernel(
        pair_kernel,
        shape(count // 2, rows // 2, columns, dtype=BF16),
        4,
    )(both)
    parts = lax.all_to_all(copies, "chan", 0, 0, tiled=True, axis_index_groups=across)
    half = kernel(chips_kernel, shape(rows // 2, columns, dtype=BF16), 4)(parts)
    return lax.all_gather(half, "chan", axis=0, tiled=True, axis_index_groups=pairs)


def local(signal, cotangent, w_proj, w_delta, delta_bias, decay_log, skip_gain):
    rows, width = signal.shape
    columns = w_proj.shape[1]
    depth = decay_log.shape[1]
    steps = rows // GROUPS
    shards = lax.axis_size("seq")
    if shards % 4:
        raise ValueError("shard count")
    w_turned = w_proj.T
    along_y = [[z * 4 + y for y in range(4)] for z in range(shards // 4)]
    along_z = [[z * 4 + y for z in range(shards // 4)] for y in range(4)]
    slots = depth + 4

    def exchange(array, groups):
        return lax.all_to_all(array, "seq", 0, 0, tiled=True, axis_index_groups=groups)

    signal_wide, part = kernel(
        project_kernel,
        (shape(rows, width), shape(rows, columns)),
        8,
        (((rows, width), BF16), ((columns, width), BF16), pltpu.SemaphoreType.DMA((2,))),
        in_specs=[pl.BlockSpec(memory_space=pltpu.HBM)] * 2,
        out_specs=(WHOLE, WHOLE),
    )(*(pltpu.with_memory_space_constraint(each, pltpu.HBM) for each in (signal, w_turned)))
    cot_wide, rates, flat, bias, gain = kernel(
        prepare_kernel,
        (
            shape(rows, width),
            shape(2, depth, GROUPS, width),
            shape(2, slots, width),
            shape(2, width),
            shape(1, width),
        ),
        8,
        cost=1 << 20,
    )(cotangent, decay_log.transpose(1, 0, 2), delta_bias, skip_gain.reshape(1, width))
    projected = sum_over_chan(part)
    wide = ((rows, 4 * depth * LANES), F32)
    stack = ((steps, depth, GROUPS, width), F32)
    delta, slope, local_states, ahead, payload = kernel(
        summary_kernel,
        (
            shape(2, rows, width),
            shape(2, rows, width),
            shape(4, depth, GROUPS, width),
            shape(4, GROUPS, width),
            shape(4, 2, slots, width, dtype=BF16),
        ),
        20,
        (((rows, width), F32), stack, wide, ((4, slots, width), F32)),
    )(projected, w_delta, bias, rates, signal_wide, cot_wide)
    parts = exchange(payload, along_y)
    copies = kernel(row_kernel, shape(shards // 4, slots, width, dtype=BF16), 4)(parts, flat)
    row_totals = exchange(copies, along_z)
    entries, others = kernel(
        entry_kernel,
        (shape(2, slots, width), shape(2, slots, width)),
        4,
        (((4, slots, width), F32),),
    )(row_totals, parts, flat)
    swapped = lax.ppermute(others, "seq", [(shard, shard ^ 1) for shard in range(shards)])
    rank = w_delta.shape[1]
    inputs = (
        projected,
        w_delta,
        rates,
        signal_wide,
        cot_wide,
        delta,
        slope,
        local_states,
        ahead,
    )
    scratch = (
        ((rows, width), F32),
        ((rows, width), F32),
        stack,
        stack,
        ((2, rows * depth, width), BF16),
        ((rows, 2 * depth * LANES), F32),
    )
    own = kernel(
        own_gradient_kernel,
        (
            shape(rows, width),
            shape(rows, width),
            shape(rows, rank),
            shape(rows, LANES),
        ),
        20,
        scratch,
        cost=1 << 22,
    )(gain, *inputs, entries)
    layer_out, grad_parts, direct = kernel(
        other_gradient_kernel,
        (
            shape(rows, width, dtype=BF16),
            shape(rows, columns),
            shape(rows, width),
        ),
        20,
        (((rows, width), F32), ((rows, rank), F32), ((rows, LANES), F32)) + scratch,
    )(*own, *inputs, swapped)
    grad_proj = sum_over_chan(grad_parts)
    signal_grad = kernel(finish_kernel, shape(rows, width, dtype=BF16), 8)(
        grad_proj, w_turned, direct
    )
    return (layer_out, signal_grad)


def solution(mesh):
    in_specs = (
        P("seq", "chan"),
        P("seq", "chan"),
        P("chan", None),
        P(None, None, "chan"),
        P(None, "chan"),
        P(None, None, "chan"),
        P("chan"),
    )
    out_specs = (P("seq", "chan"), P("seq", "chan"))
    return jax.shard_map(local, mesh=mesh, in_specs=in_specs, out_specs=out_specs, check_vma=False)
```

```python
import math

import jax
import jax.numpy as jnp
from jax import lax
from jax.experimental import pallas as pl
from jax.experimental.pallas import tpu as pltpu
from jax.sharding import PartitionSpec as P

GROUPS = 8
LANES = 128
LOG2E = math.log2(math.e)
LN2 = math.log(2.0)
FAR = 1e30
NT = (((1,), (1,)), ((), ()))
F32 = jnp.float32
BF16 = jnp.bfloat16


def dot(a, b, dims=(((1,), (0,)), ((), ()))):
    return lax.dot_general(a, b, dims, preferred_element_type=F32)


def grouping(rows, inverse=False):
    steps = rows // GROUPS
    row = lax.broadcasted_iota(jnp.int32, (rows, rows), 1 if inverse else 0)
    token = lax.broadcasted_iota(jnp.int32, (rows, rows), 0 if inverse else 1)
    return jnp.where(token == (row % GROUPS) * steps + row // GROUPS, 1.0, 0.0).astype(BF16)


def project_kernel(signal, w_proj, signal_out, part_out, signal_here, w_here, done):
    fetches = [
        pltpu.make_async_copy(signal, signal_here, done.at[0]),
        pltpu.make_async_copy(w_proj, w_here, done.at[1]),
    ]
    for fetch in fetches:
        fetch.start()
    order = grouping(signal_here.shape[0])
    fetches[0].wait()
    grouped = dot(order, signal_here[...])
    signal_out[...] = grouped
    fetches[1].wait()
    part_out[...] = dot(grouped.astype(BF16), w_here[...], NT)


def pair_kernel(both, copies):
    half = both.shape[0] // 4
    start = pl.multiple_of(lax.axis_index("chan") % 2 * half, half)
    total = both[pl.ds(start, half), :] + both[pl.ds(2 * half + start, half), :]
    for copy in range(copies.shape[0]):
        copies[copy] = total.astype(BF16)


def chips_kernel(parts, total):
    result = parts[0].astype(F32)
    for chip in range(1, parts.shape[0]):
        result = result + parts[chip].astype(F32)
    total[...] = result.astype(BF16)


def prepare_kernel(cotangent, decay_log, bias, skip_gain, cot_out, rates, flat, bias_out, gain_out):
    cot_out[...] = dot(grouping(cotangent.shape[0]), cotangent[...])
    bias_out[...] = bias[...]
    gain_out[...] = skip_gain[...]
    depth, _, width = decay_log.shape
    flat[...] = jnp.zeros_like(flat)
    for n in range(depth):
        scaled = -jnp.exp(decay_log[n]) * LOG2E
        for way in range(2):
            rates[way, n] = jnp.broadcast_to(scaled[way : way + 1], (GROUPS, width))
            flat[way, n : n + 1] = scaled[way : way + 1]


def at(step):
    return pl.ds(pl.multiple_of(step * GROUPS, GROUPS), GROUPS)


def lane_block(block):
    return slice(block * LANES, (block + 1) * LANES)


def spread_gates(gates, spread, first=0):
    count = gates.shape[1]
    for pair in range(spread.shape[1] // (2 * LANES)):
        source = lax.broadcasted_iota(jnp.int32, (count, 2 * LANES), 0)
        lane = lax.broadcasted_iota(jnp.int32, (count, 2 * LANES), 1)
        pick = jnp.where(source == first + 2 * pair + lane // LANES, 1.0, 0.0).astype(BF16)
        spread[:, pair * 2 * LANES : (pair + 1) * 2 * LANES] = dot(gates, pick)


def gate_at(spread, step, column):
    return spread[at(step), column * LANES : (column + 1) * LANES]


def put_total(shares, kind, lanes, total):
    depth = shares.shape[1] - 4
    coarse = total.astype(BF16).astype(F32)
    shares[kind, depth : depth + 1, lanes] = coarse
    shares[kind, depth + 1 : depth + 2, lanes] = total - coarse


def summary_kernel(
    projected,
    w_delta,
    bias,
    rates,
    signal,
    cot,
    delta_out,
    slope_out,
    local_out,
    ahead_out,
    payload,
    weight,
    fades,
    spread,
    shares,
):
    rows, width = signal.shape
    rank = w_delta.shape[1]
    depth = rates.shape[1]
    steps = rows // GROUPS
    blocks = width // LANES
    spread_gates(projected[:, 2 * rank :], spread)
    shares[...] = jnp.zeros_like(shares)
    group = lax.broadcasted_iota(jnp.int32, (GROUPS, LANES), 0)
    for way in range(2):
        pre = dot(projected[:, way * rank : (way + 1) * rank], w_delta[way]) + bias[way : way + 1]
        delta = jnp.maximum(pre, 0.0) + jnp.log1p(jnp.exp(-jnp.abs(pre)))
        delta_out[way] = delta
        slope_out[way] = 1.0 / (1.0 + jnp.exp(-pre))
        weight[...] = delta * signal[...]
        falling = way == 1
        zero = jnp.zeros((GROUPS, LANES), F32)
        many = (zero,) * (blocks * depth)

        def walk_states(index, carry):
            states, total = carry
            step = steps - 1 - index if falling else index
            d = [delta_out[way, at(step), lane_block(block)] for block in range(blocks)]
            w = [weight[at(step), lane_block(block)] for block in range(blocks)]
            result = []
            for n in range(depth):
                gate = gate_at(spread, step, 2 * way * depth + n)
                for block in range(blocks):
                    fade = jnp.exp2(d[block] * rates[way, n, :, lane_block(block)])
                    fades[step, n, :, lane_block(block)] = fade
                    result.append(fade * states[n * blocks + block] + w[block] * gate)
            return (tuple(result), tuple(t + x for t, x in zip(total, d)))

        states, total = lax.fori_loop(0, steps, walk_states, (many, (zero,) * blocks))

        def walk_adjoints(index, carried):
            step = index if falling else steps - 1 - index
            g = [cot[at(step), lane_block(block)] for block in range(blocks)]
            result = []
            for n in range(depth):
                gate = gate_at(spread, step, (2 * way + 1) * depth + n)
                for block in range(blocks):
                    fade = fades[step, n, :, lane_block(block)]
                    result.append(fade * (g[block] * gate + carried[n * blocks + block]))
            return tuple(result)

        carried = lax.fori_loop(0, steps, walk_adjoints, many)
        for block in range(blocks):
            lanes = lane_block(block)

            def shift(array, by, down):
                return pltpu.roll(array, GROUPS - by if down else by, 0)

            def beyond(by, down):
                return group >= GROUPS - by if down else group < by

            whole = jnp.sum(total[block], 0, keepdims=True)
            for kind, down, finals in ((0, falling, states), (1, not falling, carried)):
                windows = []
                window = total[block]
                ahead = jnp.where(beyond(1, down), 0.0, shift(window, 1, down))
                for by in (1, 2, 4):
                    windows.append(jnp.where(beyond(by, down), FAR, window))
                    outside = beyond(by, down)
                    window = window + jnp.where(outside, 0.0, shift(window, by, down))
                    ahead = ahead + jnp.where(outside, 0.0, shift(ahead, by, down))
                ahead_out[2 * way + kind, :, lanes] = ahead
                edge = 0 if down else GROUPS - 1
                for n in range(depth):
                    rate = rates[way, n, :, lanes]
                    scanned = finals[n * blocks + block]
                    for by, span in zip((1, 2, 4), windows):
                        scanned = scanned + jnp.exp2(rate * span) * shift(scanned, by, down)
                    local_out[2 * way + kind, n, :, lanes] = jnp.where(
                        beyond(1, down), 0.0, shift(scanned, 1, down)
                    )
                    shares[2 * way + kind, n : n + 1, lanes] = scanned[edge : edge + 1]
                put_total(shares, 2 * way + kind, lanes, whole)
    for shard in range(payload.shape[0]):
        way = shard % 2
        payload[shard] = shares[2 * way : 2 * way + 2].astype(BF16)


def order(count, falling):
    return range(count - 1, -1, -1) if falling else range(count)


def pass_by(state, block, rates):
    depth = block.shape[0] - 4
    total = block[depth : depth + 1] + block[depth + 1 : depth + 2]
    return jnp.exp2(rates * total) * state + block


def place_of(shards):
    place = lax.axis_index("seq")
    return place // shards, place % shards, place % 2


def row_kernel(parts, flat, copies):
    shards, _, slots, width = parts.shape
    depth = slots - 4
    here, _, way = place_of(shards)
    slot = lax.broadcasted_iota(jnp.int32, (slots, width), 0)
    packed = []
    for falling in (False, True):
        state = jnp.zeros((slots, width), F32)
        total = jnp.zeros((1, width), F32)
        for shard in order(shards, falling):
            block = parts[shard, 1 - way if falling else way].astype(F32)
            total = total + block[depth : depth + 1] + block[depth + 1 : depth + 2]
            state = pass_by(state, block, flat[way])
        coarse = total.astype(BF16).astype(F32)
        state = jnp.where(slot == depth, coarse, state)
        state = jnp.where(slot == depth + 1, total - coarse, state)
        packed.append(jnp.where(slot > depth + 1, 0.0, state).astype(BF16))
    for row in range(copies.shape[0]):

        @pl.when(row > here)
        def _():
            copies[row] = packed[0]

        @pl.when(row <= here)
        def _():
            copies[row] = packed[1]


def entry_kernel(rows, parts, flat, mine, other, every):
    count, slots, width = rows.shape
    shards = parts.shape[0]
    row_here, here, way = place_of(shards)
    rates = flat[way]
    for falling in (False, True):
        kind = 1 - way if falling else way
        state = jnp.zeros((slots, width), F32)
        for row in order(count, falling):
            passed = pass_by(state, rows[row].astype(F32), rates)
            state = jnp.where(row > row_here if falling else row < row_here, passed, state)
        for shard in order(shards, falling):
            every[shard] = state
            state = pass_by(state, parts[shard, kind].astype(F32), rates)
        mine[kind] = every[here]
        other[kind] = every[here + 1 - 2 * way]


def early_kernel(projected, rates, delta, spread, fades):
    _, steps, depth, _, _ = fades.shape
    rank = (projected.shape[1] - 4 * depth) // 2
    for way in range(2):
        spread_gates(projected[:, 2 * rank :], spread.at[way], 2 * way * depth)

    def walk(step, _):
        for way in range(2):
            d = delta[way, at(step), :]
            for n in range(depth):
                fades[way, step, n] = jnp.exp2(d * rates[way, n])
        return _

    lax.fori_loop(0, steps, walk, 0)


def direction_gradient(
    way,
    spread,
    fades,
    w_delta,
    rates,
    signal,
    cot,
    delta,
    slope,
    local,
    ahead,
    entries,
    core,
    direct,
    low,
    gate_grad,
    weight,
    grad_pre,
    kept,
    products,
):
    rows, width = signal.shape
    depth = rates.shape[1]
    steps = rows // GROUPS
    blocks = width // LANES
    first = 2 * way * depth
    weight[...] = delta[way] * signal[...]

    def entering(kind):
        gap = [ahead[2 * way + kind, :, lane_block(block)] for block in range(blocks)]
        return tuple(
            local[2 * way + kind, n, :, lane_block(block)]
            + jnp.exp2(gap[block] * rates[way, n, :, lane_block(block)])
            * entries[kind, n : n + 1, lane_block(block)]
            for n in range(depth)
            for block in range(blocks)
        )

    def pieces(array, step):
        return [array[at(step), lane_block(block)] for block in range(blocks)]

    def put_products(which, step, rows_of):
        start = pl.multiple_of(step * depth * GROUPS, 2 * GROUPS)
        for block in range(blocks):
            stacked = jnp.concatenate(rows_of[block], 0).astype(BF16)
            products[which, pl.ds(start, depth * GROUPS), lane_block(block)] = stacked

    def walk_states(index, states):
        step = index + way * (steps - 1 - 2 * index)
        w, g = pieces(weight, step), pieces(cot, step)
        total = pieces(core, step)
        rows_of = [[] for _ in range(blocks)]
        result = []
        for n in range(depth):
            gate_in = gate_at(spread.at[way], step, n)
            gate_out = gate_at(spread.at[way], step, depth + n)
            for block in range(blocks):
                lanes = lane_block(block)
                faded = fades[way, step, n, :, lanes] * states[n * blocks + block]
                kept[step, n, :, lanes] = faded
                state = faded + w[block] * gate_in
                total[block] = total[block] + gate_out * state
                rows_of[block].append(g[block] * state)
                result.append(state)
        for block in range(blocks):
            core[at(step), lane_block(block)] = total[block]
        put_products(1, step, rows_of)
        return tuple(result)

    lax.fori_loop(0, steps, walk_states, entering(0))

    def walk_adjoints(index, carried):
        step = steps - 1 - index + way * (2 * index - steps + 1)
        w, g = pieces(weight, step), pieces(cot, step)
        rows_of = [[] for _ in range(blocks)]
        through = [jnp.zeros((GROUPS, LANES), F32)] * blocks
        fading = [jnp.zeros((GROUPS, LANES), F32)] * blocks
        result = []
        for n in range(depth):
            gate_in = gate_at(spread.at[way], step, n)
            gate_out = gate_at(spread.at[way], step, depth + n)
            for block in range(blocks):
                lanes = lane_block(block)
                adjoint = g[block] * gate_out + carried[n * blocks + block]
                result.append(fades[way, step, n, :, lanes] * adjoint)
                through[block] = through[block] + adjoint * gate_in
                fading[block] = fading[block] + (
                    adjoint * kept[step, n, :, lanes] * rates[way, n, :, lanes]
                )
                rows_of[block].append(adjoint * w[block])
        put_products(0, step, rows_of)
        for block in range(blocks):
            lanes = lane_block(block)
            grad_delta = through[block] * signal[at(step), lanes] + fading[block] * LN2
            direct[at(step), lanes] = (
                direct[at(step), lanes] + through[block] * delta[way, at(step), lanes]
            )
            grad_pre[at(step), lanes] = grad_delta * slope[way, at(step), lanes]
        return tuple(result)

    lax.fori_loop(0, steps, walk_adjoints, entering(1))
    low[...] = dot(grad_pre[...].astype(BF16), w_delta[way], NT)
    ones = jnp.ones((width, LANES), BF16)
    lane = lax.broadcasted_iota(jnp.int32, (GROUPS, LANES), 1) - first
    height = depth * GROUPS
    for start in range(0, steps, 4):
        merged = [
            gate_grad[(start + step) * GROUPS : (start + step + 1) * GROUPS] for step in range(4)
        ]
        for which in range(2):
            sums = dot(products[which, start * height : (start + 4) * height], ones)
            for step in range(4):
                for n in range(depth):
                    row = step * height + n * GROUPS
                    merged[step] = jnp.where(
                        lane == which * depth + n, sums[row : row + GROUPS], merged[step]
                    )
        gate_grad[start * GROUPS : (start + 4) * GROUPS] = jnp.concatenate(merged, 0)


def own_gradient_kernel(skip_gain, *refs):
    signal, cot = refs[4:6]
    core, direct, _, gate_grad = refs[11:15]
    core[...] = skip_gain[...] * signal[...]
    direct[...] = skip_gain[...] * cot[...]
    gate_grad[...] = jnp.zeros_like(gate_grad)
    direction_gradient(lax.axis_index("seq") % 2, *refs)


def other_gradient_kernel(own_core, own_direct, own_low, own_gates, *refs):
    inputs = refs[:11]
    core, parts_out, direct, low, gate_grad = refs[11:16]
    way = 1 - lax.axis_index("seq") % 2
    core[...] = own_core[...]
    direct[...] = own_direct[...]
    gate_grad[...] = own_gates[...]
    direction_gradient(way, *inputs, core, direct, low, gate_grad, *refs[16:])
    rank = low.shape[1]
    gates = parts_out.shape[1] - 2 * rank
    parts_out[:, pl.ds(pl.multiple_of(way * rank, LANES), rank)] = low[...]
    parts_out[:, pl.ds(pl.multiple_of((1 - way) * rank, LANES), rank)] = own_low[...]
    parts_out[:, 2 * rank :] = gate_grad[:, :gates]


def layer_kernel(core, layer_out):
    ungroup = grouping(core.shape[0], inverse=True)
    layer_out[...] = dot(ungroup, core[...].astype(BF16)).astype(BF16)


def finish_kernel(grad_proj, w_proj, direct, signal_grad):
    total = dot(grad_proj[...], w_proj[...]) + direct[...]
    ungroup = grouping(direct.shape[0], inverse=True)
    signal_grad[...] = dot(ungroup, total.astype(BF16)).astype(BF16)


def shape(*dims, dtype=F32):
    return jax.ShapeDtypeStruct(dims, dtype)


WHOLE = pl.BlockSpec(memory_space=pltpu.VMEM)


def kernel(body, out_shape, mebibytes, scratch=(), cost=0, **more):
    return pl.pallas_call(
        body,
        out_shape=out_shape,
        scratch_shapes=[
            pltpu.VMEM(*each) if isinstance(each, tuple) else each for each in scratch
        ],
        compiler_params=pltpu.CompilerParams(vmem_limit_bytes=mebibytes << 20),
        cost_estimate=pl.CostEstimate(flops=cost, bytes_accessed=cost, transcendentals=0),
        name=body.__name__,
        **more,
    )


def sum_over_chan(part):
    count = lax.axis_size("chan")
    rows, columns = part.shape
    pairs = [[2 * chip, 2 * chip + 1] for chip in range(count // 2)]
    across = [list(range(core, count, 2)) for core in range(2)]
    both = lax.all_gather(part, "chan", axis=0, tiled=True, axis_index_groups=pairs)
    copies = kernel(
        pair_kernel,
        shape(count // 2, rows // 2, columns, dtype=BF16),
        4,
    )(both)
    parts = lax.all_to_all(copies, "chan", 0, 0, tiled=True, axis_index_groups=across)
    half = kernel(chips_kernel, shape(rows // 2, columns, dtype=BF16), 4)(parts)
    return lax.all_gather(half, "chan", axis=0, tiled=True, axis_index_groups=pairs)


def local(signal, cotangent, w_proj, w_delta, delta_bias, decay_log, skip_gain):
    rows, width = signal.shape
    columns = w_proj.shape[1]
    depth = decay_log.shape[1]
    steps = rows // GROUPS
    shards = lax.axis_size("seq")
    if shards % 4:
        raise ValueError("shard count")
    w_turned = w_proj.T
    along_y = [[z * 4 + y for y in range(4)] for z in range(shards // 4)]
    along_z = [[z * 4 + y for z in range(shards // 4)] for y in range(4)]
    slots = depth + 4

    def exchange(array, groups):
        return lax.all_to_all(array, "seq", 0, 0, tiled=True, axis_index_groups=groups)

    signal_wide, part = kernel(
        project_kernel,
        (shape(rows, width), shape(rows, columns)),
        8,
        (((rows, width), BF16), ((columns, width), BF16), pltpu.SemaphoreType.DMA((2,))),
        in_specs=[pl.BlockSpec(memory_space=pltpu.HBM)] * 2,
        out_specs=(WHOLE, WHOLE),
    )(*(pltpu.with_memory_space_constraint(each, pltpu.HBM) for each in (signal, w_turned)))
    cot_wide, rates, flat, bias, gain = kernel(
        prepare_kernel,
        (
            shape(rows, width),
            shape(2, depth, GROUPS, width),
            shape(2, slots, width),
            shape(2, width),
            shape(1, width),
        ),
        8,
        cost=1 << 20,
    )(cotangent, decay_log.transpose(1, 0, 2), delta_bias, skip_gain.reshape(1, width))
    projected = sum_over_chan(part)
    wide = ((rows, 4 * depth * LANES), F32)
    stack = ((steps, depth, GROUPS, width), F32)
    delta, slope, local_states, ahead, payload = kernel(
        summary_kernel,
        (
            shape(2, rows, width),
            shape(2, rows, width),
            shape(4, depth, GROUPS, width),
            shape(4, GROUPS, width),
            shape(4, 2, slots, width, dtype=BF16),
        ),
        20,
        (((rows, width), F32), stack, wide, ((4, slots, width), F32)),
    )(projected, w_delta, bias, rates, signal_wide, cot_wide)
    parts = exchange(payload, along_y)
    copies = kernel(row_kernel, shape(shards // 4, slots, width, dtype=BF16), 4)(parts, flat)
    spread, fades = kernel(
        early_kernel,
        (
            shape(2, rows, 2 * depth * LANES),
            shape(2, steps, depth, GROUPS, width),
        ),
        8,
        cost=1 << 22,
    )(projected, rates, delta)
    row_totals = exchange(copies, along_z)
    entries, others = kernel(
        entry_kernel,
        (shape(2, slots, width), shape(2, slots, width)),
        4,
        (((4, slots, width), F32),),
    )(row_totals, parts, flat)
    swapped = lax.ppermute(others, "seq", [(shard, shard ^ 1) for shard in range(shards)])
    rank = w_delta.shape[1]
    inputs = (
        spread,
        fades,
        w_delta,
        rates,
        signal_wide,
        cot_wide,
        delta,
        slope,
        local_states,
        ahead,
    )
    scratch = (
        ((rows, width), F32),
        ((rows, width), F32),
        stack,
        ((2, rows * depth, width), BF16),
    )
    own = kernel(
        own_gradient_kernel,
        (
            shape(rows, width),
            shape(rows, width),
            shape(rows, rank),
            shape(rows, LANES),
        ),
        10,
        scratch,
        cost=1 << 22,
    )(gain, *inputs, entries)
    core, grad_parts, direct = kernel(
        other_gradient_kernel,
        (shape(rows, width), shape(rows, columns), shape(rows, width)),
        10,
        (((rows, rank), F32), ((rows, LANES), F32)) + scratch,
    )(*own, *inputs, swapped)
    layer_out = kernel(layer_kernel, shape(rows, width, dtype=BF16), 4, cost=1 << 20)(core)
    grad_proj = sum_over_chan(grad_parts)
    signal_grad = kernel(finish_kernel, shape(rows, width, dtype=BF16), 8)(
        grad_proj, w_turned, direct
    )
    return (layer_out, signal_grad)


def solution(mesh):
    in_specs = (
        P("seq", "chan"),
        P("seq", "chan"),
        P("chan", None),
        P(None, None, "chan"),
        P(None, "chan"),
        P(None, None, "chan"),
        P("chan"),
    )
    out_specs = (P("seq", "chan"), P("seq", "chan"))
    return jax.shard_map(local, mesh=mesh, in_specs=in_specs, out_specs=out_specs, check_vma=False)
```

```python
import math

import jax
import jax.numpy as jnp
from jax import lax
from jax.experimental import pallas as pl
from jax.experimental.pallas import tpu as pltpu
from jax.sharding import PartitionSpec as P

GROUPS = 8
LANES = 128
LOG2E = math.log2(math.e)
LN2 = math.log(2.0)
FAR = 1e30
NT = (((1,), (1,)), ((), ()))
F32 = jnp.float32
BF16 = jnp.bfloat16


def dot(a, b, dims=(((1,), (0,)), ((), ()))):
    return lax.dot_general(a, b, dims, preferred_element_type=F32)


def grouping(rows, inverse=False):
    steps = rows // GROUPS
    row = lax.broadcasted_iota(jnp.int32, (rows, rows), 1 if inverse else 0)
    token = lax.broadcasted_iota(jnp.int32, (rows, rows), 0 if inverse else 1)
    return jnp.where(token == (row % GROUPS) * steps + row // GROUPS, 1.0, 0.0).astype(BF16)


def project_kernel(signal, w_proj, signal_out, part_out, signal_here, w_here, done):
    fetches = [
        pltpu.make_async_copy(signal, signal_here, done.at[0]),
        pltpu.make_async_copy(w_proj, w_here, done.at[1]),
    ]
    for fetch in fetches:
        fetch.start()
    order = grouping(signal_here.shape[0])
    fetches[0].wait()
    grouped = dot(order, signal_here[...])
    signal_out[...] = grouped
    fetches[1].wait()
    part_out[...] = dot(grouped.astype(BF16), w_here[...], NT)


def pair_kernel(both, copies):
    half = both.shape[0] // 4
    start = pl.multiple_of(lax.axis_index("chan") % 2 * half, half)
    total = both[pl.ds(start, half), :] + both[pl.ds(2 * half + start, half), :]
    for copy in range(copies.shape[0]):
        copies[copy] = total.astype(BF16)


def chips_kernel(parts, total):
    result = parts[0].astype(F32)
    for chip in range(1, parts.shape[0]):
        result = result + parts[chip].astype(F32)
    total[...] = result.astype(BF16)


def prepare_kernel(cotangent, decay_log, bias, skip_gain, cot_out, rates, flat, bias_out, gain_out):
    cot_out[...] = dot(grouping(cotangent.shape[0]), cotangent[...])
    bias_out[...] = bias[...]
    gain_out[...] = skip_gain[...]
    depth, _, width = decay_log.shape
    flat[...] = jnp.zeros_like(flat)
    for n in range(depth):
        scaled = -jnp.exp(decay_log[n]) * LOG2E
        for way in range(2):
            rates[way, n] = jnp.broadcast_to(scaled[way : way + 1], (GROUPS, width))
            flat[way, n : n + 1] = scaled[way : way + 1]


def at(step):
    return pl.ds(pl.multiple_of(step * GROUPS, GROUPS), GROUPS)


def lane_block(block):
    return slice(block * LANES, (block + 1) * LANES)


def spread_gates(gates, spread, first=0):
    count = gates.shape[1]
    for pair in range(spread.shape[1] // (2 * LANES)):
        source = lax.broadcasted_iota(jnp.int32, (count, 2 * LANES), 0)
        lane = lax.broadcasted_iota(jnp.int32, (count, 2 * LANES), 1)
        pick = jnp.where(source == first + 2 * pair + lane // LANES, 1.0, 0.0).astype(BF16)
        spread[:, pair * 2 * LANES : (pair + 1) * 2 * LANES] = dot(gates, pick)


def gate_at(spread, step, column):
    return spread[at(step), column * LANES : (column + 1) * LANES]


def put_total(shares, kind, lanes, total):
    depth = shares.shape[1] - 4
    coarse = total.astype(BF16).astype(F32)
    shares[kind, depth : depth + 1, lanes] = coarse
    shares[kind, depth + 1 : depth + 2, lanes] = total - coarse


def summary_kernel(
    projected,
    w_delta,
    bias,
    rates,
    signal,
    cot,
    delta_out,
    slope_out,
    local_out,
    ahead_out,
    payload,
    weight,
    fades,
    spread,
    shares,
):
    rows, width = signal.shape
    rank = w_delta.shape[1]
    depth = rates.shape[1]
    steps = rows // GROUPS
    blocks = width // LANES
    spread_gates(projected[:, 2 * rank :], spread)
    shares[...] = jnp.zeros_like(shares)
    group = lax.broadcasted_iota(jnp.int32, (GROUPS, LANES), 0)
    for way in range(2):
        pre = dot(projected[:, way * rank : (way + 1) * rank], w_delta[way]) + bias[way : way + 1]
        delta = jnp.maximum(pre, 0.0) + jnp.log1p(jnp.exp(-jnp.abs(pre)))
        delta_out[way] = delta
        slope_out[way] = 1.0 / (1.0 + jnp.exp(-pre))
        weight[...] = delta * signal[...]
        falling = way == 1
        zero = jnp.zeros((GROUPS, LANES), F32)
        many = (zero,) * (blocks * depth)

        def walk_states(index, carry):
            states, total = carry
            step = steps - 1 - index if falling else index
            d = [delta_out[way, at(step), lane_block(block)] for block in range(blocks)]
            w = [weight[at(step), lane_block(block)] for block in range(blocks)]
            result = []
            for n in range(depth):
                gate = gate_at(spread, step, 2 * way * depth + n)
                for block in range(blocks):
                    fade = jnp.exp2(d[block] * rates[way, n, :, lane_block(block)])
                    fades[step, n, :, lane_block(block)] = fade
                    result.append(fade * states[n * blocks + block] + w[block] * gate)
            return (tuple(result), tuple(t + x for t, x in zip(total, d)))

        states, total = lax.fori_loop(0, steps, walk_states, (many, (zero,) * blocks), unroll=4)

        def walk_adjoints(index, carried):
            step = index if falling else steps - 1 - index
            g = [cot[at(step), lane_block(block)] for block in range(blocks)]
            result = []
            for n in range(depth):
                gate = gate_at(spread, step, (2 * way + 1) * depth + n)
                for block in range(blocks):
                    fade = fades[step, n, :, lane_block(block)]
                    result.append(fade * (g[block] * gate + carried[n * blocks + block]))
            return tuple(result)

        carried = lax.fori_loop(0, steps, walk_adjoints, many, unroll=4)
        for block in range(blocks):
            lanes = lane_block(block)

            def shift(array, by, down):
                return pltpu.roll(array, GROUPS - by if down else by, 0)

            def beyond(by, down):
                return group >= GROUPS - by if down else group < by

            whole = jnp.sum(total[block], 0, keepdims=True)
            for kind, down, finals in ((0, falling, states), (1, not falling, carried)):
                windows = []
                window = total[block]
                ahead = jnp.where(beyond(1, down), 0.0, shift(window, 1, down))
                for by in (1, 2, 4):
                    windows.append(jnp.where(beyond(by, down), FAR, window))
                    outside = beyond(by, down)
                    window = window + jnp.where(outside, 0.0, shift(window, by, down))
                    ahead = ahead + jnp.where(outside, 0.0, shift(ahead, by, down))
                ahead_out[2 * way + kind, :, lanes] = ahead
                edge = 0 if down else GROUPS - 1
                for n in range(depth):
                    rate = rates[way, n, :, lanes]
                    scanned = finals[n * blocks + block]
                    for by, span in zip((1, 2, 4), windows):
                        scanned = scanned + jnp.exp2(rate * span) * shift(scanned, by, down)
                    local_out[2 * way + kind, n, :, lanes] = jnp.where(
                        beyond(1, down), 0.0, shift(scanned, 1, down)
                    )
                    shares[2 * way + kind, n : n + 1, lanes] = scanned[edge : edge + 1]
                put_total(shares, 2 * way + kind, lanes, whole)
    for shard in range(payload.shape[0]):
        way = shard % 2
        payload[shard] = shares[2 * way : 2 * way + 2].astype(BF16)


def order(count, falling):
    return range(count - 1, -1, -1) if falling else range(count)


def pass_by(state, block, rates):
    depth = block.shape[0] - 4
    total = block[depth : depth + 1] + block[depth + 1 : depth + 2]
    return jnp.exp2(rates * total) * state + block


def place_of(shards):
    place = lax.axis_index("seq")
    return place // shards, place % shards, place % 2


def row_kernel(parts, flat, copies):
    shards, _, slots, width = parts.shape
    depth = slots - 4
    here, _, way = place_of(shards)
    slot = lax.broadcasted_iota(jnp.int32, (slots, width), 0)
    packed = []
    for falling in (False, True):
        state = jnp.zeros((slots, width), F32)
        total = jnp.zeros((1, width), F32)
        for shard in order(shards, falling):
            block = parts[shard, 1 - way if falling else way].astype(F32)
            total = total + block[depth : depth + 1] + block[depth + 1 : depth + 2]
            state = pass_by(state, block, flat[way])
        coarse = total.astype(BF16).astype(F32)
        state = jnp.where(slot == depth, coarse, state)
        state = jnp.where(slot == depth + 1, total - coarse, state)
        packed.append(jnp.where(slot > depth + 1, 0.0, state).astype(BF16))
    for row in range(copies.shape[0]):

        @pl.when(row > here)
        def _():
            copies[row] = packed[0]

        @pl.when(row <= here)
        def _():
            copies[row] = packed[1]


def entry_kernel(rows, parts, flat, mine, other, every):
    count, slots, width = rows.shape
    shards = parts.shape[0]
    row_here, here, way = place_of(shards)
    rates = flat[way]
    for falling in (False, True):
        kind = 1 - way if falling else way
        state = jnp.zeros((slots, width), F32)
        for row in order(count, falling):
            passed = pass_by(state, rows[row].astype(F32), rates)
            state = jnp.where(row > row_here if falling else row < row_here, passed, state)
        for shard in order(shards, falling):
            every[shard] = state
            state = pass_by(state, parts[shard, kind].astype(F32), rates)
        mine[kind] = every[here]
        other[kind] = every[here + 1 - 2 * way]


def early_kernel(projected, rates, delta, spread, fades):
    _, steps, depth, _, _ = fades.shape
    rank = (projected.shape[1] - 4 * depth) // 2
    for way in range(2):
        spread_gates(projected[:, 2 * rank :], spread.at[way], 2 * way * depth)

    def walk(step, _):
        for way in range(2):
            d = delta[way, at(step), :]
            for n in range(depth):
                fades[way, step, n] = jnp.exp2(d * rates[way, n])
        return _

    lax.fori_loop(0, steps, walk, 0)


def direction_gradient(
    way,
    spread,
    fades,
    w_delta,
    rates,
    signal,
    cot,
    delta,
    slope,
    local,
    ahead,
    entries,
    core,
    direct,
    low,
    gate_grad,
    weight,
    grad_pre,
    kept,
    products,
):
    rows, width = signal.shape
    depth = rates.shape[1]
    steps = rows // GROUPS
    blocks = width // LANES
    first = 2 * way * depth
    weight[...] = delta[way] * signal[...]

    def entering(kind):
        gap = [ahead[2 * way + kind, :, lane_block(block)] for block in range(blocks)]
        return tuple(
            local[2 * way + kind, n, :, lane_block(block)]
            + jnp.exp2(gap[block] * rates[way, n, :, lane_block(block)])
            * entries[kind, n : n + 1, lane_block(block)]
            for n in range(depth)
            for block in range(blocks)
        )

    def pieces(array, step):
        return [array[at(step), lane_block(block)] for block in range(blocks)]

    def put_products(which, step, rows_of):
        start = pl.multiple_of(step * depth * GROUPS, 2 * GROUPS)
        stacked = jnp.concatenate(rows_of, 0).astype(BF16)
        products[pl.ds(start, depth * GROUPS), lane_block(which)] = stacked

    def walk_states(index, states):
        step = index + way * (steps - 1 - 2 * index)
        w, g = pieces(weight, step), pieces(cot, step)
        total = pieces(core, step)
        rows_of = []
        result = []
        for n in range(depth):
            gate_in = gate_at(spread.at[way], step, n)
            gate_out = gate_at(spread.at[way], step, depth + n)
            for block in range(blocks):
                lanes = lane_block(block)
                faded = fades[way, step, n, :, lanes] * states[n * blocks + block]
                kept[step, n, :, lanes] = faded
                state = faded + w[block] * gate_in
                total[block] = total[block] + gate_out * state
                product = g[block] * state if block == 0 else product + g[block] * state
                result.append(state)
            rows_of.append(product)
        for block in range(blocks):
            core[at(step), lane_block(block)] = total[block]
        put_products(1, step, rows_of)
        return tuple(result)

    lax.fori_loop(0, steps, walk_states, entering(0), unroll=4)

    def walk_adjoints(index, carried):
        step = steps - 1 - index + way * (2 * index - steps + 1)
        w, g = pieces(weight, step), pieces(cot, step)
        rows_of = []
        through = [jnp.zeros((GROUPS, LANES), F32)] * blocks
        fading = [jnp.zeros((GROUPS, LANES), F32)] * blocks
        result = []
        for n in range(depth):
            gate_in = gate_at(spread.at[way], step, n)
            gate_out = gate_at(spread.at[way], step, depth + n)
            for block in range(blocks):
                lanes = lane_block(block)
                adjoint = g[block] * gate_out + carried[n * blocks + block]
                result.append(fades[way, step, n, :, lanes] * adjoint)
                through[block] = through[block] + adjoint * gate_in
                fading[block] = fading[block] + (
                    adjoint * kept[step, n, :, lanes] * rates[way, n, :, lanes]
                )
                product = adjoint * w[block] if block == 0 else product + adjoint * w[block]
            rows_of.append(product)
        put_products(0, step, rows_of)
        for block in range(blocks):
            lanes = lane_block(block)
            grad_delta = through[block] * signal[at(step), lanes] + fading[block] * LN2
            direct[at(step), lanes] = (
                direct[at(step), lanes] + through[block] * delta[way, at(step), lanes]
            )
            grad_pre[at(step), lanes] = grad_delta * slope[way, at(step), lanes]
        return tuple(result)

    lax.fori_loop(0, steps, walk_adjoints, entering(1), unroll=4)
    low[...] = dot(grad_pre[...].astype(BF16), w_delta[way], NT)
    row = lax.broadcasted_iota(jnp.int32, (2 * LANES, 2 * LANES), 0)
    column = lax.broadcasted_iota(jnp.int32, (2 * LANES, 2 * LANES), 1)
    halves = jnp.where(row // LANES == column // LANES, 1.0, 0.0).astype(BF16)
    lane = lax.broadcasted_iota(jnp.int32, (GROUPS, LANES), 1) - first
    height = depth * GROUPS
    for start in range(0, steps, 4):
        sums = dot(products[start * height : (start + 4) * height, :], halves)
        for step in range(4):
            spot = slice((start + step) * GROUPS, (start + step + 1) * GROUPS)
            merged = gate_grad[spot]
            for which in range(2):
                for n in range(depth):
                    top = step * height + n * GROUPS
                    merged = jnp.where(
                        lane == which * depth + n,
                        sums[top : top + GROUPS, lane_block(which)],
                        merged,
                    )
            gate_grad[spot] = merged


def own_gradient_kernel(skip_gain, *refs):
    signal, cot = refs[4:6]
    core, direct, _, gate_grad = refs[11:15]
    core[...] = skip_gain[...] * signal[...]
    direct[...] = skip_gain[...] * cot[...]
    gate_grad[...] = jnp.zeros_like(gate_grad)
    direction_gradient(lax.axis_index("seq") % 2, *refs)


def other_gradient_kernel(own_core, own_direct, own_low, own_gates, *refs):
    inputs = refs[:11]
    core, parts_out, direct, low, gate_grad = refs[11:16]
    way = 1 - lax.axis_index("seq") % 2
    core[...] = own_core[...]
    direct[...] = own_direct[...]
    gate_grad[...] = own_gates[...]
    direction_gradient(way, *inputs, core, direct, low, gate_grad, *refs[16:])
    rank = low.shape[1]
    gates = parts_out.shape[1] - 2 * rank
    parts_out[:, pl.ds(pl.multiple_of(way * rank, LANES), rank)] = low[...]
    parts_out[:, pl.ds(pl.multiple_of((1 - way) * rank, LANES), rank)] = own_low[...]
    parts_out[:, 2 * rank :] = gate_grad[:, :gates]


def finish_kernel(grad_proj, w_proj, direct, core, layer_out, signal_grad):
    ungroup = grouping(direct.shape[0], inverse=True)
    layer_out[...] = dot(ungroup, core[...].astype(BF16)).astype(BF16)
    total = dot(grad_proj[...], w_proj[...]) + direct[...]
    signal_grad[...] = dot(ungroup, total.astype(BF16)).astype(BF16)


def shape(*dims, dtype=F32):
    return jax.ShapeDtypeStruct(dims, dtype)


WHOLE = pl.BlockSpec(memory_space=pltpu.VMEM)


def kernel(body, out_shape, mebibytes, scratch=(), cost=0, **more):
    return pl.pallas_call(
        body,
        out_shape=out_shape,
        scratch_shapes=[
            pltpu.VMEM(*each) if isinstance(each, tuple) else each for each in scratch
        ],
        compiler_params=pltpu.CompilerParams(vmem_limit_bytes=mebibytes << 20),
        cost_estimate=pl.CostEstimate(flops=cost, bytes_accessed=cost, transcendentals=0),
        name=body.__name__,
        **more,
    )


def sum_over_chan(part):
    count = lax.axis_size("chan")
    rows, columns = part.shape
    pairs = [[2 * chip, 2 * chip + 1] for chip in range(count // 2)]
    across = [list(range(core, count, 2)) for core in range(2)]
    both = lax.all_gather(part, "chan", axis=0, tiled=True, axis_index_groups=pairs)
    copies = kernel(
        pair_kernel,
        shape(count // 2, rows // 2, columns, dtype=BF16),
        4,
    )(both)
    parts = lax.all_to_all(copies, "chan", 0, 0, tiled=True, axis_index_groups=across)
    half = kernel(chips_kernel, shape(rows // 2, columns, dtype=BF16), 4)(parts)
    return lax.all_gather(half, "chan", axis=0, tiled=True, axis_index_groups=pairs)


def local(signal, cotangent, w_proj, w_delta, delta_bias, decay_log, skip_gain):
    rows, width = signal.shape
    columns = w_proj.shape[1]
    depth = decay_log.shape[1]
    steps = rows // GROUPS
    shards = lax.axis_size("seq")
    if shards % 4:
        raise ValueError("shard count")
    w_turned = w_proj.T
    along_y = [[z * 4 + y for y in range(4)] for z in range(shards // 4)]
    along_z = [[z * 4 + y for z in range(shards // 4)] for y in range(4)]
    slots = depth + 4

    def exchange(array, groups):
        return lax.all_to_all(array, "seq", 0, 0, tiled=True, axis_index_groups=groups)

    signal_wide, part = kernel(
        project_kernel,
        (shape(rows, width), shape(rows, columns)),
        8,
        (((rows, width), BF16), ((columns, width), BF16), pltpu.SemaphoreType.DMA((2,))),
        in_specs=[pl.BlockSpec(memory_space=pltpu.HBM)] * 2,
        out_specs=(WHOLE, WHOLE),
    )(*(pltpu.with_memory_space_constraint(each, pltpu.HBM) for each in (signal, w_turned)))
    cot_wide, rates, flat, bias, gain = kernel(
        prepare_kernel,
        (
            shape(rows, width),
            shape(2, depth, GROUPS, width),
            shape(2, slots, width),
            shape(2, width),
            shape(1, width),
        ),
        8,
        cost=1 << 20,
    )(cotangent, decay_log.transpose(1, 0, 2), delta_bias, skip_gain.reshape(1, width))
    projected = sum_over_chan(part)
    wide = ((rows, 4 * depth * LANES), F32)
    stack = ((steps, depth, GROUPS, width), F32)
    delta, slope, local_states, ahead, payload = kernel(
        summary_kernel,
        (
            shape(2, rows, width),
            shape(2, rows, width),
            shape(4, depth, GROUPS, width),
            shape(4, GROUPS, width),
            shape(4, 2, slots, width, dtype=BF16),
        ),
        20,
        (((rows, width), F32), stack, wide, ((4, slots, width), F32)),
    )(projected, w_delta, bias, rates, signal_wide, cot_wide)
    parts = exchange(payload, along_y)
    copies = kernel(row_kernel, shape(shards // 4, slots, width, dtype=BF16), 4)(parts, flat)
    spread, fades = kernel(
        early_kernel,
        (
            shape(2, rows, 2 * depth * LANES),
            shape(2, steps, depth, GROUPS, width),
        ),
        8,
        cost=1 << 22,
    )(projected, rates, delta)
    row_totals = exchange(copies, along_z)
    entries, others = kernel(
        entry_kernel,
        (shape(2, slots, width), shape(2, slots, width)),
        4,
        (((4, slots, width), F32),),
    )(row_totals, parts, flat)
    swapped = lax.ppermute(others, "seq", [(shard, shard ^ 1) for shard in range(shards)])
    rank = w_delta.shape[1]
    inputs = (
        spread,
        fades,
        w_delta,
        rates,
        signal_wide,
        cot_wide,
        delta,
        slope,
        local_states,
        ahead,
    )
    scratch = (
        ((rows, width), F32),
        ((rows, width), F32),
        stack,
        ((rows * depth, 2 * LANES), BF16),
    )
    own = kernel(
        own_gradient_kernel,
        (
            shape(rows, width),
            shape(rows, width),
            shape(rows, rank),
            shape(rows, LANES),
        ),
        10,
        scratch,
        cost=1 << 22,
    )(gain, *inputs, entries)
    core, grad_parts, direct = kernel(
        other_gradient_kernel,
        (shape(rows, width), shape(rows, columns), shape(rows, width)),
        10,
        (((rows, rank), F32), ((rows, LANES), F32)) + scratch,
    )(*own, *inputs, swapped)
    grad_proj = sum_over_chan(grad_parts)
    result = shape(rows, width, dtype=BF16)
    layer_out, signal_grad = kernel(finish_kernel, (result, result), 8)(
        grad_proj, w_turned, direct, core
    )
    return (layer_out, signal_grad)


def solution(mesh):
    in_specs = (
        P("seq", "chan"),
        P("seq", "chan"),
        P("chan", None),
        P(None, None, "chan"),
        P(None, "chan"),
        P(None, None, "chan"),
        P("chan"),
    )
    out_specs = (P("seq", "chan"), P("seq", "chan"))
    return jax.shard_map(local, mesh=mesh, in_specs=in_specs, out_specs=out_specs, check_vma=False)
```

```python
import math

import jax
import jax.numpy as jnp
from jax import lax
from jax.experimental import pallas as pl
from jax.experimental.pallas import tpu as pltpu
from jax.sharding import PartitionSpec as P

GROUPS = 8
LANES = 128
LOG2E = math.log2(math.e)
LN2 = math.log(2.0)
FAR = 1e30
NT = (((1,), (1,)), ((), ()))
F32 = jnp.float32
BF16 = jnp.bfloat16


def dot(a, b, dims=(((1,), (0,)), ((), ()))):
    return lax.dot_general(a, b, dims, preferred_element_type=F32)


def grouping(rows, inverse=False):
    steps = rows // GROUPS
    row = lax.broadcasted_iota(jnp.int32, (rows, rows), 1 if inverse else 0)
    token = lax.broadcasted_iota(jnp.int32, (rows, rows), 0 if inverse else 1)
    return jnp.where(token == (row % GROUPS) * steps + row // GROUPS, 1.0, 0.0).astype(BF16)


def project_kernel(signal, w_proj, signal_out, part_out, signal_here, w_here, done):
    fetches = [
        pltpu.make_async_copy(signal, signal_here, done.at[0]),
        pltpu.make_async_copy(w_proj, w_here, done.at[1]),
    ]
    for fetch in fetches:
        fetch.start()
    order = grouping(signal_here.shape[0])
    fetches[0].wait()
    grouped = dot(order, signal_here[...])
    signal_out[...] = grouped
    fetches[1].wait()
    part_out[...] = dot(grouped.astype(BF16), w_here[...], NT)


def pair_kernel(both, copies):
    half = both.shape[0] // 4
    start = pl.multiple_of(lax.axis_index("chan") % 2 * half, half)
    total = both[pl.ds(start, half), :] + both[pl.ds(2 * half + start, half), :]
    for copy in range(copies.shape[0]):
        copies[copy] = total.astype(BF16)


def chips_kernel(parts, total):
    result = parts[0].astype(F32)
    for chip in range(1, parts.shape[0]):
        result = result + parts[chip].astype(F32)
    total[...] = result.astype(BF16)


def prepare_kernel(cotangent, decay_log, bias, skip_gain, cot_out, rates, flat, bias_out, gain_out):
    cot_out[...] = dot(grouping(cotangent.shape[0]), cotangent[...])
    bias_out[...] = bias[...]
    gain_out[...] = skip_gain[...]
    depth, _, width = decay_log.shape
    flat[...] = jnp.zeros_like(flat)
    for n in range(depth):
        scaled = -jnp.exp(decay_log[n]) * LOG2E
        for way in range(2):
            rates[way, n] = jnp.broadcast_to(scaled[way : way + 1], (GROUPS, width))
            flat[way, n : n + 1] = scaled[way : way + 1]


def at(step):
    return pl.ds(pl.multiple_of(step * GROUPS, GROUPS), GROUPS)


def lane_block(block):
    return slice(block * LANES, (block + 1) * LANES)


def spread_gates(gates, spread, first=0):
    count = gates.shape[1]
    for pair in range(spread.shape[1] // (2 * LANES)):
        source = lax.broadcasted_iota(jnp.int32, (count, 2 * LANES), 0)
        lane = lax.broadcasted_iota(jnp.int32, (count, 2 * LANES), 1)
        pick = jnp.where(source == first + 2 * pair + lane // LANES, 1.0, 0.0).astype(BF16)
        spread[:, pair * 2 * LANES : (pair + 1) * 2 * LANES] = dot(gates, pick)


def gate_at(spread, step, column):
    return spread[at(step), column * LANES : (column + 1) * LANES]


def put_total(shares, kind, lanes, total):
    depth = shares.shape[1] - 4
    coarse = total.astype(BF16).astype(F32)
    shares[kind, depth : depth + 1, lanes] = coarse
    shares[kind, depth + 1 : depth + 2, lanes] = total - coarse


def summary_kernel(
    projected,
    w_delta,
    bias,
    rates,
    signal,
    cot,
    delta_out,
    pre_out,
    local_out,
    ahead_out,
    payload,
    weight,
    fades,
    spread,
    shares,
):
    rows, width = signal.shape
    rank = w_delta.shape[1]
    depth = rates.shape[1]
    steps = rows // GROUPS
    blocks = width // LANES
    spread_gates(projected[:, 2 * rank :], spread)
    shares[...] = jnp.zeros_like(shares)
    group = lax.broadcasted_iota(jnp.int32, (GROUPS, LANES), 0)
    for way in range(2):
        pre = dot(projected[:, way * rank : (way + 1) * rank], w_delta[way]) + bias[way : way + 1]
        delta = jnp.maximum(pre, 0.0) + jnp.log1p(jnp.exp(-jnp.abs(pre)))
        delta_out[way] = delta
        pre_out[way] = pre
        weight[...] = delta * signal[...]
        falling = way == 1
        zero = jnp.zeros((GROUPS, LANES), F32)
        many = (zero,) * (blocks * depth)

        def walk_states(index, carry):
            states, total = carry
            step = steps - 1 - index if falling else index
            d = [delta_out[way, at(step), lane_block(block)] for block in range(blocks)]
            w = [weight[at(step), lane_block(block)] for block in range(blocks)]
            result = []
            for n in range(depth):
                gate = gate_at(spread, step, 2 * way * depth + n)
                for block in range(blocks):
                    fade = jnp.exp2(d[block] * rates[way, n, :, lane_block(block)])
                    fades[step, n, :, lane_block(block)] = fade
                    result.append(fade * states[n * blocks + block] + w[block] * gate)
            return (tuple(result), tuple(t + x for t, x in zip(total, d)))

        states, total = lax.fori_loop(0, steps, walk_states, (many, (zero,) * blocks), unroll=4)

        def walk_adjoints(index, carried):
            step = index if falling else steps - 1 - index
            g = [cot[at(step), lane_block(block)] for block in range(blocks)]
            result = []
            for n in range(depth):
                gate = gate_at(spread, step, (2 * way + 1) * depth + n)
                for block in range(blocks):
                    fade = fades[step, n, :, lane_block(block)]
                    result.append(fade * (g[block] * gate + carried[n * blocks + block]))
            return tuple(result)

        carried = lax.fori_loop(0, steps, walk_adjoints, many, unroll=4)
        for block in range(blocks):
            lanes = lane_block(block)

            def shift(array, by, down):
                return pltpu.roll(array, GROUPS - by if down else by, 0)

            def beyond(by, down):
                return group >= GROUPS - by if down else group < by

            whole = jnp.sum(total[block], 0, keepdims=True)
            for kind, down, finals in ((0, falling, states), (1, not falling, carried)):
                windows = []
                window = total[block]
                ahead = jnp.where(beyond(1, down), 0.0, shift(window, 1, down))
                for by in (1, 2, 4):
                    windows.append(jnp.where(beyond(by, down), FAR, window))
                    outside = beyond(by, down)
                    window = window + jnp.where(outside, 0.0, shift(window, by, down))
                    ahead = ahead + jnp.where(outside, 0.0, shift(ahead, by, down))
                ahead_out[2 * way + kind, :, lanes] = ahead
                edge = 0 if down else GROUPS - 1
                for n in range(depth):
                    rate = rates[way, n, :, lanes]
                    scanned = finals[n * blocks + block]
                    for by, span in zip((1, 2, 4), windows):
                        scanned = scanned + jnp.exp2(rate * span) * shift(scanned, by, down)
                    local_out[2 * way + kind, n, :, lanes] = jnp.where(
                        beyond(1, down), 0.0, shift(scanned, 1, down)
                    )
                    shares[2 * way + kind, n : n + 1, lanes] = scanned[edge : edge + 1]
                put_total(shares, 2 * way + kind, lanes, whole)
    for shard in range(payload.shape[0]):
        way = shard % 2
        payload[shard] = shares[2 * way : 2 * way + 2].astype(BF16)


def order(count, falling):
    return range(count - 1, -1, -1) if falling else range(count)


def pass_by(state, block, rates):
    depth = block.shape[0] - 4
    total = block[depth : depth + 1] + block[depth + 1 : depth + 2]
    return jnp.exp2(rates * total) * state + block


def place_of(shards):
    place = lax.axis_index("seq")
    return place // shards, place % shards, place % 2


def row_kernel(parts, flat, copies):
    shards, _, slots, width = parts.shape
    depth = slots - 4
    here, _, way = place_of(shards)
    slot = lax.broadcasted_iota(jnp.int32, (slots, width), 0)
    packed = []
    for falling in (False, True):
        state = jnp.zeros((slots, width), F32)
        total = jnp.zeros((1, width), F32)
        for shard in order(shards, falling):
            block = parts[shard, 1 - way if falling else way].astype(F32)
            total = total + block[depth : depth + 1] + block[depth + 1 : depth + 2]
            state = pass_by(state, block, flat[way])
        coarse = total.astype(BF16).astype(F32)
        state = jnp.where(slot == depth, coarse, state)
        state = jnp.where(slot == depth + 1, total - coarse, state)
        packed.append(jnp.where(slot > depth + 1, 0.0, state).astype(BF16))
    for row in range(copies.shape[0]):

        @pl.when(row > here)
        def _():
            copies[row] = packed[0]

        @pl.when(row <= here)
        def _():
            copies[row] = packed[1]


def entry_kernel(rows, parts, flat, mine, other, every):
    count, slots, width = rows.shape
    shards = parts.shape[0]
    row_here, here, way = place_of(shards)
    rates = flat[way]
    for falling in (False, True):
        kind = 1 - way if falling else way
        state = jnp.zeros((slots, width), F32)
        for row in order(count, falling):
            passed = pass_by(state, rows[row].astype(F32), rates)
            state = jnp.where(row > row_here if falling else row < row_here, passed, state)
        for shard in order(shards, falling):
            every[shard] = state
            state = pass_by(state, parts[shard, kind].astype(F32), rates)
        mine[kind] = every[here]
        other[kind] = every[here + 1 - 2 * way].astype(BF16)


def early_kernel(projected, rates, delta, pre, spread, fades, slope):
    for way in range(2):
        slope[way] = 1.0 / (1.0 + jnp.exp(-pre[way]))
    _, steps, depth, _, _ = fades.shape
    rank = (projected.shape[1] - 4 * depth) // 2
    for way in range(2):
        spread_gates(projected[:, 2 * rank :], spread.at[way], 2 * way * depth)

    def walk(step, _):
        for way in range(2):
            d = delta[way, at(step), :]
            for n in range(depth):
                fades[way, step, n] = jnp.exp2(d * rates[way, n])
        return _

    lax.fori_loop(0, steps, walk, 0)


def direction_gradient(
    way,
    spread,
    fades,
    w_delta,
    rates,
    signal,
    cot,
    delta,
    slope,
    local,
    ahead,
    entries,
    core,
    direct,
    low,
    gate_grad,
    weight,
    grad_pre,
    kept,
    products,
):
    rows, width = signal.shape
    depth = rates.shape[1]
    steps = rows // GROUPS
    blocks = width // LANES
    first = 2 * way * depth
    weight[...] = delta[way] * signal[...]

    def entering(kind):
        arrived = entries[kind].astype(F32)
        gap = [ahead[2 * way + kind, :, lane_block(block)] for block in range(blocks)]
        return tuple(
            local[2 * way + kind, n, :, lane_block(block)]
            + jnp.exp2(gap[block] * rates[way, n, :, lane_block(block)])
            * arrived[n : n + 1, lane_block(block)]
            for n in range(depth)
            for block in range(blocks)
        )

    def pieces(array, step):
        return [array[at(step), lane_block(block)] for block in range(blocks)]

    def put_products(which, step, rows_of):
        start = pl.multiple_of(step * depth * GROUPS, 2 * GROUPS)
        stacked = jnp.concatenate(rows_of, 0).astype(BF16)
        products[pl.ds(start, depth * GROUPS), lane_block(which)] = stacked

    def walk_states(index, states):
        step = index + way * (steps - 1 - 2 * index)
        w, g = pieces(weight, step), pieces(cot, step)
        total = pieces(core, step)
        rows_of = []
        result = []
        for n in range(depth):
            gate_in = gate_at(spread.at[way], step, n)
            gate_out = gate_at(spread.at[way], step, depth + n)
            for block in range(blocks):
                lanes = lane_block(block)
                faded = fades[way, step, n, :, lanes] * states[n * blocks + block]
                kept[step, n, :, lanes] = faded
                state = faded + w[block] * gate_in
                total[block] = total[block] + gate_out * state
                product = g[block] * state if block == 0 else product + g[block] * state
                result.append(state)
            rows_of.append(product)
        for block in range(blocks):
            core[at(step), lane_block(block)] = total[block]
        put_products(1, step, rows_of)
        return tuple(result)

    lax.fori_loop(0, steps, walk_states, entering(0), unroll=4)

    def walk_adjoints(index, carried):
        step = steps - 1 - index + way * (2 * index - steps + 1)
        w, g = pieces(weight, step), pieces(cot, step)
        rows_of = []
        through = [jnp.zeros((GROUPS, LANES), F32)] * blocks
        fading = [jnp.zeros((GROUPS, LANES), F32)] * blocks
        result = []
        for n in range(depth):
            gate_in = gate_at(spread.at[way], step, n)
            gate_out = gate_at(spread.at[way], step, depth + n)
            for block in range(blocks):
                lanes = lane_block(block)
                adjoint = g[block] * gate_out + carried[n * blocks + block]
                result.append(fades[way, step, n, :, lanes] * adjoint)
                through[block] = through[block] + adjoint * gate_in
                fading[block] = fading[block] + (
                    adjoint * kept[step, n, :, lanes] * rates[way, n, :, lanes]
                )
                product = adjoint * w[block] if block == 0 else product + adjoint * w[block]
            rows_of.append(product)
        put_products(0, step, rows_of)
        for block in range(blocks):
            lanes = lane_block(block)
            grad_delta = through[block] * signal[at(step), lanes] + fading[block] * LN2
            direct[at(step), lanes] = (
                direct[at(step), lanes] + through[block] * delta[way, at(step), lanes]
            )
            grad_pre[at(step), lanes] = grad_delta * slope[way, at(step), lanes]
        return tuple(result)

    lax.fori_loop(0, steps, walk_adjoints, entering(1), unroll=4)
    low[...] = dot(grad_pre[...].astype(BF16), w_delta[way], NT)
    row = lax.broadcasted_iota(jnp.int32, (2 * LANES, 2 * LANES), 0)
    column = lax.broadcasted_iota(jnp.int32, (2 * LANES, 2 * LANES), 1)
    halves = jnp.where(row // LANES == column // LANES, 1.0, 0.0).astype(BF16)
    lane = lax.broadcasted_iota(jnp.int32, (GROUPS, LANES), 1) - first
    height = depth * GROUPS
    for start in range(0, steps, 4):
        sums = dot(products[start * height : (start + 4) * height, :], halves)
        for step in range(4):
            spot = slice((start + step) * GROUPS, (start + step + 1) * GROUPS)
            merged = gate_grad[spot]
            for which in range(2):
                for n in range(depth):
                    top = step * height + n * GROUPS
                    merged = jnp.where(
                        lane == which * depth + n,
                        sums[top : top + GROUPS, lane_block(which)],
                        merged,
                    )
            gate_grad[spot] = merged


def own_gradient_kernel(skip_gain, *refs):
    signal, cot = refs[4:6]
    core, direct, _, gate_grad = refs[11:15]
    core[...] = skip_gain[...] * signal[...]
    direct[...] = skip_gain[...] * cot[...]
    gate_grad[...] = jnp.zeros_like(gate_grad)
    direction_gradient(lax.axis_index("seq") % 2, *refs)


def other_gradient_kernel(own_core, own_direct, own_low, own_gates, *refs):
    inputs = refs[:11]
    core, parts_out, direct, low, gate_grad = refs[11:16]
    way = 1 - lax.axis_index("seq") % 2
    core[...] = own_core[...]
    direct[...] = own_direct[...]
    gate_grad[...] = own_gates[...]
    direction_gradient(way, *inputs, core, direct, low, gate_grad, *refs[16:])
    rank = low.shape[1]
    gates = parts_out.shape[1] - 2 * rank
    parts_out[:, pl.ds(pl.multiple_of(way * rank, LANES), rank)] = low[...]
    parts_out[:, pl.ds(pl.multiple_of((1 - way) * rank, LANES), rank)] = own_low[...]
    parts_out[:, 2 * rank :] = gate_grad[:, :gates]


def finish_kernel(grad_proj, w_proj, direct, core, layer_out, signal_grad):
    ungroup = grouping(direct.shape[0], inverse=True)
    layer_out[...] = dot(ungroup, core[...].astype(BF16)).astype(BF16)
    total = dot(grad_proj[...], w_proj[...]) + direct[...]
    signal_grad[...] = dot(ungroup, total.astype(BF16)).astype(BF16)


def shape(*dims, dtype=F32):
    return jax.ShapeDtypeStruct(dims, dtype)


WHOLE = pl.BlockSpec(memory_space=pltpu.VMEM)


def kernel(body, out_shape, mebibytes, scratch=(), cost=0, **more):
    return pl.pallas_call(
        body,
        out_shape=out_shape,
        scratch_shapes=[
            pltpu.VMEM(*each) if isinstance(each, tuple) else each for each in scratch
        ],
        compiler_params=pltpu.CompilerParams(vmem_limit_bytes=mebibytes << 20),
        cost_estimate=pl.CostEstimate(flops=cost, bytes_accessed=cost, transcendentals=0),
        name=body.__name__,
        **more,
    )


def sum_over_chan(part):
    count = lax.axis_size("chan")
    rows, columns = part.shape
    pairs = [[2 * chip, 2 * chip + 1] for chip in range(count // 2)]
    across = [list(range(core, count, 2)) for core in range(2)]
    both = lax.all_gather(part, "chan", axis=0, tiled=True, axis_index_groups=pairs)
    copies = kernel(
        pair_kernel,
        shape(count // 2, rows // 2, columns, dtype=BF16),
        4,
    )(both)
    parts = lax.all_to_all(copies, "chan", 0, 0, tiled=True, axis_index_groups=across)
    half = kernel(chips_kernel, shape(rows // 2, columns, dtype=BF16), 4)(parts)
    return lax.all_gather(half, "chan", axis=0, tiled=True, axis_index_groups=pairs)


def local(signal, cotangent, w_proj, w_delta, delta_bias, decay_log, skip_gain):
    rows, width = signal.shape
    columns = w_proj.shape[1]
    depth = decay_log.shape[1]
    steps = rows // GROUPS
    shards = lax.axis_size("seq")
    if shards % 4:
        raise ValueError("shard count")
    w_turned = w_proj.T
    along_y = [[z * 4 + y for y in range(4)] for z in range(shards // 4)]
    along_z = [[z * 4 + y for z in range(shards // 4)] for y in range(4)]
    slots = depth + 4

    def exchange(array, groups):
        return lax.all_to_all(array, "seq", 0, 0, tiled=True, axis_index_groups=groups)

    signal_wide, part = kernel(
        project_kernel,
        (shape(rows, width), shape(rows, columns)),
        8,
        (((rows, width), BF16), ((columns, width), BF16), pltpu.SemaphoreType.DMA((2,))),
        in_specs=[pl.BlockSpec(memory_space=pltpu.HBM)] * 2,
        out_specs=(WHOLE, WHOLE),
    )(*(pltpu.with_memory_space_constraint(each, pltpu.HBM) for each in (signal, w_turned)))
    cot_wide, rates, flat, bias, gain = kernel(
        prepare_kernel,
        (
            shape(rows, width),
            shape(2, depth, GROUPS, width),
            shape(2, slots, width),
            shape(2, width),
            shape(1, width),
        ),
        8,
        cost=1 << 20,
    )(cotangent, decay_log.transpose(1, 0, 2), delta_bias, skip_gain.reshape(1, width))
    projected = sum_over_chan(part)
    wide = ((rows, 4 * depth * LANES), F32)
    stack = ((steps, depth, GROUPS, width), F32)
    delta, pre, local_states, ahead, payload = kernel(
        summary_kernel,
        (
            shape(2, rows, width),
            shape(2, rows, width),
            shape(4, depth, GROUPS, width),
            shape(4, GROUPS, width),
            shape(4, 2, slots, width, dtype=BF16),
        ),
        20,
        (((rows, width), F32), stack, wide, ((4, slots, width), F32)),
    )(projected, w_delta, bias, rates, signal_wide, cot_wide)
    parts = exchange(payload, along_y)
    copies = kernel(row_kernel, shape(shards // 4, slots, width, dtype=BF16), 4)(parts, flat)
    spread, fades, slope = kernel(
        early_kernel,
        (
            shape(2, rows, 2 * depth * LANES),
            shape(2, steps, depth, GROUPS, width),
            shape(2, rows, width),
        ),
        8,
        cost=1 << 22,
    )(projected, rates, delta, pre)
    row_totals = exchange(copies, along_z)
    entries, others = kernel(
        entry_kernel,
        (shape(2, slots, width), shape(2, slots, width, dtype=BF16)),
        4,
        (((4, slots, width), F32),),
    )(row_totals, parts, flat)
    swapped = lax.ppermute(others, "seq", [(shard, shard ^ 1) for shard in range(shards)])
    rank = w_delta.shape[1]
    inputs = (
        spread,
        fades,
        w_delta,
        rates,
        signal_wide,
        cot_wide,
        delta,
        slope,
        local_states,
        ahead,
    )
    scratch = (
        ((rows, width), F32),
        ((rows, width), F32),
        stack,
        ((rows * depth, 2 * LANES), BF16),
    )
    own = kernel(
        own_gradient_kernel,
        (
            shape(rows, width),
            shape(rows, width),
            shape(rows, rank),
            shape(rows, LANES),
        ),
        10,
        scratch,
        cost=1 << 22,
    )(gain, *inputs, entries)
    core, grad_parts, direct = kernel(
        other_gradient_kernel,
        (shape(rows, width), shape(rows, columns), shape(rows, width)),
        10,
        (((rows, rank), F32), ((rows, LANES), F32)) + scratch,
    )(*own, *inputs, swapped)
    grad_proj = sum_over_chan(grad_parts)
    result = shape(rows, width, dtype=BF16)
    layer_out, signal_grad = kernel(finish_kernel, (result, result), 8)(
        grad_proj, w_turned, direct, core
    )
    return (layer_out, signal_grad)


def solution(mesh):
    in_specs = (
        P("seq", "chan"),
        P("seq", "chan"),
        P("chan", None),
        P(None, None, "chan"),
        P(None, "chan"),
        P(None, None, "chan"),
        P("chan"),
    )
    out_specs = (P("seq", "chan"), P("seq", "chan"))
    return jax.shard_map(local, mesh=mesh, in_specs=in_specs, out_specs=out_specs, check_vma=False)
```

```python
import math

import jax
import jax.numpy as jnp
from jax import lax
from jax.experimental import pallas as pl
from jax.experimental.pallas import tpu as pltpu
from jax.sharding import PartitionSpec as P

GROUPS = 8
LANES = 128
LOG2E = math.log2(math.e)
LN2 = math.log(2.0)
FAR = 1e30
NT = (((1,), (1,)), ((), ()))
F32 = jnp.float32
BF16 = jnp.bfloat16


def dot(a, b, dims=(((1,), (0,)), ((), ()))):
    return lax.dot_general(a, b, dims, preferred_element_type=F32)


def grouping(rows, inverse=False):
    steps = rows // GROUPS
    row = lax.broadcasted_iota(jnp.int32, (rows, rows), 1 if inverse else 0)
    token = lax.broadcasted_iota(jnp.int32, (rows, rows), 0 if inverse else 1)
    return jnp.where(token == (row % GROUPS) * steps + row // GROUPS, 1.0, 0.0).astype(BF16)


def project_kernel(signal, w_proj, signal_out, part_out, signal_here, w_here, done):
    fetches = [
        pltpu.make_async_copy(signal, signal_here, done.at[0]),
        pltpu.make_async_copy(w_proj, w_here, done.at[1]),
    ]
    for fetch in fetches:
        fetch.start()
    order = grouping(signal_here.shape[0])
    fetches[0].wait()
    grouped = dot(order, signal_here[...])
    signal_out[...] = grouped
    fetches[1].wait()
    part_out[...] = dot(grouped.astype(BF16), w_here[...], NT)


def pair_kernel(both, copies):
    half = both.shape[0] // 4
    start = pl.multiple_of(lax.axis_index("chan") % 2 * half, half)
    total = both[pl.ds(start, half), :] + both[pl.ds(2 * half + start, half), :]
    for copy in range(copies.shape[0]):
        copies[copy] = total.astype(BF16)


def chips_kernel(parts, total):
    result = parts[0].astype(F32)
    for chip in range(1, parts.shape[0]):
        result = result + parts[chip].astype(F32)
    total[...] = result.astype(BF16)


def prepare_kernel(cotangent, decay_log, bias, skip_gain, cot_out, rates, flat, bias_out, gain_out):
    cot_out[...] = dot(grouping(cotangent.shape[0]), cotangent[...])
    bias_out[...] = bias[...]
    gain_out[...] = skip_gain[...]
    depth, _, width = decay_log.shape
    flat[...] = jnp.zeros_like(flat)
    for n in range(depth):
        scaled = -jnp.exp(decay_log[n]) * LOG2E
        for way in range(2):
            rates[way, n] = jnp.broadcast_to(scaled[way : way + 1], (GROUPS, width))
            flat[way, n : n + 1] = scaled[way : way + 1]


def at(step):
    return pl.ds(pl.multiple_of(step * GROUPS, GROUPS), GROUPS)


def lane_block(block):
    return slice(block * LANES, (block + 1) * LANES)


def spread_gates(gates, spread, first=0):
    count = gates.shape[1]
    for pair in range(spread.shape[1] // (2 * LANES)):
        source = lax.broadcasted_iota(jnp.int32, (count, 2 * LANES), 0)
        lane = lax.broadcasted_iota(jnp.int32, (count, 2 * LANES), 1)
        pick = jnp.where(source == first + 2 * pair + lane // LANES, 1.0, 0.0).astype(BF16)
        spread[:, pair * 2 * LANES : (pair + 1) * 2 * LANES] = dot(gates, pick)


def gate_at(spread, step, column):
    return spread[at(step), column * LANES : (column + 1) * LANES]


def put_total(shares, kind, lanes, total):
    depth = shares.shape[1] - 4
    coarse = total.astype(BF16).astype(F32)
    shares[kind, depth : depth + 1, lanes] = coarse
    shares[kind, depth + 1 : depth + 2, lanes] = total - coarse


def summary_kernel(
    projected,
    w_delta,
    bias,
    rates,
    signal,
    cot,
    delta_out,
    slope_out,
    local_out,
    ahead_out,
    payload,
    weight,
    fades,
    spread,
    shares,
):
    rows, width = signal.shape
    rank = w_delta.shape[1]
    depth = rates.shape[1]
    steps = rows // GROUPS
    blocks = width // LANES
    spread_gates(projected[:, 2 * rank :], spread)
    shares[...] = jnp.zeros_like(shares)
    group = lax.broadcasted_iota(jnp.int32, (GROUPS, LANES), 0)
    for way in range(2):
        pre = dot(projected[:, way * rank : (way + 1) * rank], w_delta[way]) + bias[way : way + 1]
        delta = jnp.maximum(pre, 0.0) + jnp.log1p(jnp.exp(-jnp.abs(pre)))
        delta_out[way] = delta
        slope_out[way] = 1.0 / (1.0 + jnp.exp(-pre))
        weight[...] = delta * signal[...]
        falling = way == 1
        zero = jnp.zeros((GROUPS, LANES), F32)
        many = (zero,) * (blocks * depth)

        def walk_states(index, carry):
            states, total = carry
            step = steps - 1 - index if falling else index
            d = [delta_out[way, at(step), lane_block(block)] for block in range(blocks)]
            w = [weight[at(step), lane_block(block)] for block in range(blocks)]
            result = []
            for n in range(depth):
                gate = gate_at(spread, step, 2 * way * depth + n)
                for block in range(blocks):
                    fade = jnp.exp2(d[block] * rates[way, n, :, lane_block(block)])
                    fades[step, n, :, lane_block(block)] = fade
                    result.append(fade * states[n * blocks + block] + w[block] * gate)
            return (tuple(result), tuple(t + x for t, x in zip(total, d)))

        states, total = lax.fori_loop(0, steps, walk_states, (many, (zero,) * blocks), unroll=8)

        def walk_adjoints(index, carried):
            step = index if falling else steps - 1 - index
            g = [cot[at(step), lane_block(block)] for block in range(blocks)]
            result = []
            for n in range(depth):
                gate = gate_at(spread, step, (2 * way + 1) * depth + n)
                for block in range(blocks):
                    fade = fades[step, n, :, lane_block(block)]
                    result.append(fade * (g[block] * gate + carried[n * blocks + block]))
            return tuple(result)

        carried = lax.fori_loop(0, steps, walk_adjoints, many, unroll=8)
        for block in range(blocks):
            lanes = lane_block(block)

            def shift(array, by, down):
                return pltpu.roll(array, GROUPS - by if down else by, 0)

            def beyond(by, down):
                return group >= GROUPS - by if down else group < by

            whole = jnp.sum(total[block], 0, keepdims=True)
            for kind, down, finals in ((0, falling, states), (1, not falling, carried)):
                windows = []
                window = total[block]
                ahead = jnp.where(beyond(1, down), 0.0, shift(window, 1, down))
                for by in (1, 2, 4):
                    windows.append(jnp.where(beyond(by, down), FAR, window))
                    outside = beyond(by, down)
                    window = window + jnp.where(outside, 0.0, shift(window, by, down))
                    ahead = ahead + jnp.where(outside, 0.0, shift(ahead, by, down))
                ahead_out[2 * way + kind, :, lanes] = ahead
                edge = 0 if down else GROUPS - 1
                for n in range(depth):
                    rate = rates[way, n, :, lanes]
                    scanned = finals[n * blocks + block]
                    for by, span in zip((1, 2, 4), windows):
                        scanned = scanned + jnp.exp2(rate * span) * shift(scanned, by, down)
                    local_out[2 * way + kind, n, :, lanes] = jnp.where(
                        beyond(1, down), 0.0, shift(scanned, 1, down)
                    )
                    shares[2 * way + kind, n : n + 1, lanes] = scanned[edge : edge + 1]
                put_total(shares, 2 * way + kind, lanes, whole)
    for shard in range(payload.shape[0]):
        way = shard % 2
        payload[shard] = shares[2 * way : 2 * way + 2].astype(BF16)


def order(count, falling):
    return range(count - 1, -1, -1) if falling else range(count)


def pass_by(state, block, rates):
    depth = block.shape[0] - 4
    total = block[depth : depth + 1] + block[depth + 1 : depth + 2]
    return jnp.exp2(rates * total) * state + block


def place_of(shards):
    place = lax.axis_index("seq")
    return place // shards, place % shards, place % 2


def row_kernel(parts, flat, copies):
    shards, _, slots, width = parts.shape
    depth = slots - 4
    here, _, way = place_of(shards)
    slot = lax.broadcasted_iota(jnp.int32, (slots, width), 0)
    packed = []
    for falling in (False, True):
        state = jnp.zeros((slots, width), F32)
        total = jnp.zeros((1, width), F32)
        for shard in order(shards, falling):
            block = parts[shard, 1 - way if falling else way].astype(F32)
            total = total + block[depth : depth + 1] + block[depth + 1 : depth + 2]
            state = pass_by(state, block, flat[way])
        coarse = total.astype(BF16).astype(F32)
        state = jnp.where(slot == depth, coarse, state)
        state = jnp.where(slot == depth + 1, total - coarse, state)
        packed.append(jnp.where(slot > depth + 1, 0.0, state).astype(BF16))
    for row in range(copies.shape[0]):

        @pl.when(row > here)
        def _():
            copies[row] = packed[0]

        @pl.when(row <= here)
        def _():
            copies[row] = packed[1]


def entry_kernel(rows, parts, flat, mine, other, every):
    count, slots, width = rows.shape
    shards = parts.shape[0]
    row_here, here, way = place_of(shards)
    rates = flat[way]
    for falling in (False, True):
        kind = 1 - way if falling else way
        state = jnp.zeros((slots, width), F32)
        for row in order(count, falling):
            passed = pass_by(state, rows[row].astype(F32), rates)
            state = jnp.where(row > row_here if falling else row < row_here, passed, state)
        for shard in order(shards, falling):
            every[shard] = state
            state = pass_by(state, parts[shard, kind].astype(F32), rates)
        mine[kind] = every[here]
        other[kind] = every[here + 1 - 2 * way]


def early_kernel(projected, rates, delta, spread, fades):
    _, steps, depth, _, _ = fades.shape
    rank = (projected.shape[1] - 4 * depth) // 2
    for way in range(2):
        spread_gates(projected[:, 2 * rank :], spread.at[way], 2 * way * depth)

    def walk(step, _):
        for way in range(2):
            d = delta[way, at(step), :]
            for n in range(depth):
                fades[way, step, n] = jnp.exp2(d * rates[way, n])
        return _

    lax.fori_loop(0, steps, walk, 0, unroll=4)


def direction_gradient(
    way,
    spread,
    fades,
    w_delta,
    rates,
    signal,
    cot,
    delta,
    slope,
    local,
    ahead,
    entries,
    core,
    direct,
    low,
    gate_grad,
    weight,
    grad_pre,
    kept,
    products,
):
    rows, width = signal.shape
    depth = rates.shape[1]
    steps = rows // GROUPS
    blocks = width // LANES
    first = 2 * way * depth
    weight[...] = delta[way] * signal[...]

    def entering(kind):
        gap = [ahead[2 * way + kind, :, lane_block(block)] for block in range(blocks)]
        return tuple(
            local[2 * way + kind, n, :, lane_block(block)]
            + jnp.exp2(gap[block] * rates[way, n, :, lane_block(block)])
            * entries[kind, n : n + 1, lane_block(block)]
            for n in range(depth)
            for block in range(blocks)
        )

    def pieces(array, step):
        return [array[at(step), lane_block(block)] for block in range(blocks)]

    def put_products(which, step, rows_of):
        start = pl.multiple_of(step * depth * GROUPS, 2 * GROUPS)
        stacked = jnp.concatenate(rows_of, 0).astype(BF16)
        products[pl.ds(start, depth * GROUPS), lane_block(which)] = stacked

    def walk_states(index, states):
        step = index + way * (steps - 1 - 2 * index)
        w, g = pieces(weight, step), pieces(cot, step)
        total = pieces(core, step)
        rows_of = []
        result = []
        for n in range(depth):
            gate_in = gate_at(spread.at[way], step, n)
            gate_out = gate_at(spread.at[way], step, depth + n)
            for block in range(blocks):
                lanes = lane_block(block)
                faded = fades[way, step, n, :, lanes] * states[n * blocks + block]
                kept[step, n, :, lanes] = faded
                state = faded + w[block] * gate_in
                total[block] = total[block] + gate_out * state
                product = g[block] * state if block == 0 else product + g[block] * state
                result.append(state)
            rows_of.append(product)
        for block in range(blocks):
            core[at(step), lane_block(block)] = total[block]
        put_products(1, step, rows_of)
        return tuple(result)

    lax.fori_loop(0, steps, walk_states, entering(0), unroll=8)

    def walk_adjoints(index, carried):
        step = steps - 1 - index + way * (2 * index - steps + 1)
        w, g = pieces(weight, step), pieces(cot, step)
        rows_of = []
        through = [jnp.zeros((GROUPS, LANES), F32)] * blocks
        fading = [jnp.zeros((GROUPS, LANES), F32)] * blocks
        result = []
        for n in range(depth):
            gate_in = gate_at(spread.at[way], step, n)
            gate_out = gate_at(spread.at[way], step, depth + n)
            for block in range(blocks):
                lanes = lane_block(block)
                adjoint = g[block] * gate_out + carried[n * blocks + block]
                result.append(fades[way, step, n, :, lanes] * adjoint)
                through[block] = through[block] + adjoint * gate_in
                fading[block] = fading[block] + (
                    adjoint * kept[step, n, :, lanes] * rates[way, n, :, lanes]
                )
                product = adjoint * w[block] if block == 0 else product + adjoint * w[block]
            rows_of.append(product)
        put_products(0, step, rows_of)
        for block in range(blocks):
            lanes = lane_block(block)
            grad_delta = through[block] * signal[at(step), lanes] + fading[block] * LN2
            direct[at(step), lanes] = (
                direct[at(step), lanes] + through[block] * delta[way, at(step), lanes]
            )
            grad_pre[at(step), lanes] = grad_delta * slope[way, at(step), lanes]
        return tuple(result)

    lax.fori_loop(0, steps, walk_adjoints, entering(1), unroll=8)
    low[...] = dot(grad_pre[...].astype(BF16), w_delta[way], NT)
    row = lax.broadcasted_iota(jnp.int32, (2 * LANES, 2 * LANES), 0)
    column = lax.broadcasted_iota(jnp.int32, (2 * LANES, 2 * LANES), 1)
    halves = jnp.where(row // LANES == column // LANES, 1.0, 0.0).astype(BF16)
    lane = lax.broadcasted_iota(jnp.int32, (GROUPS, LANES), 1) - first
    height = depth * GROUPS
    for start in range(0, steps, 4):
        sums = dot(products[start * height : (start + 4) * height, :], halves)
        for step in range(4):
            spot = slice((start + step) * GROUPS, (start + step + 1) * GROUPS)
            merged = gate_grad[spot]
            for which in range(2):
                for n in range(depth):
                    top = step * height + n * GROUPS
                    merged = jnp.where(
                        lane == which * depth + n,
                        sums[top : top + GROUPS, lane_block(which)],
                        merged,
                    )
            gate_grad[spot] = merged


def own_gradient_kernel(skip_gain, *refs):
    signal, cot = refs[4:6]
    core, direct, _, gate_grad = refs[11:15]
    core[...] = skip_gain[...] * signal[...]
    direct[...] = skip_gain[...] * cot[...]
    gate_grad[...] = jnp.zeros_like(gate_grad)
    direction_gradient(lax.axis_index("seq") % 2, *refs)


def other_gradient_kernel(own_core, own_direct, own_low, own_gates, *refs):
    inputs = refs[:11]
    core, parts_out, direct, low, gate_grad = refs[11:16]
    way = 1 - lax.axis_index("seq") % 2
    core[...] = own_core[...]
    direct[...] = own_direct[...]
    gate_grad[...] = own_gates[...]
    direction_gradient(way, *inputs, core, direct, low, gate_grad, *refs[16:])
    rank = low.shape[1]
    gates = parts_out.shape[1] - 2 * rank
    parts_out[:, pl.ds(pl.multiple_of(way * rank, LANES), rank)] = low[...]
    parts_out[:, pl.ds(pl.multiple_of((1 - way) * rank, LANES), rank)] = own_low[...]
    parts_out[:, 2 * rank :] = gate_grad[:, :gates]


def finish_kernel(grad_proj, w_proj, direct, core, layer_out, signal_grad):
    ungroup = grouping(direct.shape[0], inverse=True)
    layer_out[...] = dot(ungroup, core[...].astype(BF16)).astype(BF16)
    total = dot(grad_proj[...], w_proj[...]) + direct[...]
    signal_grad[...] = dot(ungroup, total.astype(BF16)).astype(BF16)


def shape(*dims, dtype=F32):
    return jax.ShapeDtypeStruct(dims, dtype)


WHOLE = pl.BlockSpec(memory_space=pltpu.VMEM)


def kernel(body, out_shape, mebibytes, scratch=(), cost=0, **more):
    return pl.pallas_call(
        body,
        out_shape=out_shape,
        scratch_shapes=[
            pltpu.VMEM(*each) if isinstance(each, tuple) else each for each in scratch
        ],
        compiler_params=pltpu.CompilerParams(vmem_limit_bytes=mebibytes << 20),
        cost_estimate=pl.CostEstimate(flops=cost, bytes_accessed=cost, transcendentals=0),
        name=body.__name__,
        **more,
    )


def sum_over_chan(part):
    count = lax.axis_size("chan")
    rows, columns = part.shape
    pairs = [[2 * chip, 2 * chip + 1] for chip in range(count // 2)]
    across = [list(range(core, count, 2)) for core in range(2)]
    both = lax.all_gather(part, "chan", axis=0, tiled=True, axis_index_groups=pairs)
    copies = kernel(
        pair_kernel,
        shape(count // 2, rows // 2, columns, dtype=BF16),
        4,
    )(both)
    parts = lax.all_to_all(copies, "chan", 0, 0, tiled=True, axis_index_groups=across)
    half = kernel(chips_kernel, shape(rows // 2, columns, dtype=BF16), 4)(parts)
    return lax.all_gather(half, "chan", axis=0, tiled=True, axis_index_groups=pairs)


def local(signal, cotangent, w_proj, w_delta, delta_bias, decay_log, skip_gain):
    rows, width = signal.shape
    columns = w_proj.shape[1]
    depth = decay_log.shape[1]
    steps = rows // GROUPS
    shards = lax.axis_size("seq")
    if shards % 4:
        raise ValueError("shard count")
    w_turned = w_proj.T
    along_y = [[z * 4 + y for y in range(4)] for z in range(shards // 4)]
    along_z = [[z * 4 + y for z in range(shards // 4)] for y in range(4)]
    slots = depth + 4

    def exchange(array, groups):
        return lax.all_to_all(array, "seq", 0, 0, tiled=True, axis_index_groups=groups)

    signal_wide, part = kernel(
        project_kernel,
        (shape(rows, width), shape(rows, columns)),
        8,
        (((rows, width), BF16), ((columns, width), BF16), pltpu.SemaphoreType.DMA((2,))),
        in_specs=[pl.BlockSpec(memory_space=pltpu.HBM)] * 2,
        out_specs=(WHOLE, WHOLE),
    )(*(pltpu.with_memory_space_constraint(each, pltpu.HBM) for each in (signal, w_turned)))
    cot_wide, rates, flat, bias, gain = kernel(
        prepare_kernel,
        (
            shape(rows, width),
            shape(2, depth, GROUPS, width),
            shape(2, slots, width),
            shape(2, width),
            shape(1, width),
        ),
        8,
        cost=1 << 20,
    )(cotangent, decay_log.transpose(1, 0, 2), delta_bias, skip_gain.reshape(1, width))
    projected = sum_over_chan(part)
    wide = ((rows, 4 * depth * LANES), F32)
    stack = ((steps, depth, GROUPS, width), F32)
    delta, slope, local_states, ahead, payload = kernel(
        summary_kernel,
        (
            shape(2, rows, width),
            shape(2, rows, width),
            shape(4, depth, GROUPS, width),
            shape(4, GROUPS, width),
            shape(4, 2, slots, width, dtype=BF16),
        ),
        20,
        (((rows, width), F32), stack, wide, ((4, slots, width), F32)),
    )(projected, w_delta, bias, rates, signal_wide, cot_wide)
    parts = exchange(payload, along_y)
    copies = kernel(row_kernel, shape(shards // 4, slots, width, dtype=BF16), 4)(parts, flat)
    spread, fades = kernel(
        early_kernel,
        (
            shape(2, rows, 2 * depth * LANES),
            shape(2, steps, depth, GROUPS, width),
        ),
        8,
        cost=1 << 22,
    )(projected, rates, delta)
    row_totals = exchange(copies, along_z)
    entries, others = kernel(
        entry_kernel,
        (shape(2, slots, width), shape(2, slots, width)),
        4,
        (((4, slots, width), F32),),
    )(row_totals, parts, flat)
    swapped = lax.ppermute(others, "seq", [(shard, shard ^ 1) for shard in range(shards)])
    rank = w_delta.shape[1]
    inputs = (
        spread,
        fades,
        w_delta,
        rates,
        signal_wide,
        cot_wide,
        delta,
        slope,
        local_states,
        ahead,
    )
    scratch = (
        ((rows, width), F32),
        ((rows, width), F32),
        stack,
        ((rows * depth, 2 * LANES), BF16),
    )
    own = kernel(
        own_gradient_kernel,
        (
            shape(rows, width),
            shape(rows, width),
            shape(rows, rank),
            shape(rows, LANES),
        ),
        10,
        scratch,
        cost=1 << 22,
    )(gain, *inputs, entries)
    core, grad_parts, direct = kernel(
        other_gradient_kernel,
        (shape(rows, width), shape(rows, columns), shape(rows, width)),
        10,
        (((rows, rank), F32), ((rows, LANES), F32)) + scratch,
    )(*own, *inputs, swapped)
    grad_proj = sum_over_chan(grad_parts)
    result = shape(rows, width, dtype=BF16)
    layer_out, signal_grad = kernel(finish_kernel, (result, result), 8)(
        grad_proj, w_turned, direct, core
    )
    return (layer_out, signal_grad)


def solution(mesh):
    in_specs = (
        P("seq", "chan"),
        P("seq", "chan"),
        P("chan", None),
        P(None, None, "chan"),
        P(None, "chan"),
        P(None, None, "chan"),
        P("chan"),
    )
    out_specs = (P("seq", "chan"), P("seq", "chan"))
    return jax.shard_map(local, mesh=mesh, in_specs=in_specs, out_specs=out_specs, check_vma=False)
```

```python
import math

import jax
import jax.numpy as jnp
from jax import lax
from jax.experimental import pallas as pl
from jax.experimental.pallas import tpu as pltpu
from jax.sharding import PartitionSpec as P

GROUPS = 8
LANES = 128
LOG2E = math.log2(math.e)
LN2 = math.log(2.0)
FAR = 1e30
NT = (((1,), (1,)), ((), ()))
F32 = jnp.float32
BF16 = jnp.bfloat16


def dot(a, b, dims=(((1,), (0,)), ((), ()))):
    return lax.dot_general(a, b, dims, preferred_element_type=F32)


def grouping(rows, inverse=False):
    steps = rows // GROUPS
    row = lax.broadcasted_iota(jnp.int32, (rows, rows), 1 if inverse else 0)
    token = lax.broadcasted_iota(jnp.int32, (rows, rows), 0 if inverse else 1)
    return jnp.where(token == (row % GROUPS) * steps + row // GROUPS, 1.0, 0.0).astype(BF16)


def project_kernel(signal, w_proj, signal_out, part_out, signal_here, w_here, done):
    fetches = [
        pltpu.make_async_copy(signal, signal_here, done.at[0]),
        pltpu.make_async_copy(w_proj, w_here, done.at[1]),
    ]
    for fetch in fetches:
        fetch.start()
    order = grouping(signal_here.shape[0])
    fetches[0].wait()
    grouped = dot(order, signal_here[...])
    signal_out[...] = grouped
    fetches[1].wait()
    part_out[...] = dot(grouped.astype(BF16), w_here[...], NT)


def pair_kernel(both, copies):
    half = both.shape[0] // 4
    start = pl.multiple_of(lax.axis_index("chan") % 2 * half, half)
    total = both[pl.ds(start, half), :] + both[pl.ds(2 * half + start, half), :]
    for copy in range(copies.shape[0]):
        copies[copy] = total.astype(BF16)


def chips_kernel(parts, total):
    result = parts[0].astype(F32)
    for chip in range(1, parts.shape[0]):
        result = result + parts[chip].astype(F32)
    total[...] = result.astype(BF16)


def prepare_kernel(cotangent, decay_log, bias, skip_gain, cot_out, rates, flat, bias_out, gain_out):
    cot_out[...] = dot(grouping(cotangent.shape[0]), cotangent[...])
    bias_out[...] = bias[...]
    gain_out[...] = skip_gain[...]
    depth, _, width = decay_log.shape
    flat[...] = jnp.zeros_like(flat)
    for n in range(depth):
        scaled = -jnp.exp(decay_log[n]) * LOG2E
        for way in range(2):
            rates[way, n] = jnp.broadcast_to(scaled[way : way + 1], (GROUPS, width))
            flat[way, n : n + 1] = scaled[way : way + 1]


def at(step):
    return pl.ds(pl.multiple_of(step * GROUPS, GROUPS), GROUPS)


def lane_block(block):
    return slice(block * LANES, (block + 1) * LANES)


def spread_gates(gates, spread, first=0):
    count = gates.shape[1]
    for pair in range(spread.shape[1] // (2 * LANES)):
        source = lax.broadcasted_iota(jnp.int32, (count, 2 * LANES), 0)
        lane = lax.broadcasted_iota(jnp.int32, (count, 2 * LANES), 1)
        pick = jnp.where(source == first + 2 * pair + lane // LANES, 1.0, 0.0).astype(BF16)
        spread[:, pair * 2 * LANES : (pair + 1) * 2 * LANES] = dot(gates, pick)


def gate_at(spread, step, column):
    return spread[at(step), column * LANES : (column + 1) * LANES]


def put_total(shares, kind, lanes, total):
    depth = shares.shape[1] - 4
    coarse = total.astype(BF16).astype(F32)
    shares[kind, depth : depth + 1, lanes] = coarse
    shares[kind, depth + 1 : depth + 2, lanes] = total - coarse


def summary_kernel(
    projected,
    w_delta,
    bias,
    rates,
    signal,
    cot,
    delta_out,
    pre_out,
    local_out,
    ahead_out,
    payload,
    weight,
    fades,
    spread,
    shares,
):
    rows, width = signal.shape
    rank = w_delta.shape[1]
    depth = rates.shape[1]
    steps = rows // GROUPS
    blocks = width // LANES
    spread_gates(projected[:, 2 * rank :], spread)
    shares[...] = jnp.zeros_like(shares)
    group = lax.broadcasted_iota(jnp.int32, (GROUPS, LANES), 0)
    for way in range(2):
        pre = dot(projected[:, way * rank : (way + 1) * rank], w_delta[way]) + bias[way : way + 1]
        delta = jnp.maximum(pre, 0.0) + jnp.log1p(jnp.exp(-jnp.abs(pre)))
        delta_out[way] = delta
        pre_out[way] = pre
        weight[...] = delta * signal[...]
        falling = way == 1
        zero = jnp.zeros((GROUPS, LANES), F32)
        many = (zero,) * (blocks * depth)

        def walk_states(index, carry):
            states, total = carry
            step = steps - 1 - index if falling else index
            d = [delta_out[way, at(step), lane_block(block)] for block in range(blocks)]
            w = [weight[at(step), lane_block(block)] for block in range(blocks)]
            result = []
            for n in range(depth):
                gate = gate_at(spread, step, 2 * way * depth + n)
                for block in range(blocks):
                    fade = jnp.exp2(d[block] * rates[way, n, :, lane_block(block)])
                    fades[step, n, :, lane_block(block)] = fade
                    result.append(fade * states[n * blocks + block] + w[block] * gate)
            return (tuple(result), tuple(t + x for t, x in zip(total, d)))

        states, total = lax.fori_loop(0, steps, walk_states, (many, (zero,) * blocks), unroll=8)

        def walk_adjoints(index, carried):
            step = index if falling else steps - 1 - index
            g = [cot[at(step), lane_block(block)] for block in range(blocks)]
            result = []
            for n in range(depth):
                gate = gate_at(spread, step, (2 * way + 1) * depth + n)
                for block in range(blocks):
                    fade = fades[step, n, :, lane_block(block)]
                    result.append(fade * (g[block] * gate + carried[n * blocks + block]))
            return tuple(result)

        carried = lax.fori_loop(0, steps, walk_adjoints, many, unroll=8)
        for block in range(blocks):
            lanes = lane_block(block)

            def shift(array, by, down):
                return pltpu.roll(array, GROUPS - by if down else by, 0)

            def beyond(by, down):
                return group >= GROUPS - by if down else group < by

            whole = jnp.sum(total[block], 0, keepdims=True)
            for kind, down, finals in ((0, falling, states), (1, not falling, carried)):
                windows = []
                window = total[block]
                ahead = jnp.where(beyond(1, down), 0.0, shift(window, 1, down))
                for by in (1, 2, 4):
                    windows.append(jnp.where(beyond(by, down), FAR, window))
                    outside = beyond(by, down)
                    window = window + jnp.where(outside, 0.0, shift(window, by, down))
                    ahead = ahead + jnp.where(outside, 0.0, shift(ahead, by, down))
                ahead_out[2 * way + kind, :, lanes] = ahead
                edge = 0 if down else GROUPS - 1
                for n in range(depth):
                    rate = rates[way, n, :, lanes]
                    scanned = finals[n * blocks + block]
                    for by, span in zip((1, 2, 4), windows):
                        scanned = scanned + jnp.exp2(rate * span) * shift(scanned, by, down)
                    local_out[2 * way + kind, n, :, lanes] = jnp.where(
                        beyond(1, down), 0.0, shift(scanned, 1, down)
                    )
                    shares[2 * way + kind, n : n + 1, lanes] = scanned[edge : edge + 1]
                put_total(shares, 2 * way + kind, lanes, whole)
    for shard in range(payload.shape[0]):
        way = shard % 2
        payload[shard] = shares[2 * way : 2 * way + 2].astype(BF16)


def order(count, falling):
    return range(count - 1, -1, -1) if falling else range(count)


def pass_by(state, block, rates):
    depth = block.shape[0] - 4
    total = block[depth : depth + 1] + block[depth + 1 : depth + 2]
    return jnp.exp2(rates * total) * state + block


def place_of(shards):
    place = lax.axis_index("seq")
    return place // shards, place % shards, place % 2


def row_kernel(parts, flat, copies):
    shards, _, slots, width = parts.shape
    depth = slots - 4
    here, _, way = place_of(shards)
    slot = lax.broadcasted_iota(jnp.int32, (slots, width), 0)
    packed = []
    for falling in (False, True):
        state = jnp.zeros((slots, width), F32)
        total = jnp.zeros((1, width), F32)
        for shard in order(shards, falling):
            block = parts[shard, 1 - way if falling else way].astype(F32)
            total = total + block[depth : depth + 1] + block[depth + 1 : depth + 2]
            state = pass_by(state, block, flat[way])
        coarse = total.astype(BF16).astype(F32)
        state = jnp.where(slot == depth, coarse, state)
        state = jnp.where(slot == depth + 1, total - coarse, state)
        packed.append(jnp.where(slot > depth + 1, 0.0, state).astype(BF16))
    for row in range(copies.shape[0]):

        @pl.when(row > here)
        def _():
            copies[row] = packed[0]

        @pl.when(row <= here)
        def _():
            copies[row] = packed[1]


def entry_kernel(rows, parts, flat, mine, other, every):
    count, slots, width = rows.shape
    shards = parts.shape[0]
    row_here, here, way = place_of(shards)
    rates = flat[way]
    for falling in (False, True):
        kind = 1 - way if falling else way
        state = jnp.zeros((slots, width), F32)
        for row in order(count, falling):
            passed = pass_by(state, rows[row].astype(F32), rates)
            state = jnp.where(row > row_here if falling else row < row_here, passed, state)
        for shard in order(shards, falling):
            every[shard] = state
            state = pass_by(state, parts[shard, kind].astype(F32), rates)
        mine[kind] = every[here]
        other[kind] = every[here + 1 - 2 * way].astype(BF16)


def early_kernel(projected, rates, delta, pre, spread, fades, slope):
    for way in range(2):
        slope[way] = 1.0 / (1.0 + jnp.exp(-pre[way]))
    _, steps, depth, _, _ = fades.shape
    rank = (projected.shape[1] - 4 * depth) // 2
    for way in range(2):
        spread_gates(projected[:, 2 * rank :], spread.at[way], 2 * way * depth)

    def walk(step, _):
        for way in range(2):
            d = delta[way, at(step), :]
            for n in range(depth):
                fades[way, step, n] = jnp.exp2(d * rates[way, n])
        return _

    lax.fori_loop(0, steps, walk, 0, unroll=4)


def direction_gradient(
    way,
    spread,
    fades,
    w_delta,
    rates,
    signal,
    cot,
    delta,
    slope,
    local,
    ahead,
    entries,
    core,
    direct,
    low,
    gate_grad,
    weight,
    grad_pre,
    kept,
    products,
):
    rows, width = signal.shape
    depth = rates.shape[1]
    steps = rows // GROUPS
    blocks = width // LANES
    first = 2 * way * depth
    weight[...] = delta[way] * signal[...]

    def entering(kind):
        arrived = entries[kind].astype(F32)
        gap = [ahead[2 * way + kind, :, lane_block(block)] for block in range(blocks)]
        return tuple(
            local[2 * way + kind, n, :, lane_block(block)]
            + jnp.exp2(gap[block] * rates[way, n, :, lane_block(block)])
            * arrived[n : n + 1, lane_block(block)]
            for n in range(depth)
            for block in range(blocks)
        )

    def pieces(array, step):
        return [array[at(step), lane_block(block)] for block in range(blocks)]

    def put_products(which, step, rows_of):
        start = pl.multiple_of(step * depth * GROUPS, 2 * GROUPS)
        stacked = jnp.concatenate(rows_of, 0).astype(BF16)
        products[pl.ds(start, depth * GROUPS), lane_block(which)] = stacked

    def walk_states(index, states):
        step = index + way * (steps - 1 - 2 * index)
        w, g = pieces(weight, step), pieces(cot, step)
        total = pieces(core, step)
        rows_of = []
        result = []
        for n in range(depth):
            gate_in = gate_at(spread.at[way], step, n)
            gate_out = gate_at(spread.at[way], step, depth + n)
            for block in range(blocks):
                lanes = lane_block(block)
                faded = fades[way, step, n, :, lanes] * states[n * blocks + block]
                kept[step, n, :, lanes] = faded
                state = faded + w[block] * gate_in
                total[block] = total[block] + gate_out * state
                product = g[block] * state if block == 0 else product + g[block] * state
                result.append(state)
            rows_of.append(product)
        for block in range(blocks):
            core[at(step), lane_block(block)] = total[block]
        put_products(1, step, rows_of)
        return tuple(result)

    lax.fori_loop(0, steps, walk_states, entering(0), unroll=8)

    def walk_adjoints(index, carried):
        step = steps - 1 - index + way * (2 * index - steps + 1)
        w, g = pieces(weight, step), pieces(cot, step)
        rows_of = []
        through = [jnp.zeros((GROUPS, LANES), F32)] * blocks
        fading = [jnp.zeros((GROUPS, LANES), F32)] * blocks
        result = []
        for n in range(depth):
            gate_in = gate_at(spread.at[way], step, n)
            gate_out = gate_at(spread.at[way], step, depth + n)
            for block in range(blocks):
                lanes = lane_block(block)
                adjoint = g[block] * gate_out + carried[n * blocks + block]
                result.append(fades[way, step, n, :, lanes] * adjoint)
                through[block] = through[block] + adjoint * gate_in
                fading[block] = fading[block] + (
                    adjoint * kept[step, n, :, lanes] * rates[way, n, :, lanes]
                )
                product = adjoint * w[block] if block == 0 else product + adjoint * w[block]
            rows_of.append(product)
        put_products(0, step, rows_of)
        for block in range(blocks):
            lanes = lane_block(block)
            grad_delta = through[block] * signal[at(step), lanes] + fading[block] * LN2
            direct[at(step), lanes] = (
                direct[at(step), lanes] + through[block] * delta[way, at(step), lanes]
            )
            grad_pre[at(step), lanes] = grad_delta * slope[way, at(step), lanes]
        return tuple(result)

    lax.fori_loop(0, steps, walk_adjoints, entering(1), unroll=8)
    low[...] = dot(grad_pre[...].astype(BF16), w_delta[way], NT)
    row = lax.broadcasted_iota(jnp.int32, (2 * LANES, 2 * LANES), 0)
    column = lax.broadcasted_iota(jnp.int32, (2 * LANES, 2 * LANES), 1)
    halves = jnp.where(row // LANES == column // LANES, 1.0, 0.0).astype(BF16)
    lane = lax.broadcasted_iota(jnp.int32, (GROUPS, LANES), 1) - first
    height = depth * GROUPS
    for start in range(0, steps, 4):
        sums = dot(products[start * height : (start + 4) * height, :], halves)
        for step in range(4):
            spot = slice((start + step) * GROUPS, (start + step + 1) * GROUPS)
            merged = gate_grad[spot]
            for which in range(2):
                for n in range(depth):
                    top = step * height + n * GROUPS
                    merged = jnp.where(
                        lane == which * depth + n,
                        sums[top : top + GROUPS, lane_block(which)],
                        merged,
                    )
            gate_grad[spot] = merged


def own_gradient_kernel(skip_gain, *refs):
    signal, cot = refs[4:6]
    core, direct, _, gate_grad = refs[11:15]
    core[...] = skip_gain[...] * signal[...]
    direct[...] = skip_gain[...] * cot[...]
    gate_grad[...] = jnp.zeros_like(gate_grad)
    direction_gradient(lax.axis_index("seq") % 2, *refs)


def other_gradient_kernel(own_core, own_direct, own_low, own_gates, *refs):
    inputs = refs[:11]
    core, parts_out, direct, low, gate_grad = refs[11:16]
    way = 1 - lax.axis_index("seq") % 2
    core[...] = own_core[...]
    direct[...] = own_direct[...]
    gate_grad[...] = own_gates[...]
    direction_gradient(way, *inputs, core, direct, low, gate_grad, *refs[16:])
    rank = low.shape[1]
    gates = parts_out.shape[1] - 2 * rank
    parts_out[:, pl.ds(pl.multiple_of(way * rank, LANES), rank)] = low[...]
    parts_out[:, pl.ds(pl.multiple_of((1 - way) * rank, LANES), rank)] = own_low[...]
    parts_out[:, 2 * rank :] = gate_grad[:, :gates]


def finish_kernel(grad_proj, w_proj, direct, core, layer_out, signal_grad):
    ungroup = grouping(direct.shape[0], inverse=True)
    layer_out[...] = dot(ungroup, core[...].astype(BF16)).astype(BF16)
    total = dot(grad_proj[...], w_proj[...]) + direct[...]
    signal_grad[...] = dot(ungroup, total.astype(BF16)).astype(BF16)


def shape(*dims, dtype=F32):
    return jax.ShapeDtypeStruct(dims, dtype)


WHOLE = pl.BlockSpec(memory_space=pltpu.VMEM)


def kernel(body, out_shape, mebibytes, scratch=(), cost=0, **more):
    return pl.pallas_call(
        body,
        out_shape=out_shape,
        scratch_shapes=[
            pltpu.VMEM(*each) if isinstance(each, tuple) else each for each in scratch
        ],
        compiler_params=pltpu.CompilerParams(vmem_limit_bytes=mebibytes << 20),
        cost_estimate=pl.CostEstimate(flops=cost, bytes_accessed=cost, transcendentals=0),
        name=body.__name__,
        **more,
    )


def sum_over_chan(part):
    count = lax.axis_size("chan")
    rows, columns = part.shape
    pairs = [[2 * chip, 2 * chip + 1] for chip in range(count // 2)]
    across = [list(range(core, count, 2)) for core in range(2)]
    both = lax.all_gather(part, "chan", axis=0, tiled=True, axis_index_groups=pairs)
    copies = kernel(
        pair_kernel,
        shape(count // 2, rows // 2, columns, dtype=BF16),
        4,
    )(both)
    parts = lax.all_to_all(copies, "chan", 0, 0, tiled=True, axis_index_groups=across)
    half = kernel(chips_kernel, shape(rows // 2, columns, dtype=BF16), 4)(parts)
    return lax.all_gather(half, "chan", axis=0, tiled=True, axis_index_groups=pairs)


def local(signal, cotangent, w_proj, w_delta, delta_bias, decay_log, skip_gain):
    rows, width = signal.shape
    columns = w_proj.shape[1]
    depth = decay_log.shape[1]
    steps = rows // GROUPS
    shards = lax.axis_size("seq")
    if shards % 4:
        raise ValueError("shard count")
    w_turned = w_proj.T
    along_y = [[z * 4 + y for y in range(4)] for z in range(shards // 4)]
    along_z = [[z * 4 + y for z in range(shards // 4)] for y in range(4)]
    slots = depth + 4

    def exchange(array, groups):
        return lax.all_to_all(array, "seq", 0, 0, tiled=True, axis_index_groups=groups)

    signal_wide, part = kernel(
        project_kernel,
        (shape(rows, width), shape(rows, columns)),
        8,
        (((rows, width), BF16), ((columns, width), BF16), pltpu.SemaphoreType.DMA((2,))),
        in_specs=[pl.BlockSpec(memory_space=pltpu.HBM)] * 2,
        out_specs=(WHOLE, WHOLE),
    )(*(pltpu.with_memory_space_constraint(each, pltpu.HBM) for each in (signal, w_turned)))
    cot_wide, rates, flat, bias, gain = kernel(
        prepare_kernel,
        (
            shape(rows, width),
            shape(2, depth, GROUPS, width),
            shape(2, slots, width),
            shape(2, width),
            shape(1, width),
        ),
        8,
        cost=1 << 20,
    )(cotangent, decay_log.transpose(1, 0, 2), delta_bias, skip_gain.reshape(1, width))
    projected = sum_over_chan(part)
    wide = ((rows, 4 * depth * LANES), F32)
    stack = ((steps, depth, GROUPS, width), F32)
    delta, pre, local_states, ahead, payload = kernel(
        summary_kernel,
        (
            shape(2, rows, width),
            shape(2, rows, width),
            shape(4, depth, GROUPS, width),
            shape(4, GROUPS, width),
            shape(4, 2, slots, width, dtype=BF16),
        ),
        20,
        (((rows, width), F32), stack, wide, ((4, slots, width), F32)),
    )(projected, w_delta, bias, rates, signal_wide, cot_wide)
    parts = exchange(payload, along_y)
    copies = kernel(row_kernel, shape(shards // 4, slots, width, dtype=BF16), 4)(parts, flat)
    spread, fades, slope = kernel(
        early_kernel,
        (
            shape(2, rows, 2 * depth * LANES),
            shape(2, steps, depth, GROUPS, width),
            shape(2, rows, width),
        ),
        8,
        cost=1 << 22,
    )(projected, rates, delta, pre)
    row_totals = exchange(copies, along_z)
    entries, others = kernel(
        entry_kernel,
        (shape(2, slots, width), shape(2, slots, width, dtype=BF16)),
        4,
        (((4, slots, width), F32),),
    )(row_totals, parts, flat)
    swapped = lax.ppermute(others, "seq", [(shard, shard ^ 1) for shard in range(shards)])
    rank = w_delta.shape[1]
    inputs = (
        spread,
        fades,
        w_delta,
        rates,
        signal_wide,
        cot_wide,
        delta,
        slope,
        local_states,
        ahead,
    )
    scratch = (
        ((rows, width), F32),
        ((rows, width), F32),
        stack,
        ((rows * depth, 2 * LANES), BF16),
    )
    own = kernel(
        own_gradient_kernel,
        (
            shape(rows, width),
            shape(rows, width),
            shape(rows, rank),
            shape(rows, LANES),
        ),
        10,
        scratch,
        cost=1 << 22,
    )(gain, *inputs, entries)
    core, grad_parts, direct = kernel(
        other_gradient_kernel,
        (shape(rows, width), shape(rows, columns), shape(rows, width)),
        10,
        (((rows, rank), F32), ((rows, LANES), F32)) + scratch,
    )(*own, *inputs, swapped)
    grad_proj = sum_over_chan(grad_parts)
    result = shape(rows, width, dtype=BF16)
    layer_out, signal_grad = kernel(finish_kernel, (result, result), 8)(
        grad_proj, w_turned, direct, core
    )
    return (layer_out, signal_grad)


def solution(mesh):
    in_specs = (
        P("seq", "chan"),
        P("seq", "chan"),
        P("chan", None),
        P(None, None, "chan"),
        P(None, "chan"),
        P(None, None, "chan"),
        P("chan"),
    )
    out_specs = (P("seq", "chan"), P("seq", "chan"))
    return jax.shard_map(local, mesh=mesh, in_specs=in_specs, out_specs=out_specs, check_vma=False)
```
